32 devices in a mesh: groups: 2 (over x), sub: 16 (over z, y, core).
Axes of the slice: x: 2, y: 2, z: 4, core: 2. Of those that a mesh axis runs over, the one named last changes fastest.
Arguments:
- modes_start: float32 [48, 6, 8192], P(None, None, ('groups', 'sub')), parts along dimension 2, may hold values from -6 to 6
- stiffness: float32 [24, 24, 8192], P(None, None, ('groups', 'sub')), parts along dimension 2, as said below
- mass: float32 [24, 24, 8192], P(None, None, ('groups', 'sub')), parts along dimension 2, as said below
- connect: int32 [4, 8192], P(None, ('groups', 'sub')), parts along dimension 1, may hold values from 0 to 382, as said below
Outputs:
- modes: float32 [48, 6, 8192], P(None, None, ('groups', 'sub')), parts along dimension 2
- ritz: float32 [96], P('groups'), parts along dimension 0
The draws below stay inside these ranges and needn't reach their ends.
There are 2 independent parts, one for each index of `groups`. The reference program is written for one: setup_inputs(seed, part) draws one part's arguments, and reference() takes and returns one part's arrays. A program takes and returns all parts, laid end to end along the dimension named above; each array names one. Nothing has to cross between parts.
Inputs may be any that keep to these rules, and one draw needn't show every extreme that they name: `connect`: for element l of a subdomain, the four nodes are l + 64, one above it by less than 32, one below it by at most 64, and one above it by 32 or more and less than 64. `stiffness`: each block is symmetric positive definite. `mass`: each block is symmetric positive definite.
All inputs are finite; a program needn't handle non-finite values.
Results may differ from the reference program's by a relative error of at most 0.0001.
Values sent between devices are 32-bit elements; how exact they have to be, the bound alone decides.
No kernel may reach another device: no remote copies, remote signals or barrier semaphores. Data moves between devices by JAX's collectives and lax.ppermute only.
A program may use at most 64 MiB of HBM per device.

```python
import math
import jax
import jax.numpy as jnp
from jax import lax

MODES = 48
NODE_DEV = 256
HALO = 64
ITERS = 2
SMALL_STEPS = 2
NODES = 4096
ELEMS = 4096
N_SUB = 16


def element_blocks(key, shift):
    raw = jax.random.normal(key, (ELEMS, 24, 24), jnp.float32)
    blocks = jnp.einsum('eik,ejk->eij', raw, raw) / 24.0 + shift * jnp.eye(24, dtype=jnp.float32)[None]
    return jnp.transpose(blocks, (1, 2, 0))


def draw_stiffness(key, part):
    first, second = jax.random.split(jax.random.fold_in(key, 21))
    top = math.log(4.0)
    spread = jnp.exp(jax.random.uniform(second, (ELEMS,), jnp.float32, 0.0, top))
    return element_blocks(first, 0.5) * spread[None, None, :]


def draw_mass(key, part):
    first = jax.random.fold_in(key, 37)
    return element_blocks(first, 0.5)


def draw_connect(key, part):
    keys = jax.random.split(jax.random.fold_in(key, 53), 3)
    local = jnp.arange(ELEMS, dtype=jnp.int32) % NODE_DEV + HALO
    nearby = jax.random.randint(keys[0], (ELEMS,), 1, HALO // 2, dtype=jnp.int32)
    behind = jax.random.randint(keys[1], (ELEMS,), 1, HALO + 1, dtype=jnp.int32)
    farther = jax.random.randint(keys[2], (ELEMS,), HALO // 2, HALO, dtype=jnp.int32)
    return jnp.stack([local, local + nearby, local - behind, local + farther]).astype(jnp.int32)


def steps_of(key, dims, shards, least, largest):
    loudness, own = 1.0, jax.random.fold_in(key, 6)
    for position, blocks in shards:
        steps = jnp.exp(jax.random.uniform(jax.random.fold_in(own, position), (blocks,), jnp.float32, least / len(shards), largest / len(shards)))
        loudness = loudness * jnp.repeat(steps, dims[position] // blocks).reshape([-1 if axis == position else 1 for axis in range(len(dims))])
    return loudness


def normal_values(key, extent, scale, bound, cuts=(), kind=jnp.bfloat16):
    loudness = steps_of(key, extent, cuts, -0.22, 0.18) if cuts else 1.0
    array = jax.random.normal(key, extent, jnp.float32) * scale * loudness
    return jnp.minimum(jnp.maximum(array, -bound), bound).astype(kind)


def setup_inputs(seed: int = 0, part: int = 0) -> dict:
    key_list = jax.random.split(jax.random.key(seed), 5)
    part_keys = jax.random.split(jax.random.fold_in(key_list[4], part), 5)
    return {
        "modes_start": normal_values(part_keys[0], (MODES, 6, NODES), 1.0, 6.0, ((2, 16),), jnp.float32),
        "stiffness": draw_stiffness(jax.random.fold_in(jax.random.fold_in(key_list[4], part), 71), part),
        "mass": draw_mass(jax.random.fold_in(jax.random.fold_in(key_list[4], part), 71), part),
        "connect": draw_connect(jax.random.fold_in(jax.random.fold_in(key_list[4], part), 71), part),
    }


highest = lax.Precision.HIGHEST

def inner(left, right):
    return jnp.einsum('acn,bcn->ab', left, right, precision=highest)

def combine(coeff, block):
    return jnp.einsum('ab,bcn->acn', coeff, block, precision=highest)

def symmetric(matrix):
    return 0.5 * (matrix + matrix.T)

def lower_solve(factor, rhs, transpose):
    return lax.linalg.triangular_solve(factor, rhs, left_side=True, lower=True, transpose_a=transpose)

def small_step(stiff_gram, mass_gram):
    scaling = 1.0 / jnp.sqrt(jnp.diagonal(mass_gram))
    outer = scaling[:, None] * scaling[None, :]
    stiff_scaled = symmetric(stiff_gram * outer)
    mass_scaled = symmetric(mass_gram * outer)
    factor = jnp.linalg.cholesky(stiff_scaled)
    coeff = jnp.eye(stiff_gram.shape[0], MODES, dtype=stiff_gram.dtype)
    for sweep in range(SMALL_STEPS):
        pushed = jnp.dot(mass_scaled, coeff, precision=highest)
        solved = lower_solve(factor, lower_solve(factor, pushed, False), True)
        normal_gram = symmetric(jnp.dot(solved.T, jnp.dot(mass_scaled, solved, precision=highest), precision=highest))
        small_factor = jnp.linalg.cholesky(normal_gram)
        coeff = lower_solve(small_factor, solved.T, False).T
    return coeff * scaling[:, None]

def apply_pair(block, stiffness, mass, connect):
    rows = block.shape[0]
    elements = connect.shape[1]
    total_nodes = NODE_DEV * N_SUB
    owner = jnp.arange(elements, dtype=jnp.int32) // NODE_DEV * NODE_DEV
    global_node = connect + owner[None, :] - HALO
    valid = (global_node >= 0) & (global_node < total_nodes)
    safe = jnp.clip(global_node, 0, total_nodes - 1).astype(jnp.int32)
    weight = valid.astype(block.dtype)
    picked = (jnp.take(block, safe, axis=2) * weight).reshape(rows, 24, elements)
    stiff_part = jnp.einsum('ije,rje->rie', stiffness, picked, precision=highest)
    mass_part = jnp.einsum('ije,rje->rie', mass, picked, precision=highest)
    parts = jnp.stack([stiff_part, mass_part]).reshape(2, rows, 6, 4, elements) * weight
    summed = jnp.zeros((2, rows, 6, total_nodes), block.dtype).at[:, :, :, safe].add(parts)
    return (summed[0], summed[1])

def reference(modes_start, stiffness, mass, connect):
    stiff_start, mass_start = apply_pair(modes_start, stiffness, mass, connect)
    stiff_proj = inner(modes_start, stiff_start)
    mass_proj = inner(modes_start, mass_start)
    factor = jnp.linalg.cholesky(symmetric(mass_proj))
    inverse = lower_solve(factor, jnp.eye(MODES, dtype=mass_proj.dtype), False)
    current = combine(inverse, modes_start)
    stiff_cur = combine(inverse, stiff_start)
    mass_cur = combine(inverse, mass_start)
    rayleigh = symmetric(jnp.dot(inverse, jnp.dot(stiff_proj, inverse.T, precision=highest), precision=highest))
    direction = current
    stiff_dir = current
    mass_dir = current
    carried = rayleigh
    for sweep in range(ITERS):
        if sweep > 0:
            rayleigh = symmetric(inner(current, stiff_cur))
        residual = stiff_cur - combine(rayleigh, mass_cur)
        stiff_res, mass_res = apply_pair(residual, stiffness, mass, connect)
        if sweep == 0:
            basis = jnp.concatenate([current, residual])
            stiff_basis = jnp.concatenate([stiff_cur, stiff_res])
            mass_basis = jnp.concatenate([mass_cur, mass_res])
        else:
            basis = jnp.concatenate([current, residual, direction])
            stiff_basis = jnp.concatenate([stiff_cur, stiff_res, stiff_dir])
            mass_basis = jnp.concatenate([mass_cur, mass_res, mass_dir])
        stiff_gram = inner(basis, stiff_basis)
        mass_gram = inner(basis, mass_basis)
        coeff = small_step(stiff_gram, mass_gram)
        carried = symmetric(jnp.dot(coeff.T, jnp.dot(stiff_gram, coeff, precision=highest), precision=highest))
        current = combine(coeff.T, basis)
        direction = combine(coeff[MODES:].T, basis[MODES:])
        if sweep + 1 < ITERS:
            stiff_both, mass_both = apply_pair(jnp.concatenate([current, direction]), stiffness, mass, connect)
            stiff_cur = stiff_both[:MODES]
            stiff_dir = stiff_both[MODES:]
            mass_cur = mass_both[:MODES]
            mass_dir = mass_both[MODES:]
    return (current, jnp.diagonal(carried))
```

```python
import functools

import jax
import jax.numpy as jnp
from jax import lax
from jax.experimental import pallas as pl
from jax.experimental.pallas import tpu as pltpu
from jax.sharding import PartitionSpec as P

HALO = 64
LANES = 128
CORNERS = 4
F32 = jnp.float32
BF16 = jnp.bfloat16

NN = (((1,), (0,)), ((), ()))
NT = (((1,), (1,)), ((), ()))
TN = (((0,), (0,)), ((), ()))


def split(value):
    high = value.astype(BF16)
    return high, (value - high.astype(F32)).astype(BF16)


def dot1(left, right, dims):
    return lax.dot_general(left, right, dims, preferred_element_type=F32)


def dot3(left, right, dims=NN):
    left_high, left_low = split(left)
    right_high, right_low = split(right)
    return dot1(left_high, right_high, dims) + (
        dot1(left_high, right_low, dims) + dot1(left_low, right_high, dims)
    )


def dotf(left, right, dims=NN):
    return lax.dot_general(
        left, right, dims, precision=lax.Precision.HIGHEST, preferred_element_type=F32
    )


def symmetric(matrix):
    return 0.5 * (matrix + matrix.T)


def eliminate(work, modes):
    rows = lax.broadcasted_iota(jnp.int32, (modes, 1), 0)
    scale = jnp.zeros((modes, 1), F32)
    for k in range(modes):
        pivot = work[k : k + 1, :]
        inverse = 1.0 / pivot[:, k : k + 1]
        column = work[:, k : k + 1]
        factor = jnp.where(rows > k, column * inverse, 0.0)
        scale = jnp.where(rows == k, inverse, scale)
        work = work - factor * pivot
    return (work * jnp.sqrt(scale))[:, modes:]


def eye(modes):
    row = lax.broadcasted_iota(jnp.int32, (modes, modes), 0)
    col = lax.broadcasted_iota(jnp.int32, (modes, modes), 1)
    return (row == col).astype(F32)


def store_lanes(ref, value):
    rows, width = value.shape
    ref[0:rows, 0:width] = value


def element_products(dims, ext, stiffness, mass, stiff_edge, mass_edge, connect, edge_nodes, picked, high, low, out):
    comps, modes = dims
    ext_high, ext_low = split(ext[...])
    own_nodes = connect[...] + (LANES - HALO)
    blocks = (
        (stiffness, mass, 0, own_nodes[:, :LANES], 0, 3 * LANES),
        (stiffness, mass, LANES, own_nodes[:, LANES:], LANES, 3 * LANES),
        (stiff_edge, mass_edge, 0, edge_nodes, 0, 4 * LANES),
    )
    for number, (stiff, weigh, lane, nodes, base, window) in enumerate(blocks):
        place = lax.broadcasted_iota(jnp.int32, (window, LANES), 0) + base
        chosen = jnp.concatenate(
            [(place == nodes[a : a + 1, :]).astype(F32).astype(BF16) for a in range(CORNERS)], axis=1
        )
        picked[...] = dot1(ext_high[:, base : base + window], chosen, NN) + dot1(
            ext_low[:, base : base + window], chosen, NN
        )

        def one(step, unused):
            comp = step // 2
            pair = (step % 2) * 2
            totals = [jnp.zeros((modes, LANES), F32) for _ in range(4)]
            for j in range(comps * CORNERS):
                start = (j // CORNERS) * modes
                value = picked[start : start + modes, (j % CORNERS) * LANES : (j % CORNERS + 1) * LANES]
                for q in range(2):
                    for m, matrix in enumerate((stiff, weigh)):
                        entry = matrix[comp * CORNERS + pair + q, j : j + 1, lane : lane + LANES]
                        totals[2 * q + m] = totals[2 * q + m] + entry * value
            for q in range(2):
                for m in range(2):
                    upper, lower = split(totals[2 * q + m])
                    row = pl.multiple_of((comp * 2 + m) * modes, 16)
                    col = pl.multiple_of((pair + q) * LANES, LANES)
                    high[pl.ds(row, modes), pl.ds(col, LANES)] = upper
                    low[pl.ds(row, modes), pl.ds(col, LANES)] = lower
            return unused

        lax.fori_loop(0, comps * 2, one, 0)
        target = chosen[LANES - base : 3 * LANES - base, :]
        total = dot1(high[...], target, NT) + dot1(low[...], target, NT)
        if number == 0:
            out[...] = total
        else:
            out[...] += total


def grams(basis, products, dims):
    comps, modes = dims
    total = None
    for c in range(comps):
        left = jnp.concatenate([part[c * modes : (c + 1) * modes, :] for part in basis], axis=0)
        right = products[c * 2 * modes : (c + 1) * 2 * modes, :]
        term = dot3(left, right, NT)
        total = term if total is None else total + term
    return total


def pack_kernel(dims, block, stiffness, mass, connect, up, down):
    comps, modes = dims
    size = comps * CORNERS
    first = lax.broadcasted_iota(jnp.int32, (size, LANES), 1) < HALO

    def one(i, unused):
        row = pl.multiple_of(i * size, 8)
        up[pl.ds(row, size), :] = jnp.where(
            first, pltpu.roll(stiffness[i, :, LANES:], HALO, 1), mass[i, :, LANES:]
        )
        down[pl.ds(row, size), :] = jnp.where(
            first, stiffness[i, :, :LANES], pltpu.roll(mass[i, :, :LANES], HALO, 1)
        )
        return unused

    lax.fori_loop(0, size, one, 0)
    links = connect[...].astype(F32)
    pad = jnp.zeros((8 - CORNERS, LANES), F32)
    top = size * size
    up[top : top + 8, :] = jnp.concatenate([pltpu.roll(links[:, LANES:], HALO, 1), pad], axis=0)
    down[top : top + 8, :] = jnp.concatenate([links[:, :LANES], pad], axis=0)
    for c in range(comps):
        row = top + 8 + c * modes
        up[row : row + modes, :] = block[:, c, LANES:]
        down[row : row + modes, :] = block[:, c, :LANES]


def first_kernel(dims, stiffness, mass, connect, up, down, below, above, edges, edge_nodes, prod_low, prod_high, gram, ext, picked, high, low, out):
    comps, modes = dims
    size = comps * CORNERS
    top = size * size
    first = lax.broadcasted_iota(jnp.int32, (size, LANES), 1) < HALO

    def one(i, unused):
        row = pl.multiple_of(i * size, 8)
        lower = below[pl.ds(row, size), :]
        upper = above[pl.ds(row, size), :]
        edges[0, i] = jnp.where(first, lower, pltpu.roll(upper, HALO, 1))
        edges[1, i] = jnp.where(first, pltpu.roll(lower, HALO, 1), upper)
        return unused

    lax.fori_loop(0, size, one, 0)
    count = connect.shape[1]
    before = below[top : top + 8, :] + (LANES - HALO - count)
    after = pltpu.roll(above[top : top + 8, :], HALO, 1) + (LANES - HALO + count)
    edge_nodes[...] = jnp.where(first[:8], before, after).astype(jnp.int32)
    nodes = slice(top + 8, top + 8 + comps * modes)
    for tile, part in enumerate((below, down, up, above)):
        ext[:, tile * LANES : (tile + 1) * LANES] = part[nodes, :]
    element_products(dims, ext, stiffness, mass, edges.at[0], edges.at[1], connect, edge_nodes[...], picked, high, low, out)
    prod_low[...] = out[:, :LANES]
    prod_high[...] = out[:, LANES:]
    store_lanes(gram, grams([ext[:, LANES : 3 * LANES]], out[...], dims))


def second_kernel(dims, gram_in, stiffness, mass, connect, edges, edge_nodes, up, down, p_below, p_low, p_high, p_above, res_low, res_high, prod_low, prod_high, gram, state, ext, picked, high, low, out):
    comps, modes = dims
    size = comps * CORNERS
    reduced = gram_in[...]
    stiff_gram = symmetric(reduced[:, :modes])
    mass_gram = symmetric(reduced[:, modes : 2 * modes])
    unit = eye(modes)
    inverse = eliminate(jnp.concatenate([mass_gram, unit], axis=1), modes)
    stiff_root = eliminate(jnp.concatenate([stiff_gram, unit], axis=1), modes)
    ratio = dotf(stiff_gram, dotf(inverse, inverse, TN))
    state[0] = inverse
    state[1] = dotf(stiff_root, stiff_root, TN)
    state[2] = mass_gram
    ratio_high, ratio_low = split(ratio)
    for c in range(comps):
        for tile, part in enumerate((p_below, p_low, p_high, p_above)):
            row = c * 2 * modes
            right_high, right_low = split(part[row + modes : row + 2 * modes, :])
            moved = dot1(ratio_high, right_high, NN) + (dot1(ratio_high, right_low, NN) + dot1(ratio_low, right_high, NN))
            ext[c * modes : (c + 1) * modes, tile * LANES : (tile + 1) * LANES] = part[row : row + modes, :] - moved
    element_products(dims, ext, stiffness, mass, edges.at[0], edges.at[1], connect, edge_nodes[...], picked, high, low, out)
    prod_low[...] = out[:, :LANES]
    prod_high[...] = out[:, LANES:]
    res_low[...] = ext[:, LANES : 2 * LANES]
    res_high[...] = ext[:, 2 * LANES : 3 * LANES]
    nodes = slice(size * size + 8, size * size + 8 + comps * modes)
    block = jnp.concatenate([down[nodes, :], up[nodes, :]], axis=1)
    store_lanes(gram, grams([block, ext[:, LANES : 3 * LANES]], out[...], dims))


def small_step(reduced, solver, mass_old, start, modes):
    rows = reduced.shape[0]
    old = rows - modes
    turned = reduced.T
    cross = reduced[:old, :modes]
    corner = symmetric(reduced[old:, :modes])
    mass_cross = reduced[:old, modes : 2 * modes]
    mass_corner = symmetric(reduced[old:, modes : 2 * modes])
    mass_turned = turned[modes : 2 * modes, :old]
    mass_all = jnp.concatenate(
        [
            jnp.concatenate([mass_old, mass_cross], axis=1),
            jnp.concatenate([mass_turned, mass_corner], axis=1),
        ],
        axis=0,
    )
    unit = eye(modes)
    carried = dotf(turned[:modes, :old], solver)
    schur = symmetric(corner - dotf(carried, cross))
    root = eliminate(jnp.concatenate([schur, -carried, unit], axis=1), modes)
    wide = jnp.concatenate(
        [
            jnp.concatenate([solver, jnp.zeros((old, modes), F32)], axis=1),
            jnp.zeros((modes, rows), F32),
        ],
        axis=0,
    )
    solver = wide + dotf(root, root, TN)
    pushed = dotf(start, mass_all[: start.shape[1], :])
    solved = dotf(pushed, solver)
    again = dotf(solved, mass_all)
    pushed = eliminate(jnp.concatenate([symmetric(dotf(solved, again, NT)), again], axis=1), modes)
    solved = dotf(pushed, solver)
    again = dotf(solved, mass_all)
    normal = symmetric(dotf(solved, again, NT))
    energy = dotf(solved, pushed, NT)
    last = eliminate(jnp.concatenate([normal, solved, energy, unit], axis=1), modes)
    coeff = last[:, :rows]
    return coeff, last[:, rows : rows + modes], last[:, rows + modes :], solver, mass_all


def third_kernel(dims, gram_in, state_in, stiffness, mass, connect, edges, edge_nodes, up, down, p_below, p_low, p_high, p_above, q_below, q_low, q_high, q_above, res_low, res_high, new_low, new_high, gram, coeff_out, state, ext, picked, high, low, out):
    comps, modes = dims
    size = comps * CORNERS
    coeff, half, root, solver, mass_all = small_step(gram_in[...], state_in[1], state_in[2], state_in[0], modes)
    rayleigh = symmetric(dotf(half, root, NT))
    coeff_out[...] = coeff
    state[0] = solver
    state[1] = mass_all
    bent = dotf(rayleigh, coeff)
    mixed = jnp.concatenate([coeff[:, :modes], -bent[:, :modes], coeff[:, modes:], -bent[:, modes:]], axis=1)
    mixed_high, mixed_low = split(mixed)
    tiles = ((p_below, q_below), (p_low, q_low), (p_high, q_high), (p_above, q_above))
    for c in range(comps):
        for tile, parts in enumerate(tiles):
            row = c * 2 * modes
            right = jnp.concatenate([part[row : row + 2 * modes, :] for part in parts], axis=0)
            right_high, right_low = split(right)
            ext[c * modes : (c + 1) * modes, tile * LANES : (tile + 1) * LANES] = dot1(mixed_high, right_high, NN) + (
                dot1(mixed_high, right_low, NN) + dot1(mixed_low, right_high, NN)
            )
    element_products(dims, ext, stiffness, mass, edges.at[0], edges.at[1], connect, edge_nodes[...], picked, high, low, out)
    new_low[...] = ext[:, LANES : 2 * LANES]
    new_high[...] = ext[:, 2 * LANES : 3 * LANES]
    nodes = slice(size * size + 8, size * size + 8 + comps * modes)
    block = jnp.concatenate([down[nodes, :], up[nodes, :]], axis=1)
    residual = jnp.concatenate([res_low[...], res_high[...]], axis=1)
    store_lanes(gram, grams([block, residual, ext[:, LANES : 3 * LANES]], out[...], dims))


def last_kernel(dims, gram_in, coeff_in, state_in, up, down, res_low, res_high, new_low, new_high, modes_out, ritz_out):
    comps, modes = dims
    size = comps * CORNERS
    coeff, half, root, solver, mass_all = small_step(gram_in[...], state_in[0], state_in[1], coeff_in[...], modes)
    ritz = jnp.sum(half * root, axis=1, keepdims=True)
    ritz_out[...] = jnp.broadcast_to(ritz, (modes, LANES))
    coeff_high, coeff_low = split(coeff)
    top = size * size + 8
    for tile, parts in enumerate(((down, res_low, new_low), (up, res_high, new_high))):
        for c in range(comps):
            row = c * modes
            right = jnp.concatenate(
                [parts[0][top + row : top + row + modes, :]] + [part[row : row + modes, :] for part in parts[1:]], axis=0
            )
            right_high, right_low = split(right)
            modes_out[:, c, tile * LANES : (tile + 1) * LANES] = dot1(coeff_high, right_high, NN) + (
                dot1(coeff_high, right_low, NN) + dot1(coeff_low, right_high, NN)
            )


def total_over(value, axis):
    count = lax.axis_size(axis)
    if count & (count - 1):
        return lax.psum(value, axis)

    def from_partner(part, bits):
        return lax.ppermute(part, axis, [(i, i ^ bits) for i in range(count)])

    stride = 1
    while stride < count:
        if 4 * stride <= count:
            one, two, three = (from_partner(value, k * stride) for k in (1, 2, 3))
            value = (value + one) + (two + three)
            stride *= 4
        else:
            value = value + from_partner(value, stride)
            stride *= 2
    return value


def from_neighbours(upward, downward, axis):
    count = lax.axis_size(axis)
    below = lax.ppermute(upward, axis, [(i, i + 1) for i in range(count - 1)])
    above = lax.ppermute(downward, axis, [(i + 1, i) for i in range(count - 1)])
    return below, above


def call(kernel, dims, name, outs, scratch, *operands):
    shapes = tuple(jax.ShapeDtypeStruct(shape, dtype) for shape, dtype in outs)
    return pl.pallas_call(
        functools.partial(kernel, dims),
        out_shape=shapes,
        in_specs=[pl.BlockSpec(memory_space=pltpu.VMEM)] * len(operands),
        out_specs=tuple(pl.BlockSpec(memory_space=pltpu.VMEM) for _ in shapes),
        scratch_shapes=scratch,
        name=name,
    )(*operands)


def body(modes_start, stiffness, mass, connect):
    modes, comps, count = modes_start.shape
    size = comps * CORNERS
    dims = (comps, modes)
    packed = size * size + 8 + comps * modes
    scratch = [
        pltpu.VMEM((comps * modes, 4 * LANES), F32),
        pltpu.VMEM((comps * modes, 4 * LANES), F32),
        pltpu.VMEM((comps * 2 * modes, 4 * LANES), BF16),
        pltpu.VMEM((comps * 2 * modes, 4 * LANES), BF16),
        pltpu.VMEM((comps * 2 * modes, 2 * LANES), F32),
    ]
    half = ((comps * modes, LANES), F32)
    prods = ((comps * 2 * modes, LANES), F32)

    up, down = call(
        pack_kernel, dims, "pack", [((packed, LANES), F32)] * 2, [], modes_start, stiffness, mass, connect
    )
    below, above = from_neighbours(up, down, "sub")
    edges, edge_nodes, p_low, p_high, gram = call(
        first_kernel,
        dims,
        "first",
        [((2, size, size, LANES), F32), ((8, LANES), jnp.int32), prods, prods, ((modes, LANES), F32)],
        scratch,
        stiffness, mass, connect, up, down, below, above,
    )
    gram = total_over(gram, "sub")
    p_below, p_above = from_neighbours(p_high, p_low, "sub")
    res_low, res_high, q_low, q_high, gram, state = call(
        second_kernel,
        dims,
        "second",
        [half, half, prods, prods, ((2 * modes, LANES), F32), ((3, modes, modes), F32)],
        scratch,
        gram, stiffness, mass, connect, edges, edge_nodes, up, down, p_below, p_low, p_high, p_above,
    )
    gram = total_over(gram, "sub")
    q_below, q_above = from_neighbours(q_high, q_low, "sub")
    new_low, new_high, gram, coeff, state = call(
        third_kernel,
        dims,
        "third",
        [half, half, ((3 * modes, LANES), F32), ((modes, 2 * modes), F32), ((2, 2 * modes, 2 * modes), F32)],
        scratch,
        gram, state, stiffness, mass, connect, edges, edge_nodes, up, down,
        p_below, p_low, p_high, p_above, q_below, q_low, q_high, q_above, res_low, res_high,
    )
    gram = total_over(gram, "sub")
    result, ritz = call(
        last_kernel,
        dims,
        "last",
        [((modes, comps, count), F32), ((modes, LANES), F32)],
        [],
        gram, coeff, state, up, down, res_low, res_high, new_low, new_high,
    )
    return result, ritz[:, 0]


def solution(mesh):
    in_specs = (
        P(None, None, ("groups", "sub")),
        P(None, None, ("groups", "sub")),
        P(None, None, ("groups", "sub")),
        P(None, ("groups", "sub")),
    )
    out_specs = (P(None, None, ("groups", "sub")), P("groups"))
    return jax.shard_map(body, mesh=mesh, in_specs=in_specs, out_specs=out_specs, check_vma=False)
```

```python
import functools

import jax
import jax.numpy as jnp
from jax import lax
from jax.experimental import pallas as pl
from jax.experimental.pallas import tpu as pltpu
from jax.sharding import PartitionSpec as P

HALO = 64
LANES = 128
SUB = 8
CORNERS = 4
F32 = jnp.float32
BF16 = jnp.bfloat16

NN = (((1,), (0,)), ((), ()))
NT = (((1,), (1,)), ((), ()))
TN = (((0,), (0,)), ((), ()))


def split(value):
    high = value.astype(BF16)
    return high, (value - high.astype(F32)).astype(BF16)


def dot1(left, right, dims):
    return lax.dot_general(left, right, dims, preferred_element_type=F32)


def dot3(left, right, dims=NN):
    left_high, left_low = split(left)
    right_high, right_low = split(right)
    return dot1(left_high, right_high, dims) + (
        dot1(left_high, right_low, dims) + dot1(left_low, right_high, dims)
    )


def dotf(left, right, dims=NN):
    return lax.dot_general(
        left, right, dims, precision=lax.Precision.HIGHEST, preferred_element_type=F32
    )


def symmetric(matrix):
    return 0.5 * (matrix + matrix.T)


def whole(row):
    return jnp.broadcast_to(row,(SUB,row.shape[1]))
def eliminate(matrix, others, modes):
    tiles = modes // SUB
    chunks = []
    for other in others:
        for start in range(0, other.shape[1], LANES):
            chunks.append(other[:, start : start + LANES])
    unit = 1.0 / matrix[:1, :1]
    matrix = matrix * unit
    root = jnp.sqrt(jnp.broadcast_to(unit, (SUB, LANES)))
    left = [matrix[SUB * t : SUB * (t + 1), :] for t in range(tiles)]
    rest = [[chunk[SUB * t : SUB * (t + 1), :] for t in range(tiles)] for chunk in chunks]
    line = lax.broadcasted_iota(jnp.int32, (SUB, LANES), 0)
    outs = [[] for _ in chunks]
    for g in range(tiles):
        cols = [
            [jnp.broadcast_to(left[t][:, SUB * g + j : SUB * g + j + 1], (SUB, LANES)) for t in range(g, tiles)]
            for j in range(SUB)
        ]
        head = jnp.ones((SUB, LANES), F32)
        cross = jnp.zeros((SUB, LANES), F32)
        area = jnp.ones((SUB, LANES), F32)
        for s in range(0, SUB, 2):
            a = whole(cols[s][0][s : s + 1, :])
            b = whole(cols[s][0][s + 1 : s + 2, :])
            d = whole(cols[s + 1][0][s + 1 : s + 2, :])
            det = a * d - b * b
            inverse = 1.0 / det
            mine = (line // 2) == (s // 2)
            head = jnp.where(mine, a, head)
            cross = jnp.where(mine, b, cross)
            area = jnp.where(mine, det, area)
            p, q, r = d * inverse, b * inverse, a * inverse
            first, second = [], []
            for n, (x, y) in enumerate(zip(cols[s], cols[s + 1])):
                f0 = x * p - y * q
                f1 = y * r - x * q
                if n == 0:
                    f0 = jnp.where(line > s + 1, f0, 0.0)
                    f1 = jnp.where(line > s + 1, f1, 0.0)
                first.append(f0)
                second.append(f1)
            for j in range(s + 2, SUB):
                r0 = whole(cols[j][0][s : s + 1, :])
                r1 = whole(cols[j][0][s + 1 : s + 2, :])
                cols[j] = [c - (f0 * r0 + f1 * r1) for c, f0, f1 in zip(cols[j], first, second)]
            for group in ([left] if g + 1 < tiles else []) + rest:
                width = group[g].shape[1]
                r0 = whole(group[g][s : s + 1, :])
                r1 = whole(group[g][s + 1 : s + 2, :])
                for n, t in enumerate(range(g, tiles)):
                    if n == 0 and s + 2 == SUB:
                        continue
                    group[t] = group[t] - (first[n][:, :width] * r0 + second[n][:, :width] * r1)
        odd = (line % 2) == 1
        scale = lax.rsqrt(jnp.where(odd, area * head, head)) * root
        own = jnp.where(odd, head * scale, scale)
        mix = jnp.where(odd, cross * scale, 0.0)
        for i, group in enumerate(rest):
            width = group[g].shape[1]
            above = jnp.concatenate([group[g][SUB - 1 :, :], group[g][: SUB - 1, :]], axis=0)
            outs[i].append(own[:, :width] * group[g] - mix[:, :width] * above)
    joined = [jnp.concatenate(parts, axis=0) for parts in outs]
    results, at = [], 0
    for other in others:
        count = -(-other.shape[1] // LANES)
        part = joined[at : at + count]
        results.append(part[0] if count == 1 else jnp.concatenate(part, axis=1))
        at += count
    return results


def eye(modes):
    row = lax.broadcasted_iota(jnp.int32, (modes, modes), 0)
    col = lax.broadcasted_iota(jnp.int32, (modes, modes), 1)
    return (row == col).astype(F32)


def store_lanes(ref, value):
    rows, width = value.shape
    ref[0:rows, 0:width] = value


def element_products(dims, halves, stiff, weigh, lane, nodes, base, window, picked, high, low):
    comps, modes = dims
    place = lax.broadcasted_iota(jnp.int32, (window, LANES), 0) + base
    chosen = jnp.concatenate(
        [(place == nodes[a : a + 1, :]).astype(F32).astype(BF16) for a in range(CORNERS)], axis=1
    )
    picked[...] = dot1(halves[0][:, base : base + window], chosen, NN) + dot1(
        halves[1][:, base : base + window], chosen, NN
    )

    def one(step, unused):
        comp = step // 2
        pair = (step % 2) * 2
        totals = [jnp.zeros((modes, LANES), F32) for _ in range(4)]
        for j in range(comps * CORNERS):
            start = (j // CORNERS) * modes
            value = picked[start : start + modes, (j % CORNERS) * LANES : (j % CORNERS + 1) * LANES]
            for q in range(2):
                for m, matrix in enumerate((stiff, weigh)):
                    entry = matrix[comp * CORNERS + pair + q, j : j + 1, lane : lane + LANES]
                    totals[2 * q + m] = totals[2 * q + m] + entry * value
        for q in range(2):
            for m in range(2):
                upper, lower = split(totals[2 * q + m])
                row = pl.multiple_of((comp * 2 + m) * modes, 16)
                col = pl.multiple_of((pair + q) * LANES, LANES)
                high[pl.ds(row, modes), pl.ds(col, LANES)] = upper
                low[pl.ds(row, modes), pl.ds(col, LANES)] = lower
        return unused

    lax.fori_loop(0, comps * 2, one, 0)
    target = chosen[LANES - base : 3 * LANES - base, :]
    return dot1(high[...], target, NT) + dot1(low[...], target, NT)


def own_products(dims, halves, stiffness, mass, connect, picked, high, low, out):
    nodes = connect[...] + (LANES - HALO)
    for number in range(2):
        lane = number * LANES
        total = element_products(
            dims, halves, stiffness, mass, lane, nodes[:, lane : lane + LANES], lane, 3 * LANES, picked, high, low
        )
        if number == 0:
            out[...] = total
        else:
            out[...] += total


def edge_products(dims, halves, edges, edge_nodes, picked, high, low, out):
    out[...] += element_products(
        dims, halves, edges.at[0], edges.at[1], 0, edge_nodes, 0, 4 * LANES, picked, high, low
    )


def grams(basis, products, dims):
    comps, modes = dims
    total = None
    for c in range(comps):
        left = jnp.concatenate([part[c * modes : (c + 1) * modes, :] for part in basis], axis=0)
        right = products[c * 2 * modes : (c + 1) * 2 * modes, :]
        term = dot3(left, right, NT)
        total = term if total is None else total + term
    return total


def pack_kernel(dims, stiffness, mass, connect, up, down):
    comps, modes = dims
    size = comps * CORNERS
    first = lax.broadcasted_iota(jnp.int32, (size, LANES), 1) < HALO

    def one(i, unused):
        row = pl.multiple_of(i * size, 8)
        up[pl.ds(row, size), :] = jnp.where(
            first, pltpu.roll(stiffness[i, :, LANES:], HALO, 1), mass[i, :, LANES:]
        )
        down[pl.ds(row, size), :] = jnp.where(
            first, stiffness[i, :, :LANES], pltpu.roll(mass[i, :, :LANES], HALO, 1)
        )
        return unused

    lax.fori_loop(0, size, one, 0)
    links = connect[...].astype(F32)
    pad = jnp.zeros((SUB - CORNERS, LANES), F32)
    top = size * size
    up[top : top + SUB, :] = jnp.concatenate([pltpu.roll(links[:, LANES:], HALO, 1), pad], axis=0)
    down[top : top + SUB, :] = jnp.concatenate([links[:, :LANES], pad], axis=0)


def first_kernel(dims, block, below, above, stiffness, mass, connect, out, picked, high, low):
    ext = jnp.concatenate([below[...], block[...], above[...]], axis=1)
    own_products(dims, split(ext), stiffness, mass, connect, picked, high, low, out)


def edge_kernel(dims, block, below, above, part, from_below, from_above, connect, edges, edge_nodes, prod_low, prod_high, gram, picked, high, low, out):
    comps, modes = dims
    size = comps * CORNERS
    top = size * size
    first = lax.broadcasted_iota(jnp.int32, (size, LANES), 1) < HALO

    def one(i, unused):
        row = pl.multiple_of(i * size, 8)
        lower = from_below[pl.ds(row, size), :]
        upper = from_above[pl.ds(row, size), :]
        edges[0, i] = jnp.where(first, lower, pltpu.roll(upper, HALO, 1))
        edges[1, i] = jnp.where(first, pltpu.roll(lower, HALO, 1), upper)
        return unused

    lax.fori_loop(0, size, one, 0)
    count = connect.shape[1]
    before = from_below[top : top + SUB, :] + (LANES - HALO - count)
    after = pltpu.roll(from_above[top : top + SUB, :], HALO, 1) + (LANES - HALO + count)
    nodes = jnp.where(first[:SUB], before, after).astype(jnp.int32)
    edge_nodes[...] = nodes
    ext = jnp.concatenate([below[...], block[...], above[...]], axis=1)
    out[...] = part[...]
    edge_products(dims, split(ext), edges, nodes, picked, high, low, out)
    prod_low[...] = out[:, :LANES]
    prod_high[...] = out[:, LANES:]
    store_lanes(gram, grams([block[...]], out[...], dims))


def start_all(sources, targets, sems):
    copies = [pltpu.make_async_copy(a, b, sems.at[i]) for i, (a, b) in enumerate(zip(sources, targets))]
    for copy in copies:
        copy.start()
    return copies


def second_kernel(dims, gram_in, connect, edge_nodes, block, *refs):
    comps, modes = dims
    sources, refs = refs[:7], refs[7:]
    res_low, res_high, prod_low, prod_high, gram, state = refs[:6]
    ext, picked, high, low, out, *targets, sems = refs[6:]
    copies = start_all(sources, targets, sems)
    tiles, (stiffness, mass, edges) = targets[:4], targets[4:]
    reduced = gram_in[...]
    stiff_gram = symmetric(reduced[:, :modes])
    mass_gram = symmetric(reduced[:, modes : 2 * modes])
    unit = eye(modes)
    (inverse,) = eliminate(mass_gram, [unit], modes)
    (stiff_root,) = eliminate(stiff_gram, [unit], modes)
    ratio = dotf(stiff_gram, dotf(inverse, inverse, TN))
    state[0] = inverse
    state[1] = dotf(stiff_root, stiff_root, TN)
    state[2] = mass_gram
    ratio_high, ratio_low = split(ratio)
    for copy in copies[:4]:
        copy.wait()
    for c in range(comps):
        for tile, part in enumerate(tiles):
            row = c * 2 * modes
            right_high, right_low = split(part[row + modes : row + 2 * modes, :])
            moved = dot1(ratio_high, right_high, NN) + (dot1(ratio_high, right_low, NN) + dot1(ratio_low, right_high, NN))
            ext[c * modes : (c + 1) * modes, tile * LANES : (tile + 1) * LANES] = part[row : row + modes, :] - moved
    for copy in copies[4:]:
        copy.wait()
    halves = split(ext[...])
    own_products(dims, halves, stiffness, mass, connect, picked, high, low, out)
    edge_products(dims, halves, edges, edge_nodes[...], picked, high, low, out)
    prod_low[...] = out[:, :LANES]
    prod_high[...] = out[:, LANES:]
    res_low[...] = ext[:, LANES : 2 * LANES]
    res_high[...] = ext[:, 2 * LANES : 3 * LANES]
    store_lanes(gram, grams([block[...], ext[:, LANES : 3 * LANES]], out[...], dims))


def small_step(reduced, solver, mass_old, start, modes):
    rows = reduced.shape[0]
    old = rows - modes
    turned = reduced.T
    cross = reduced[:old, :modes]
    corner = symmetric(reduced[old:, :modes])
    mass_cross = reduced[:old, modes : 2 * modes]
    mass_corner = symmetric(reduced[old:, modes : 2 * modes])
    mass_turned = turned[modes : 2 * modes, :old]
    mass_all = jnp.concatenate(
        [
            jnp.concatenate([mass_old, mass_cross], axis=1),
            jnp.concatenate([mass_turned, mass_corner], axis=1),
        ],
        axis=0,
    )
    unit = eye(modes)
    carried = dotf(turned[:modes, :old], solver)
    schur = symmetric(corner - dotf(carried, cross))
    root = jnp.concatenate(eliminate(schur, [-carried, unit], modes), axis=1)
    wide = jnp.concatenate(
        [
            jnp.concatenate([solver, jnp.zeros((old, modes), F32)], axis=1),
            jnp.zeros((modes, rows), F32),
        ],
        axis=0,
    )
    solver = wide + dotf(root, root, TN)
    pushed = dotf(start, mass_all[: start.shape[1], :])
    solved = dotf(pushed, solver)
    again = dotf(solved, mass_all)
    (pushed,) = eliminate(symmetric(dotf(solved, again, NT)), [again], modes)
    solved = dotf(pushed, solver)
    again = dotf(solved, mass_all)
    normal = symmetric(dotf(solved, again, NT))
    energy = dotf(solved, pushed, NT)
    coeff, half, root = eliminate(normal, [solved, energy, unit], modes)
    return coeff, half, root, solver, mass_all


def third_kernel(dims, gram_in, state_in, connect, edge_nodes, block, *refs):
    comps, modes = dims
    sources, refs = refs[:13], refs[13:]
    new_low, new_high, gram, coeff_out, state = refs[:5]
    ext, picked, high, low, out, *targets, sems = refs[5:]
    copies = start_all(sources, targets, sems)
    coeff, half, root, solver, mass_all = small_step(gram_in[...], state_in[1], state_in[2], state_in[0], modes)
    rayleigh = symmetric(dotf(half, root, NT))
    coeff_out[...] = coeff
    state[0] = solver
    state[1] = mass_all
    bent = dotf(rayleigh, coeff)
    mixed = jnp.concatenate([coeff[:, :modes], -bent[:, :modes], coeff[:, modes:], -bent[:, modes:]], axis=1)
    mixed_high, mixed_low = split(mixed)
    for copy in copies[:8]:
        copy.wait()
    for c in range(comps):
        for tile in range(4):
            row = c * 2 * modes
            right = jnp.concatenate([part[row : row + 2 * modes, :] for part in (targets[tile], targets[4 + tile])], axis=0)
            right_high, right_low = split(right)
            ext[c * modes : (c + 1) * modes, tile * LANES : (tile + 1) * LANES] = dot1(mixed_high, right_high, NN) + (
                dot1(mixed_high, right_low, NN) + dot1(mixed_low, right_high, NN)
            )
    for copy in copies[8:]:
        copy.wait()
    stiffness, mass, edges, res_low, res_high = targets[8:]
    halves = split(ext[...])
    own_products(dims, halves, stiffness, mass, connect, picked, high, low, out)
    edge_products(dims, halves, edges, edge_nodes[...], picked, high, low, out)
    new_low[...] = ext[:, LANES : 2 * LANES]
    new_high[...] = ext[:, 2 * LANES : 3 * LANES]
    residual = jnp.concatenate([res_low[...], res_high[...]], axis=1)
    store_lanes(gram, grams([block[...], residual, ext[:, LANES : 3 * LANES]], out[...], dims))


def last_kernel(dims, gram_in, coeff_in, state_in, block, res_low, res_high, new_low, new_high, modes_out, ritz_out):
    comps, modes = dims
    coeff, half, root, solver, mass_all = small_step(gram_in[...], state_in[0], state_in[1], coeff_in[...], modes)
    ritz_out[...] = jnp.sum(dotf(half, root, NT) * eye(modes), axis=0, keepdims=True)
    coeff_high, coeff_low = split(coeff)
    for tile, parts in enumerate(((res_low, new_low), (res_high, new_high))):
        lanes = slice(tile * LANES, (tile + 1) * LANES)
        for c in range(comps):
            rows = slice(c * modes, (c + 1) * modes)
            right = jnp.concatenate([block[rows, lanes]] + [part[rows, :] for part in parts], axis=0)
            right_high, right_low = split(right)
            modes_out[rows, lanes] = dot1(coeff_high, right_high, NN) + (
                dot1(coeff_high, right_low, NN) + dot1(coeff_low, right_high, NN)
            )


def total_over(value, axis):
    count = lax.axis_size(axis)
    if count & (count - 1):
        return lax.psum(value, axis)

    def from_partner(part, bits):
        return lax.ppermute(part, axis, [(i, i ^ bits) for i in range(count)])

    stride = 1
    while stride < count:
        if 4 * stride <= count:
            one, two, three = (from_partner(value, k * stride) for k in (1, 2, 3))
            value = (value + one) + (two + three)
            stride *= 4
        else:
            value = value + from_partner(value, stride)
            stride *= 2
    return value


def from_neighbours(upward, downward, axis):
    count = lax.axis_size(axis)
    below = lax.ppermute(upward, axis, [(i, i + 1) for i in range(count - 1)])
    above = lax.ppermute(downward, axis, [(i + 1, i) for i in range(count - 1)])
    return below, above


VMEM = pl.BlockSpec(memory_space=pltpu.VMEM)
ANY = pl.BlockSpec(memory_space=pl.ANY)


def call(kernel, dims, name, outs, scratch, operands, remote=()):
    shapes = tuple(jax.ShapeDtypeStruct(shape, dtype) for shape, dtype in outs)
    if remote:
        scratch = scratch + [pltpu.VMEM(x.shape, x.dtype) for x in remote] + [pltpu.SemaphoreType.DMA((len(remote),))]
    return pl.pallas_call(
        functools.partial(kernel, dims),
        out_shape=shapes,
        in_specs=[VMEM] * len(operands) + [ANY] * len(remote),
        out_specs=tuple(VMEM for _ in shapes),
        scratch_shapes=scratch,
        name=name,
    )(*operands, *remote)


def body(modes_start, stiffness, mass, connect):
    modes, comps, count = modes_start.shape
    size = comps * CORNERS
    dims = (comps, modes)
    rows = comps * modes
    picked = pltpu.VMEM((rows, 4 * LANES), F32)
    parts = pltpu.VMEM((2 * rows, 4 * LANES), BF16)
    total = pltpu.VMEM((2 * rows, 2 * LANES), F32)
    half = ((rows, LANES), F32)
    prods = ((2 * rows, LANES), F32)
    packed = ((size * size + SUB, LANES), F32)
    block = modes_start.transpose(1, 0, 2).reshape(rows, count)

    v_below, v_above = from_neighbours(block[:, LANES:], block[:, :LANES], "sub")
    up, down = call(pack_kernel, dims, "pack", [packed, packed], [], (stiffness, mass, connect))
    below, above = from_neighbours(up, down, "sub")
    (part,) = call(
        first_kernel,
        dims,
        "first",
        [((2 * rows, 2 * LANES), F32)],
        [picked, parts, parts],
        (block, v_below, v_above, stiffness, mass, connect),
    )
    edges, edge_nodes, p_low, p_high, gram = call(
        edge_kernel,
        dims,
        "edge",
        [((2, size, size, LANES), F32), ((SUB, LANES), jnp.int32), prods, prods, ((modes, LANES), F32)],
        [picked, parts, parts, total],
        (block, v_below, v_above, part, below, above, connect),
    )
    gram = total_over(gram, "sub")
    p_below, p_above = from_neighbours(p_high, p_low, "sub")
    scratch = [picked, picked, parts, parts, total]
    res_low, res_high, q_low, q_high, gram, state = call(
        second_kernel,
        dims,
        "second",
        [half, half, prods, prods, ((2 * modes, LANES), F32), ((3, modes, modes), F32)],
        scratch,
        (gram, connect, edge_nodes, block),
        (p_below, p_low, p_high, p_above, stiffness, mass, edges),
    )
    gram = total_over(gram, "sub")
    q_below, q_above = from_neighbours(q_high, q_low, "sub")
    new_low, new_high, gram, coeff, state = call(
        third_kernel,
        dims,
        "third",
        [half, half, ((3 * modes, LANES), F32), ((modes, 2 * modes), F32), ((2, 2 * modes, 2 * modes), F32)],
        scratch,
        (gram, state, connect, edge_nodes, block),
        (p_below, p_low, p_high, p_above, q_below, q_low, q_high, q_above, stiffness, mass, edges, res_low, res_high),
    )
    gram = total_over(gram, "sub")
    result, ritz = call(
        last_kernel,
        dims,
        "last",
        [((rows, count), F32), ((1, modes), F32)],
        [],
        (gram, coeff, state, block, res_low, res_high, new_low, new_high),
    )
    return result.reshape(comps, modes, count).transpose(1, 0, 2), ritz.reshape(modes)


def solution(mesh):
    in_specs = (
        P(None, None, ("groups", "sub")),
        P(None, None, ("groups", "sub")),
        P(None, None, ("groups", "sub")),
        P(None, ("groups", "sub")),
    )
    out_specs = (P(None, None, ("groups", "sub")), P("groups"))
    return jax.shard_map(body, mesh=mesh, in_specs=in_specs, out_specs=out_specs, check_vma=False)
```

```python
import functools

import jax
import jax.numpy as jnp
from jax import lax
from jax.experimental import pallas as pl
from jax.experimental.pallas import tpu as pltpu
from jax.sharding import PartitionSpec as P

HALO = 64
LANES = 128
SUB = 8
CORNERS = 4
F32 = jnp.float32
BF16 = jnp.bfloat16

NN = (((1,), (0,)), ((), ()))
NT = (((1,), (1,)), ((), ()))
TN = (((0,), (0,)), ((), ()))


def split(value):
    high = value.astype(BF16)
    return high, (value - high.astype(F32)).astype(BF16)


def dot1(left, right, dims):
    return lax.dot_general(left, right, dims, preferred_element_type=F32)


def dot3(left, right, dims=NN):
    left_high, left_low = split(left)
    right_high, right_low = split(right)
    return dot1(left_high, right_high, dims) + (
        dot1(left_high, right_low, dims) + dot1(left_low, right_high, dims)
    )


def dotf(left, right, dims=NN):
    return lax.dot_general(
        left, right, dims, precision=lax.Precision.HIGHEST, preferred_element_type=F32
    )


def symmetric(matrix):
    return 0.5 * (matrix + matrix.T)


def whole(row):
    return jnp.broadcast_to(row,(SUB,row.shape[1]))
def eliminate(matrix, others, modes):
    tiles = modes // SUB
    chunks = []
    for other in others:
        for start in range(0, other.shape[1], LANES):
            chunks.append(other[:, start : start + LANES])
    unit = 1.0 / matrix[:1, :1]
    matrix = matrix * unit
    root = jnp.sqrt(jnp.broadcast_to(unit, (SUB, LANES)))
    left = [matrix[SUB * t : SUB * (t + 1), :] for t in range(tiles)]
    rest = [[chunk[SUB * t : SUB * (t + 1), :] for t in range(tiles)] for chunk in chunks]
    line = lax.broadcasted_iota(jnp.int32, (SUB, LANES), 0)
    outs = [[] for _ in chunks]
    for g in range(tiles):
        cols = [
            [jnp.broadcast_to(left[t][:, SUB * g + j : SUB * g + j + 1], (SUB, LANES)) for t in range(g, tiles)]
            for j in range(SUB)
        ]
        head = jnp.ones((SUB, LANES), F32)
        cross = jnp.zeros((SUB, LANES), F32)
        area = jnp.ones((SUB, LANES), F32)
        for s in range(0, SUB, 2):
            a = whole(cols[s][0][s : s + 1, :])
            b = whole(cols[s][0][s + 1 : s + 2, :])
            d = whole(cols[s + 1][0][s + 1 : s + 2, :])
            det = a * d - b * b
            inverse = 1.0 / det
            mine = (line // 2) == (s // 2)
            head = jnp.where(mine, a, head)
            cross = jnp.where(mine, b, cross)
            area = jnp.where(mine, det, area)
            p, q, r = d * inverse, b * inverse, a * inverse
            first, second = [], []
            for n, (x, y) in enumerate(zip(cols[s], cols[s + 1])):
                f0 = x * p - y * q
                f1 = y * r - x * q
                if n == 0:
                    f0 = jnp.where(line > s + 1, f0, 0.0)
                    f1 = jnp.where(line > s + 1, f1, 0.0)
                first.append(f0)
                second.append(f1)
            for j in range(s + 2, SUB):
                r0 = whole(cols[j][0][s : s + 1, :])
                r1 = whole(cols[j][0][s + 1 : s + 2, :])
                cols[j] = [c - (f0 * r0 + f1 * r1) for c, f0, f1 in zip(cols[j], first, second)]
            for group in ([left] if g + 1 < tiles else []) + rest:
                width = group[g].shape[1]
                r0 = whole(group[g][s : s + 1, :])
                r1 = whole(group[g][s + 1 : s + 2, :])
                for n, t in enumerate(range(g, tiles)):
                    if n == 0 and s + 2 == SUB:
                        continue
                    group[t] = group[t] - (first[n][:, :width] * r0 + second[n][:, :width] * r1)
        odd = (line % 2) == 1
        scale = lax.rsqrt(jnp.where(odd, area * head, head)) * root
        own = jnp.where(odd, head * scale, scale)
        mix = jnp.where(odd, cross * scale, 0.0)
        for i, group in enumerate(rest):
            width = group[g].shape[1]
            above = jnp.concatenate([group[g][SUB - 1 :, :], group[g][: SUB - 1, :]], axis=0)
            outs[i].append(own[:, :width] * group[g] - mix[:, :width] * above)
    joined = [jnp.concatenate(parts, axis=0) for parts in outs]
    results, at = [], 0
    for other in others:
        count = -(-other.shape[1] // LANES)
        part = joined[at : at + count]
        results.append(part[0] if count == 1 else jnp.concatenate(part, axis=1))
        at += count
    return results


def eye(modes):
    row = lax.broadcasted_iota(jnp.int32, (modes, modes), 0)
    col = lax.broadcasted_iota(jnp.int32, (modes, modes), 1)
    return (row == col).astype(F32)


def store_lanes(ref, value):
    rows, width = value.shape
    ref[0:rows, 0:width] = value


def chosen_nodes(nodes, base, window):
    place = lax.broadcasted_iota(jnp.int32, (window, LANES), 0) + base
    parts = [(place == nodes[a : a + 1, :]).astype(F32).astype(BF16) for a in range(nodes.shape[0])]
    return jnp.concatenate(parts, axis=1)


def pick(halves, chosen, base, picked):
    window = chosen.shape[0]
    picked[...] = dot1(halves[0][:, base : base + window], chosen, NN) + dot1(
        halves[1][:, base : base + window], chosen, NN
    )


def multiply(dims, entries, groups, picked, high, low):
    comps, modes = dims

    def one(step, unused):
        comp = step // groups
        group = step % groups
        totals = [jnp.zeros((modes, LANES), F32) for _ in range(4)]
        for j in range(comps * CORNERS):
            start = (j // CORNERS) * modes
            value = picked[start : start + modes, (j % CORNERS) * LANES : (j % CORNERS + 1) * LANES]
            for q in range(2):
                for m in range(2):
                    totals[2 * q + m] = totals[2 * q + m] + entries(comp, group, q, m, j) * value
        for q in range(2):
            for m in range(2):
                upper, lower = split(totals[2 * q + m])
                row = pl.multiple_of((comp * 2 + m) * modes, 16)
                col = pl.multiple_of((group * 2 + q) * LANES, LANES)
                high[pl.ds(row, modes), pl.ds(col, LANES)] = upper
                low[pl.ds(row, modes), pl.ds(col, LANES)] = lower
        return unused

    lax.fori_loop(0, comps * groups, one, 0)


def place_sums(high, low, target):
    return dot1(high, target, NT) + dot1(low, target, NT)


def all_products(dims, ext, stiffness, mass, edges, connect, edge_nodes, picked, high, low, out):
    comps, modes = dims
    halves = split(ext)
    own_nodes = connect[...] + (LANES - HALO)
    for number in range(2):
        lane = number * LANES
        chosen = chosen_nodes(own_nodes[:, lane : lane + LANES], lane, 3 * LANES)
        pick(halves, chosen, lane, picked)

        def entries(comp, group, q, m, j):
            matrix = mass if m else stiffness
            return matrix[comp * CORNERS + group * 2 + q, j : j + 1, lane : lane + LANES]

        multiply(dims, entries, CORNERS // 2, picked, high, low)
        total = place_sums(high[...], low[...], chosen[LANES - lane : 3 * LANES - lane, :])
        if number == 0:
            out[...] = total
        else:
            out[...] += total
    nodes = edge_nodes[...]
    pick(halves, chosen_nodes(nodes[:CORNERS], 0, 4 * LANES), 0, picked)
    multiply(dims, lambda comp, group, q, m, j: edges[m, q * comps + comp, j : j + 1, :], 1, picked, high, low)
    first = lax.broadcasted_iota(jnp.int32, (1, LANES), 1) < HALO
    reached = jnp.concatenate(
        [jnp.where(first, nodes[3:4], nodes[2:3]), jnp.where(first, nodes[1:2], -1)], axis=0
    )
    target = chosen_nodes(reached, LANES, 2 * LANES)
    out[...] += place_sums(high[:, : 2 * LANES], low[:, : 2 * LANES], target)


def grams(basis, products, dims):
    comps, modes = dims
    total = None
    for c in range(comps):
        left = jnp.concatenate([part[c * modes : (c + 1) * modes, :] for part in basis], axis=0)
        right = products[c * 2 * modes : (c + 1) * 2 * modes, :]
        term = dot3(left, right, NT)
        total = term if total is None else total + term
    return total


def by_side(first_case, second_case):
    odd = lax.rem(lax.axis_index("sub"), 2)
    pl.when(odd == 0)(first_case)
    pl.when(odd == 1)(second_case)


def start_all(pairs, sems, first=0):
    copies = [pltpu.make_async_copy(a, b, sems.at[first + i]) for i, (a, b) in enumerate(pairs)]
    for copy in copies:
        copy.start()
    return copies


def start_sides(from_a, from_b, below, above, sems, first):
    by_side(
        lambda: start_all([(from_b, below), (from_a, above)], sems, first) and None,
        lambda: start_all([(from_a, below), (from_b, above)], sems, first) and None,
    )
    return [pltpu.make_async_copy(a, b, sems.at[first + i]) for i, (a, b) in enumerate([(from_a, below), (from_b, above)])]


def pack_kernel(dims, block, connect, stiffness, mass, side_a, side_b, high_stiff, high_mass, low_stiff, low_mass, sems):
    comps, modes = dims
    size = comps * CORNERS
    upper, lower = pl.ds(LANES, LANES), pl.ds(0, LANES)
    copies = start_all(
        [
            (stiffness.at[:, 3, :, upper], high_stiff.at[0]),
            (stiffness.at[:, 1, :, upper], high_stiff.at[1]),
            (mass.at[:, 3, :, upper], high_mass.at[0]),
            (mass.at[:, 1, :, upper], high_mass.at[1]),
            (stiffness.at[:, 2, :, lower], low_stiff),
            (mass.at[:, 2, :, lower], low_mass),
        ],
        sems,
    )
    links = connect[...].astype(F32)
    pad = jnp.zeros((SUB - CORNERS, LANES), F32)
    rows = comps * size
    first = lax.broadcasted_iota(jnp.int32, (rows, LANES), 1) < HALO
    top = 2 * rows
    for copy in copies:
        copy.wait()

    def fill(up, down):
        for slot in range(2):
            up[slot * rows : (slot + 1) * rows, :] = jnp.where(
                first, pltpu.roll(high_stiff[slot].reshape(rows, LANES), HALO, 1), high_mass[slot].reshape(rows, LANES)
            )
        down[:rows, :] = jnp.where(
            first, low_stiff[...].reshape(rows, LANES), pltpu.roll(low_mass[...].reshape(rows, LANES), HALO, 1)
        )
        down[rows:top, :] = jnp.zeros((rows, LANES), F32)
        up[top : top + SUB, :] = jnp.concatenate([pltpu.roll(links[:, LANES:], HALO, 1), pad], axis=0)
        down[top : top + SUB, :] = jnp.concatenate([links[:, :LANES], pad], axis=0)
        up[top + SUB :, :] = block[:, LANES:]
        down[top + SUB :, :] = block[:, :LANES]

    by_side(lambda: fill(side_a, side_b), lambda: fill(side_b, side_a))


def store_sides(out, side_a, side_b):
    def put(low, high):
        low[...] = out[:, :LANES]
        high[...] = out[:, LANES:]

    by_side(lambda: put(side_b, side_a), lambda: put(side_a, side_b))


def first_kernel(dims, block, connect, from_a, from_b, stiff_in, mass_in, edges, edge_nodes, side_a, side_b, gram, picked, high, low, out, below, above, stiffness, mass, sems):
    comps, modes = dims
    size = comps * CORNERS
    rows = comps * size
    top = 2 * rows
    sides = start_sides(from_a, from_b, below, above, sems, 0)
    copies = start_all([(stiff_in, stiffness), (mass_in, mass)], sems, 2)
    first = lax.broadcasted_iota(jnp.int32, (rows, LANES), 1) < HALO
    for copy in sides:
        copy.wait()
    for slot in range(2):
        lower = below[slot * rows : (slot + 1) * rows, :]
        upper = above[slot * rows : (slot + 1) * rows, :]
        rest = jnp.zeros((rows, LANES), F32)
        here = slice(slot * comps, (slot + 1) * comps)
        edges[0, here] = jnp.where(first, lower, rest if slot else pltpu.roll(upper, HALO, 1)).reshape(comps, size, LANES)
        edges[1, here] = jnp.where(first, pltpu.roll(lower, HALO, 1), rest if slot else upper).reshape(comps, size, LANES)
    count = connect.shape[1]
    before = below[top : top + SUB, :] + (LANES - HALO - count)
    after = pltpu.roll(above[top : top + SUB, :], HALO, 1) + (LANES - HALO + count)
    edge_nodes[...] = jnp.where(first[:SUB], before, after).astype(jnp.int32)
    ext = jnp.concatenate([below[top + SUB :, :], block[...], above[top + SUB :, :]], axis=1)
    for copy in copies:
        copy.wait()
    all_products(dims, ext, stiffness, mass, edges, connect, edge_nodes, picked, high, low, out)
    store_sides(out, side_a, side_b)
    store_lanes(gram, grams([block[...]], out[...], dims))


def second_kernel(dims, gram_in, connect, edge_nodes, block, from_a, from_b, own_a, own_b, stiff_in, mass_in, edges_in, residual, side_a, side_b, gram, state, picked, high, low, out, below, above, lower, upper, stiffness, mass, edges, sems):
    comps, modes = dims
    tiles = (below, lower, upper, above)
    copies = start_sides(from_a, from_b, below, above, sems, 0)
    copies += start_sides(own_a, own_b, lower, upper, sems, 2)
    others = start_all([(stiff_in, stiffness), (mass_in, mass), (edges_in, edges)], sems, 4)
    reduced = gram_in[...]
    stiff_gram = symmetric(reduced[:, :modes])
    mass_gram = symmetric(reduced[:, modes : 2 * modes])
    unit = eye(modes)
    (inverse,) = eliminate(mass_gram, [unit], modes)
    (stiff_root,) = eliminate(stiff_gram, [unit], modes)
    ratio = dotf(stiff_gram, dotf(inverse, inverse, TN))
    state[0] = inverse
    state[1] = dotf(stiff_root, stiff_root, TN)
    state[2] = mass_gram
    ratio_high, ratio_low = split(ratio)
    for copy in copies:
        copy.wait()
    pieces = []
    for c in range(comps):
        row = c * 2 * modes
        left = jnp.concatenate([part[row : row + modes, :] for part in tiles], axis=1)
        right_high, right_low = split(jnp.concatenate([part[row + modes : row + 2 * modes, :] for part in tiles], axis=1))
        pieces.append(
            left - (dot1(ratio_high, right_high, NN) + (dot1(ratio_high, right_low, NN) + dot1(ratio_low, right_high, NN)))
        )
    ext = jnp.concatenate(pieces, axis=0)
    for copy in others:
        copy.wait()
    residual[...] = ext[:, LANES : 3 * LANES]
    all_products(dims, ext, stiffness, mass, edges, connect, edge_nodes, picked, high, low, out)
    store_sides(out, side_a, side_b)
    store_lanes(gram, grams([block[...], residual[...]], out[...], dims))


def small_step(reduced, solver, mass_old, start, modes):
    rows = reduced.shape[0]
    old = rows - modes
    turned = reduced.T
    cross = reduced[:old, :modes]
    corner = symmetric(reduced[old:, :modes])
    mass_cross = reduced[:old, modes : 2 * modes]
    mass_corner = symmetric(reduced[old:, modes : 2 * modes])
    mass_turned = turned[modes : 2 * modes, :old]
    mass_all = jnp.concatenate(
        [
            jnp.concatenate([mass_old, mass_cross], axis=1),
            jnp.concatenate([mass_turned, mass_corner], axis=1),
        ],
        axis=0,
    )
    unit = eye(modes)
    carried = dotf(turned[:modes, :old], solver)
    schur = symmetric(corner - dotf(carried, cross))
    root = jnp.concatenate(eliminate(schur, [-carried, unit], modes), axis=1)
    wide = jnp.concatenate(
        [
            jnp.concatenate([solver, jnp.zeros((old, modes), F32)], axis=1),
            jnp.zeros((modes, rows), F32),
        ],
        axis=0,
    )
    solver = wide + dotf(root, root, TN)
    pushed = dotf(start, mass_all[: start.shape[1], :])
    solved = dotf(pushed, solver)
    again = dotf(solved, mass_all)
    (pushed,) = eliminate(symmetric(dotf(solved, again, NT)), [again], modes)
    solved = dotf(pushed, solver)
    again = dotf(solved, mass_all)
    normal = symmetric(dotf(solved, again, NT))
    energy = dotf(solved, pushed, NT)
    coeff, half, root = eliminate(normal, [solved, energy, unit], modes)
    return coeff, half, root, solver, mass_all


def third_kernel(dims, gram_in, state_in, connect, edge_nodes, block, residual, from_a, from_b, own_a, own_b, more_a, more_b, new_a, new_b, stiff_in, mass_in, edges_in, new, gram, coeff_out, state, picked, high, low, out, below, above, lower, upper, new_below, new_above, new_lower, new_upper, stiffness, mass, edges, sems):
    comps, modes = dims
    tiles = ((below, new_below), (lower, new_lower), (upper, new_upper), (above, new_above))
    copies = start_sides(from_a, from_b, below, above, sems, 0)
    copies += start_sides(own_a, own_b, lower, upper, sems, 2)
    copies += start_sides(more_a, more_b, new_below, new_above, sems, 4)
    copies += start_sides(new_a, new_b, new_lower, new_upper, sems, 6)
    others = start_all([(stiff_in, stiffness), (mass_in, mass), (edges_in, edges)], sems, 8)
    coeff, half, root, solver, mass_all = small_step(gram_in[...], state_in[1], state_in[2], state_in[0], modes)
    rayleigh = symmetric(dotf(half, root, NT))
    coeff_out[...] = coeff
    state[0] = solver
    state[1] = mass_all
    bent = dotf(rayleigh, coeff)
    mixed = jnp.concatenate([coeff[:, :modes], -bent[:, :modes], coeff[:, modes:], -bent[:, modes:]], axis=1)
    mixed_high, mixed_low = split(mixed)
    for copy in copies:
        copy.wait()
    pieces = []
    for c in range(comps):
        rows = slice(c * 2 * modes, (c + 1) * 2 * modes)
        right = jnp.concatenate(
            [jnp.concatenate([part[rows, :] for part in parts], axis=0) for parts in tiles], axis=1
        )
        right_high, right_low = split(right)
        pieces.append(dot1(mixed_high, right_high, NN) + (dot1(mixed_high, right_low, NN) + dot1(mixed_low, right_high, NN)))
    ext = jnp.concatenate(pieces, axis=0)
    for copy in others:
        copy.wait()
    new[...] = ext[:, LANES : 3 * LANES]
    all_products(dims, ext, stiffness, mass, edges, connect, edge_nodes, picked, high, low, out)
    store_lanes(gram, grams([block[...], residual[...], new[...]], out[...], dims))


def last_kernel(dims, gram_in, coeff_in, state_in, block, residual, new, modes_out, ritz_out):
    comps, modes = dims
    coeff, half, root, solver, mass_all = small_step(gram_in[...], state_in[0], state_in[1], coeff_in[...], modes)
    ritz_out[...] = jnp.sum(dotf(half, root, NT) * eye(modes), axis=0, keepdims=True)
    coeff_high, coeff_low = split(coeff)
    for c in range(comps):
        rows = slice(c * modes, (c + 1) * modes)
        right_high, right_low = split(jnp.concatenate([part[rows, :] for part in (block, residual, new)], axis=0))
        modes_out[rows, :] = dot1(coeff_high, right_high, NN) + (
            dot1(coeff_high, right_low, NN) + dot1(coeff_low, right_high, NN)
        )


def total_over(value, axis):
    count = lax.axis_size(axis)
    if count & (count - 1):
        return lax.psum(value, axis)

    def from_partner(part, bits):
        return lax.ppermute(part, axis, [(i, i ^ bits) for i in range(count)])

    stride = 1
    while stride < count:
        if 4 * stride <= count:
            one, two, three = (from_partner(value, k * stride) for k in (1, 2, 3))
            value = (value + one) + (two + three)
            stride *= 4
        else:
            value = value + from_partner(value, stride)
            stride *= 2
    return value


def exchange(side_a, side_b, axis):
    count = lax.axis_size(axis)

    def swap(value, start):
        pairs = [(i, i + 1) for i in range(start, count - 1, 2)]
        return lax.ppermute(value, axis, pairs + [(b, a) for a, b in pairs])

    return swap(side_a, 0), swap(side_b, 1)


VMEM = pl.BlockSpec(memory_space=pltpu.VMEM)
HBM = pl.BlockSpec(memory_space=pltpu.HBM)


def call(kernel, dims, name, outs, scratch, operands, remote):
    shapes = tuple(jax.ShapeDtypeStruct(shape, dtype) for shape, dtype in outs)
    return pl.pallas_call(
        functools.partial(kernel, dims),
        out_shape=shapes,
        in_specs=[VMEM] * len(operands) + [HBM] * len(remote),
        out_specs=tuple(VMEM for _ in shapes),
        scratch_shapes=scratch,
        name=name,
    )(*operands, *remote)


def room(*arrays):
    return [pltpu.VMEM(x.shape, x.dtype) for x in arrays]


def body(modes_start, stiffness, mass, connect):
    modes, comps, count = modes_start.shape
    size = comps * CORNERS
    dims = (comps, modes)
    rows = comps * modes
    work = [
        pltpu.VMEM((rows, CORNERS * LANES), F32),
        pltpu.VMEM((2 * rows, CORNERS * LANES), BF16),
        pltpu.VMEM((2 * rows, CORNERS * LANES), BF16),
        pltpu.VMEM((2 * rows, count), F32),
    ]
    wide = ((rows, count), F32)
    side = ((2 * rows, LANES), F32)
    packed = ((2 * comps * size + SUB + rows, LANES), F32)
    edge = pltpu.VMEM((comps, size, LANES), F32)
    edges_pair = pltpu.VMEM((2, comps, size, LANES), F32)
    sems = pltpu.SemaphoreType.DMA
    block = modes_start.transpose(1, 0, 2).reshape(rows, count)

    by_corner = [x.reshape(comps, CORNERS, size, count) for x in (stiffness, mass)]
    side_a, side_b = call(
        pack_kernel,
        dims,
        "pack",
        [packed, packed],
        [edges_pair, edges_pair, edge, edge, sems((6,))],
        (block, connect),
        by_corner,
    )
    from_a, from_b = exchange(side_a, side_b, "sub")
    edges, edge_nodes, p_a, p_b, gram = call(
        first_kernel,
        dims,
        "first",
        [((2, 2 * comps, size, LANES), F32), ((SUB, LANES), jnp.int32), side, side, ((modes, LANES), F32)],
        work + room(from_a, from_b, stiffness, mass) + [sems((4,))],
        (block, connect),
        (from_a, from_b, stiffness, mass),
    )
    gram = total_over(gram, "sub")
    p_from_a, p_from_b = exchange(p_a, p_b, "sub")
    p = (p_from_a, p_from_b, p_a, p_b)
    residual, q_a, q_b, gram, state = call(
        second_kernel,
        dims,
        "second",
        [wide, side, side, ((2 * modes, LANES), F32), ((3, modes, modes), F32)],
        work + room(*p, stiffness, mass, edges) + [sems((7,))],
        (gram, connect, edge_nodes, block),
        (*p, stiffness, mass, edges),
    )
    gram = total_over(gram, "sub")
    q_from_a, q_from_b = exchange(q_a, q_b, "sub")
    q = (q_from_a, q_from_b, q_a, q_b)
    new, gram, coeff, state = call(
        third_kernel,
        dims,
        "third",
        [wide, ((3 * modes, LANES), F32), ((modes, 2 * modes), F32), ((2, 2 * modes, 2 * modes), F32)],
        work + room(*p, *q, stiffness, mass, edges) + [sems((11,))],
        (gram, state, connect, edge_nodes, block, residual),
        (*p, *q, stiffness, mass, edges),
    )
    gram = total_over(gram, "sub")
    result, ritz = call(
        last_kernel,
        dims,
        "last",
        [wide, ((1, modes), F32)],
        [],
        (gram, coeff, state, block, residual, new),
        (),
    )
    return result.reshape(comps, modes, count).transpose(1, 0, 2), ritz.reshape(modes)


def solution(mesh):
    in_specs = (
        P(None, None, ("groups", "sub")),
        P(None, None, ("groups", "sub")),
        P(None, None, ("groups", "sub")),
        P(None, ("groups", "sub")),
    )
    out_specs = (P(None, None, ("groups", "sub")), P("groups"))
    return jax.shard_map(body, mesh=mesh, in_specs=in_specs, out_specs=out_specs, check_vma=False)
```

```python
import functools

import jax
import jax.numpy as jnp
from jax import lax
from jax.experimental import pallas as pl
from jax.experimental.pallas import tpu as pltpu
from jax.sharding import PartitionSpec as P


HALO = 64
LANES = 128
SUB = 8
CORNERS = 4
F32 = jnp.float32
BF16 = jnp.bfloat16

NN = (((1,), (0,)), ((), ()))
NT = (((1,), (1,)), ((), ()))
TN = (((0,), (0,)), ((), ()))


def split(value):
    high = value.astype(BF16)
    return high, (value - high.astype(F32)).astype(BF16)


def dot1(left, right, dims):
    return lax.dot_general(left, right, dims, preferred_element_type=F32)


def dot3(left, right, dims=NN):
    left_high, left_low = split(left)
    right_high, right_low = split(right)
    return dot1(left_high, right_high, dims) + (
        dot1(left_high, right_low, dims) + dot1(left_low, right_high, dims)
    )


def dotf(left, right, dims=NN):
    return lax.dot_general(
        left, right, dims, precision=lax.Precision.HIGHEST, preferred_element_type=F32
    )


def symmetric(matrix):
    return 0.5 * (matrix + matrix.T)


def whole(row):
    return jnp.broadcast_to(row,(SUB,row.shape[1]))


def eliminate(matrix, others, modes):
    tiles = modes // SUB
    chunks = []
    for other in others:
        for start in range(0, other.shape[1], LANES):
            chunks.append(other[:, start : start + LANES])
    unit = 1.0 / matrix[:1, :1]
    matrix = matrix * unit
    root = jnp.sqrt(jnp.broadcast_to(unit, (SUB, LANES)))
    left = [matrix[SUB * t : SUB * (t + 1), :] for t in range(tiles)]
    rest = [[chunk[SUB * t : SUB * (t + 1), :] for t in range(tiles)] for chunk in chunks]
    line = lax.broadcasted_iota(jnp.int32, (SUB, LANES), 0)
    outs = [[] for _ in chunks]
    for g in range(tiles):
        cols = [
            [jnp.broadcast_to(left[t][:, SUB * g + j : SUB * g + j + 1], (SUB, LANES)) for t in range(g, tiles)]
            for j in range(SUB)
        ]
        head = jnp.ones((SUB, LANES), F32)
        cross = jnp.zeros((SUB, LANES), F32)
        area = jnp.ones((SUB, LANES), F32)
        for s in range(0, SUB, 2):
            a = whole(cols[s][0][s : s + 1, :])
            b = whole(cols[s][0][s + 1 : s + 2, :])
            d = whole(cols[s + 1][0][s + 1 : s + 2, :])
            det = a * d - b * b
            inverse = 1.0 / det
            mine = (line // 2) == (s // 2)
            head = jnp.where(mine, a, head)
            cross = jnp.where(mine, b, cross)
            area = jnp.where(mine, det, area)
            p, q, r = d * inverse, b * inverse, a * inverse
            first, second = [], []
            for n, (x, y) in enumerate(zip(cols[s], cols[s + 1])):
                f0 = x * p - y * q
                f1 = y * r - x * q
                if n == 0:
                    f0 = jnp.where(line > s + 1, f0, 0.0)
                    f1 = jnp.where(line > s + 1, f1, 0.0)
                first.append(f0)
                second.append(f1)
            for j in range(s + 2, SUB):
                r0 = whole(cols[j][0][s : s + 1, :])
                r1 = whole(cols[j][0][s + 1 : s + 2, :])
                cols[j] = [c - (f0 * r0 + f1 * r1) for c, f0, f1 in zip(cols[j], first, second)]
            for group in ([left] if g + 1 < tiles else []) + rest:
                width = group[g].shape[1]
                r0 = whole(group[g][s : s + 1, :])
                r1 = whole(group[g][s + 1 : s + 2, :])
                for n, t in enumerate(range(g, tiles)):
                    if n == 0 and s + 2 == SUB:
                        continue
                    group[t] = group[t] - (first[n][:, :width] * r0 + second[n][:, :width] * r1)
        odd = (line % 2) == 1
        scale = lax.rsqrt(jnp.where(odd, area * head, head)) * root
        own = jnp.where(odd, head * scale, scale)
        mix = jnp.where(odd, cross * scale, 0.0)
        for i, group in enumerate(rest):
            width = group[g].shape[1]
            above = jnp.concatenate([group[g][SUB - 1 :, :], group[g][: SUB - 1, :]], axis=0)
            outs[i].append(own[:, :width] * group[g] - mix[:, :width] * above)
    joined = [jnp.concatenate(parts, axis=0) for parts in outs]
    results, at = [], 0
    for other in others:
        count = -(-other.shape[1] // LANES)
        part = joined[at : at + count]
        results.append(part[0] if count == 1 else jnp.concatenate(part, axis=1))
        at += count
    return results


def eye(modes):
    row = lax.broadcasted_iota(jnp.int32, (modes, modes), 0)
    col = lax.broadcasted_iota(jnp.int32, (modes, modes), 1)
    return (row == col).astype(F32)


def store_lanes(ref, value):
    rows, width = value.shape
    ref[0:rows, 0:width] = value


def chosen_nodes(nodes, base, window):
    place = lax.broadcasted_iota(jnp.int32, (window, LANES), 0) + base
    parts = [(place == nodes[a : a + 1, :]).astype(F32).astype(BF16) for a in range(nodes.shape[0])]
    return jnp.concatenate(parts, axis=1)


def pick(halves, chosen, base, picked):
    window = chosen.shape[0]
    picked[...] = dot1(halves[0][:, base : base + window], chosen, NN) + dot1(
        halves[1][:, base : base + window], chosen, NN
    )


def multiply(dims, entries, groups, picked, high, low):
    comps, modes = dims

    def one(step, unused):
        comp = step // groups
        group = step % groups
        totals = [jnp.zeros((modes, LANES), F32) for _ in range(4)]
        for j in range(comps * CORNERS):
            start = (j // CORNERS) * modes
            value = picked[start : start + modes, (j % CORNERS) * LANES : (j % CORNERS + 1) * LANES]
            for q in range(2):
                for m in range(2):
                    totals[2 * q + m] = totals[2 * q + m] + entries(comp, group, q, m, j) * value
        for q in range(2):
            for m in range(2):
                upper, lower = split(totals[2 * q + m])
                row = pl.multiple_of((comp * 2 + m) * modes, 16)
                col = pl.multiple_of((group * 2 + q) * LANES, LANES)
                high[pl.ds(row, modes), pl.ds(col, LANES)] = upper
                low[pl.ds(row, modes), pl.ds(col, LANES)] = lower
        return unused

    lax.fori_loop(0, comps * groups, one, 0, unroll=2)


def place_sums(high, low, target):
    return dot1(high, target, NT) + dot1(low, target, NT)


def all_products(dims, ext, stiffness, mass, edges, connect, edge_nodes, picked, high, low, out):
    halves = split(ext)
    own_products(dims, halves, stiffness, mass, connect, picked, high, low, out)
    edge_products(dims, halves, edges, edge_nodes, picked, high, low, out)


def own_products(dims, halves, stiffness, mass, connect, picked, high, low, out):
    own_nodes = connect[...] + (LANES - HALO)
    for number in range(2):
        lane = number * LANES
        chosen = chosen_nodes(own_nodes[:, lane : lane + LANES], lane, 3 * LANES)
        pick(halves, chosen, lane, picked)

        def entries(comp, group, q, m, j):
            matrix = mass if m else stiffness
            return matrix[comp * CORNERS + group * 2 + q, j : j + 1, lane : lane + LANES]

        multiply(dims, entries, CORNERS // 2, picked, high, low)
        total = place_sums(high[...], low[...], chosen[LANES - lane : 3 * LANES - lane, :])
        if number == 0:
            out[...] = total
        else:
            out[...] += total


def edge_products(dims, halves, edges, edge_nodes, picked, high, low, out):
    comps, _ = dims
    nodes = edge_nodes[...]
    pick(halves, chosen_nodes(nodes[:CORNERS], 0, 4 * LANES), 0, picked)
    multiply(dims, lambda comp, group, q, m, j: edges[m, q * comps + comp, j : j + 1, :], 1, picked, high, low)
    first = lax.broadcasted_iota(jnp.int32, (1, LANES), 1) < HALO
    reached = jnp.concatenate(
        [jnp.where(first, nodes[3:4], nodes[2:3]), jnp.where(first, nodes[1:2], -1)], axis=0
    )
    target = chosen_nodes(reached, LANES, 2 * LANES)
    out[...] += place_sums(high[:, : 2 * LANES], low[:, : 2 * LANES], target)


def grams(basis, products, dims):
    comps, modes = dims
    total = None
    for c in range(comps):
        left = jnp.concatenate([part[c * modes : (c + 1) * modes, :] for part in basis], axis=0)
        right = products[c * 2 * modes : (c + 1) * 2 * modes, :]
        term = dot3(left, right, NT)
        total = term if total is None else total + term
    return total


def by_side(first_case, second_case):
    odd = lax.rem(lax.axis_index("sub"), 2)
    pl.when(odd == 0)(first_case)
    pl.when(odd == 1)(second_case)


def start_all(pairs, sems, first=0):
    copies = [pltpu.make_async_copy(a, b, sems.at[first + i]) for i, (a, b) in enumerate(pairs)]
    for copy in copies:
        copy.start()
    return copies


def start_sides(from_a, from_b, below, above, sems, first):
    by_side(
        lambda: start_all([(from_b, below), (from_a, above)], sems, first) and None,
        lambda: start_all([(from_a, below), (from_b, above)], sems, first) and None,
    )
    return [pltpu.make_async_copy(a, b, sems.at[first + i]) for i, (a, b) in enumerate([(from_a, below), (from_b, above)])]


def node_kernel(dims, block_in, block, node_a, node_b, sems):
    for copy in start_all([(block_in, block)], sems):
        copy.wait()
    store_sides(block, node_a, node_b)


def pack_kernel(dims, connect_in, stiff_in, mass_in, connect, stiffness, mass, edge_a, edge_b, sems):
    comps, _ = dims
    size = comps * CORNERS
    copies = start_all([(connect_in, connect), (stiff_in, stiffness), (mass_in, mass)], sems)
    pad = jnp.zeros((SUB - CORNERS, LANES), F32)
    rows = comps * size
    first = lax.broadcasted_iota(jnp.int32, (rows, LANES), 1) < HALO
    top = 2 * rows
    for copy in copies:
        copy.wait()
    links = connect[...].astype(F32)

    def corner(matrix, which, lane):
        return jnp.concatenate([matrix[c * CORNERS + which, :, lane : lane + LANES] for c in range(comps)], axis=0)

    def fill(up, down):
        for slot, which in enumerate((3, 1)):
            up[slot * rows : (slot + 1) * rows, :] = jnp.where(
                first, pltpu.roll(corner(stiffness, which, LANES), HALO, 1), corner(mass, which, LANES)
            )
        down[:rows, :] = jnp.where(first, corner(stiffness, 2, 0), pltpu.roll(corner(mass, 2, 0), HALO, 1))
        down[rows:top, :] = jnp.zeros((rows, LANES), F32)
        up[top:, :] = jnp.concatenate([pltpu.roll(links[:, LANES:], HALO, 1), pad], axis=0)
        down[top:, :] = jnp.concatenate([links[:, :LANES], pad], axis=0)

    by_side(lambda: fill(edge_a, edge_b), lambda: fill(edge_b, edge_a))


def store_sides(out, side_a, side_b):
    def put(low, high):
        low[...] = out[:, :LANES]
        high[...] = out[:, LANES:]

    by_side(lambda: put(side_b, side_a), lambda: put(side_a, side_b))


def first_kernel(dims, block, connect, stiffness, mass, from_a, from_b, ext, out, picked, high, low, sems):
    below, above = ext.at[:, :LANES], ext.at[:, 3 * LANES :]
    copies = start_sides(from_a, from_b, below, above, sems, 0)
    ext[:, LANES : 3 * LANES] = block[...]
    for copy in copies:
        copy.wait()
    own_products(dims, split(ext[...]), stiffness, mass, connect, picked, high, low, out)


def edge_kernel(dims, block, connect, ext, part, from_a, from_b, edges, edge_nodes, side_a, side_b, gram, picked, high, low, out, below, above, sems):
    comps, _ = dims
    size = comps * CORNERS
    rows = comps * size
    top = 2 * rows
    copies = start_sides(from_a, from_b, below, above, sems, 0)
    first = lax.broadcasted_iota(jnp.int32, (rows, LANES), 1) < HALO
    halves = split(ext[...])
    out[...] = part[...]
    for copy in copies:
        copy.wait()
    for slot in range(2):
        lower = below[slot * rows : (slot + 1) * rows, :]
        upper = above[slot * rows : (slot + 1) * rows, :]
        rest = jnp.zeros((rows, LANES), F32)
        here = slice(slot * comps, (slot + 1) * comps)
        edges[0, here] = jnp.where(first, lower, rest if slot else pltpu.roll(upper, HALO, 1)).reshape(comps, size, LANES)
        edges[1, here] = jnp.where(first, pltpu.roll(lower, HALO, 1), rest if slot else upper).reshape(comps, size, LANES)
    count = connect.shape[1]
    before = below[top:, :] + (LANES - HALO - count)
    after = pltpu.roll(above[top:, :], HALO, 1) + (LANES - HALO + count)
    edge_nodes[...] = jnp.where(first[:SUB], before, after).astype(jnp.int32)
    edge_products(dims, halves, edges, edge_nodes, picked, high, low, out)
    store_sides(out, side_a, side_b)
    store_lanes(gram, grams([block[...]], out[...], dims))


def second_kernel(dims, gram_in, connect, edge_nodes, block, stiffness, mass, edges, from_a, from_b, own_a, own_b, residual, side_a, side_b, gram, state, picked, high, low, out, below, above, lower, upper, sems):
    comps, modes = dims
    tiles = (below, lower, upper, above)
    copies = start_sides(from_a, from_b, below, above, sems, 0)
    copies += start_sides(own_a, own_b, lower, upper, sems, 2)
    reduced = gram_in[...]
    stiff_gram = symmetric(reduced[:, :modes])
    mass_gram = symmetric(reduced[:, modes : 2 * modes])
    unit = eye(modes)
    (inverse,) = eliminate(mass_gram, [unit], modes)
    (stiff_root,) = eliminate(stiff_gram, [unit], modes)
    ratio = dotf(stiff_gram, dotf(inverse, inverse, TN))
    state[0] = inverse
    state[1] = dotf(stiff_root, stiff_root, TN)
    state[2] = mass_gram
    ratio_high, ratio_low = split(ratio)
    for copy in copies:
        copy.wait()
    pieces = []
    for c in range(comps):
        row = c * 2 * modes
        left = jnp.concatenate([part[row : row + modes, :] for part in tiles], axis=1)
        right_high, right_low = split(jnp.concatenate([part[row + modes : row + 2 * modes, :] for part in tiles], axis=1))
        pieces.append(
            left - (dot1(ratio_high, right_high, NN) + (dot1(ratio_high, right_low, NN) + dot1(ratio_low, right_high, NN)))
        )
    ext = jnp.concatenate(pieces, axis=0)
    residual[...] = ext[:, LANES : 3 * LANES]
    all_products(dims, ext, stiffness, mass, edges, connect, edge_nodes, picked, high, low, out)
    store_sides(out, side_a, side_b)
    store_lanes(gram, grams([block[...], residual[...]], out[...], dims))


def small_step(reduced, solver, mass_old, start, modes):
    rows = reduced.shape[0]
    old = rows - modes
    turned = reduced.T
    cross = reduced[:old, :modes]
    corner = symmetric(reduced[old:, :modes])
    mass_cross = reduced[:old, modes : 2 * modes]
    mass_corner = symmetric(reduced[old:, modes : 2 * modes])
    mass_turned = turned[modes : 2 * modes, :old]
    mass_all = jnp.concatenate(
        [
            jnp.concatenate([mass_old, mass_cross], axis=1),
            jnp.concatenate([mass_turned, mass_corner], axis=1),
        ],
        axis=0,
    )
    unit = eye(modes)
    carried = dotf(turned[:modes, :old], solver)
    schur = symmetric(corner - dotf(carried, cross))
    root = jnp.concatenate(eliminate(schur, [-carried, unit], modes), axis=1)
    wide = jnp.concatenate(
        [
            jnp.concatenate([solver, jnp.zeros((old, modes), F32)], axis=1),
            jnp.zeros((modes, rows), F32),
        ],
        axis=0,
    )
    solver = wide + dotf(root, root, TN)
    pushed = dotf(start, mass_all[: start.shape[1], :])
    solved = dotf(pushed, solver)
    again = dotf(solved, mass_all)
    (pushed,) = eliminate(symmetric(dotf(solved, again, NT)), [again], modes)
    solved = dotf(pushed, solver)
    again = dotf(solved, mass_all)
    normal = symmetric(dotf(solved, again, NT))
    energy = dotf(solved, pushed, NT)
    coeff, half, root = eliminate(normal, [solved, energy, unit], modes)
    return coeff, half, root, solver, mass_all


def third_kernel(dims, gram_in, state_in, connect, edge_nodes, block, residual, stiffness, mass, edges, from_a, from_b, own_a, own_b, more_a, more_b, new_a, new_b, new, gram, coeff_out, state, picked, high, low, out, below, above, lower, upper, new_below, new_above, new_lower, new_upper, sems):
    comps, modes = dims
    tiles = ((below, new_below), (lower, new_lower), (upper, new_upper), (above, new_above))
    copies = start_sides(from_a, from_b, below, above, sems, 0)
    copies += start_sides(own_a, own_b, lower, upper, sems, 2)
    copies += start_sides(more_a, more_b, new_below, new_above, sems, 4)
    copies += start_sides(new_a, new_b, new_lower, new_upper, sems, 6)
    coeff, half, root, solver, mass_all = small_step(gram_in[...], state_in[1], state_in[2], state_in[0], modes)
    rayleigh = symmetric(dotf(half, root, NT))
    coeff_out[...] = coeff
    state[0] = solver
    state[1] = mass_all
    bent = dotf(rayleigh, coeff)
    mixed = jnp.concatenate([coeff[:, :modes], -bent[:, :modes], coeff[:, modes:], -bent[:, modes:]], axis=1)
    mixed_high, mixed_low = split(mixed)
    for copy in copies:
        copy.wait()
    pieces = []
    for c in range(comps):
        rows = slice(c * 2 * modes, (c + 1) * 2 * modes)
        right = jnp.concatenate(
            [jnp.concatenate([part[rows, :] for part in parts], axis=0) for parts in tiles], axis=1
        )
        right_high, right_low = split(right)
        pieces.append(dot1(mixed_high, right_high, NN) + (dot1(mixed_high, right_low, NN) + dot1(mixed_low, right_high, NN)))
    ext = jnp.concatenate(pieces, axis=0)
    new[...] = ext[:, LANES : 3 * LANES]
    all_products(dims, ext, stiffness, mass, edges, connect, edge_nodes, picked, high, low, out)
    store_lanes(gram, grams([block[...], residual[...], new[...]], out[...], dims))


def last_kernel(dims, gram_in, coeff_in, state_in, block, residual, new, modes_out, ritz_out):
    comps, modes = dims
    coeff, half, root, _, _ = small_step(gram_in[...], state_in[0], state_in[1], coeff_in[...], modes)
    ritz_out[...] = jnp.sum(dotf(half, root, NT) * eye(modes), axis=0, keepdims=True)
    coeff_high, coeff_low = split(coeff)
    for c in range(comps):
        rows = slice(c * modes, (c + 1) * modes)
        right_high, right_low = split(jnp.concatenate([part[rows, :] for part in (block, residual, new)], axis=0))
        modes_out[rows, :] = dot1(coeff_high, right_high, NN) + (
            dot1(coeff_high, right_low, NN) + dot1(coeff_low, right_high, NN)
        )


def total_over(value, axis):
    count = lax.axis_size(axis)
    if count & (count - 1):
        return lax.psum(value, axis)

    def from_partner(part, bits):
        return lax.ppermute(part, axis, [(i, i ^ bits) for i in range(count)])

    stride = 1
    while stride < count:
        if 4 * stride <= count:
            one, two, three = (from_partner(value, k * stride) for k in (1, 2, 3))
            value = (value + one) + (two + three)
            stride *= 4
        else:
            value = value + from_partner(value, stride)
            stride *= 2
    return value


def exchange(side_a, side_b, axis):
    count = lax.axis_size(axis)

    def swap(value, start):
        pairs = [(i, i + 1) for i in range(start, count - 1, 2)]
        return lax.ppermute(value, axis, pairs + [(b, a) for a, b in pairs])

    from_a = swap(side_a, 0)
    from_b = swap(side_b, 1)
    return from_a, from_b


VMEM = pl.BlockSpec(memory_space=pltpu.VMEM)
HBM = pl.BlockSpec(memory_space=pltpu.HBM)


def call(kernel, dims, outs, scratch, operands, remote):
    shapes = tuple(kind(shape, dtype) for kind, shape, dtype in outs)
    operands = [pltpu.with_memory_space_constraint(x, pltpu.VMEM) for x in operands]
    return pl.pallas_call(
        functools.partial(kernel, dims),
        out_shape=shapes,
        in_specs=[VMEM] * len(operands) + [HBM] * len(remote),
        out_specs=tuple(VMEM for _ in shapes),
        scratch_shapes=scratch,
        compiler_params=pltpu.CompilerParams(vmem_limit_bytes=24 << 20),
    )(*operands, *[pltpu.with_memory_space_constraint(x, pltpu.HBM) for x in remote])


def room(*arrays):
    return [pltpu.VMEM(x.shape, x.dtype) for x in arrays]


def body(modes_start, stiffness, mass, connect):
    modes, comps, count = modes_start.shape
    size = comps * CORNERS
    dims = (comps, modes)
    rows = comps * modes
    work = [
        pltpu.VMEM((rows, CORNERS * LANES), F32),
        pltpu.VMEM((2 * rows, CORNERS * LANES), BF16),
        pltpu.VMEM((2 * rows, CORNERS * LANES), BF16),
        pltpu.VMEM((2 * rows, count), F32),
    ]
    near, far = pltpu.VMEM, jax.ShapeDtypeStruct
    wide = (near, (rows, count), F32)
    side = (near, (2 * rows, LANES), F32)
    node = (near, (rows, LANES), F32)
    packed = (near, (2 * comps * size + SUB, LANES), F32)
    sems = pltpu.SemaphoreType.DMA
    block = modes_start.transpose(1, 0, 2).reshape(rows, count)

    block, node_a, node_b = call(node_kernel, dims, [wide, node, node], [sems((1,))], (), (block,))
    node_from = exchange(node_a, node_b, "sub")
    link, stiff_near, mass_near, edge_a, edge_b = call(
        pack_kernel,
        dims,
        [(near, connect.shape, connect.dtype), (near, stiffness.shape, F32), (near, mass.shape, F32), packed, packed],
        [sems((3,))],
        (),
        (connect, stiffness, mass),
    )
    edge_from = exchange(edge_a, edge_b, "sub")
    ext, part = call(
        first_kernel,
        dims,
        [(near, (rows, 2 * count), F32), (near, (2 * rows, count), F32)],
        work[:3] + [sems((2,))],
        (block, link, stiff_near, mass_near, *node_from),
        (),
    )
    edges, edge_nodes, p_a, p_b, gram = call(
        edge_kernel,
        dims,
        [(near, (2, 2 * comps, size, LANES), F32), (near, (SUB, LANES), jnp.int32), side, side, (near, (modes, LANES), F32)],
        work + room(*edge_from) + [sems((2,))],
        (block, link, ext, part, *edge_from),
        (),
    )
    gram = total_over(gram, "sub")
    p_from_a, p_from_b = exchange(p_a, p_b, "sub")
    p = (p_from_a, p_from_b, p_a, p_b)
    residual, q_a, q_b, gram, state = call(
        second_kernel,
        dims,
        [wide, side, side, (near, (2 * modes, LANES), F32), (near, (3, modes, modes), F32)],
        work + room(*p) + [sems((4,))],
        (gram, link, edge_nodes, block, stiff_near, mass_near, edges, *p),
        (),
    )
    gram = total_over(gram, "sub")
    q_from_a, q_from_b = exchange(q_a, q_b, "sub")
    q = (q_from_a, q_from_b, q_a, q_b)
    new, gram, coeff, state = call(
        third_kernel,
        dims,
        [wide, (near, (3 * modes, LANES), F32), (near, (modes, 2 * modes), F32), (near, (2, 2 * modes, 2 * modes), F32)],
        work + room(*p, *q) + [sems((8,))],
        (gram, state, link, edge_nodes, block, residual, stiff_near, mass_near, edges, *p, *q),
        (),
    )
    gram = total_over(gram, "sub")
    result, ritz = call(
        last_kernel,
        dims,
        [(far, (rows, count), F32), (far, (1, modes), F32)],
        [],
        (gram, coeff, state, block, residual, new),
        (),
    )
    return result.reshape(comps, modes, count).transpose(1, 0, 2), ritz.reshape(modes)


def solution(mesh):
    in_specs = (
        P(None, None, ("groups", "sub")),
        P(None, None, ("groups", "sub")),
        P(None, None, ("groups", "sub")),
        P(None, ("groups", "sub")),
    )
    out_specs = (P(None, None, ("groups", "sub")), P("groups"))
    return jax.shard_map(body, mesh=mesh, in_specs=in_specs, out_specs=out_specs, check_vma=False)
```

```python
import functools

import jax
import jax.numpy as jnp
from jax import lax
from jax.experimental import pallas as pl
from jax.experimental.pallas import tpu as pltpu
from jax.sharding import PartitionSpec as P


HALO = 64
LANES = 128
SUB = 8
CORNERS = 4
F32 = jnp.float32
BF16 = jnp.bfloat16

NN = (((1,), (0,)), ((), ()))
NT = (((1,), (1,)), ((), ()))
TN = (((0,), (0,)), ((), ()))


def split(value):
    high = value.astype(BF16)
    return high, (value - high.astype(F32)).astype(BF16)


def dot1(left, right, dims):
    return lax.dot_general(left, right, dims, preferred_element_type=F32)


def dot3(left, right, dims=NN):
    left_high, left_low = split(left)
    right_high, right_low = split(right)
    return dot1(left_high, right_high, dims) + (
        dot1(left_high, right_low, dims) + dot1(left_low, right_high, dims)
    )


def dotf(left, right, dims=NN):
    return lax.dot_general(
        left, right, dims, precision=lax.Precision.HIGHEST, preferred_element_type=F32
    )


def symmetric(matrix):
    return 0.5 * (matrix + matrix.T)


def whole(row):
    return jnp.broadcast_to(row,(SUB,row.shape[1]))


def eliminate(matrix, others, modes):
    tiles = modes // SUB
    chunks = []
    for other in others:
        for start in range(0, other.shape[1], LANES):
            chunks.append(other[:, start : start + LANES])
    unit = 1.0 / matrix[:1, :1]
    matrix = matrix * unit
    root = jnp.sqrt(jnp.broadcast_to(unit, (SUB, LANES)))
    left = [matrix[SUB * t : SUB * (t + 1), :] for t in range(tiles)]
    rest = [[chunk[SUB * t : SUB * (t + 1), :] for t in range(tiles)] for chunk in chunks]
    line = lax.broadcasted_iota(jnp.int32, (SUB, LANES), 0)
    outs = [[] for _ in chunks]
    for g in range(tiles):
        cols = [
            [jnp.broadcast_to(left[t][:, SUB * g + j : SUB * g + j + 1], (SUB, LANES)) for t in range(g, tiles)]
            for j in range(SUB)
        ]
        head = jnp.ones((SUB, LANES), F32)
        cross = jnp.zeros((SUB, LANES), F32)
        area = jnp.ones((SUB, LANES), F32)
        for s in range(0, SUB, 2):
            a = whole(cols[s][0][s : s + 1, :])
            b = whole(cols[s][0][s + 1 : s + 2, :])
            d = whole(cols[s + 1][0][s + 1 : s + 2, :])
            det = a * d - b * b
            inverse = 1.0 / det
            mine = (line // 2) == (s // 2)
            head = jnp.where(mine, a, head)
            cross = jnp.where(mine, b, cross)
            area = jnp.where(mine, det, area)
            p, q, r = d * inverse, b * inverse, a * inverse
            first, second = [], []
            for n, (x, y) in enumerate(zip(cols[s], cols[s + 1])):
                f0 = x * p - y * q
                f1 = y * r - x * q
                if n == 0:
                    f0 = jnp.where(line > s + 1, f0, 0.0)
                    f1 = jnp.where(line > s + 1, f1, 0.0)
                first.append(f0)
                second.append(f1)
            for j in range(s + 2, SUB):
                r0 = whole(cols[j][0][s : s + 1, :])
                r1 = whole(cols[j][0][s + 1 : s + 2, :])
                cols[j] = [c - (f0 * r0 + f1 * r1) for c, f0, f1 in zip(cols[j], first, second)]
            for group in ([left] if g + 1 < tiles else []) + rest:
                width = group[g].shape[1]
                r0 = whole(group[g][s : s + 1, :])
                r1 = whole(group[g][s + 1 : s + 2, :])
                for n, t in enumerate(range(g, tiles)):
                    if n == 0 and s + 2 == SUB:
                        continue
                    group[t] = group[t] - (first[n][:, :width] * r0 + second[n][:, :width] * r1)
        odd = (line % 2) == 1
        scale = lax.rsqrt(jnp.where(odd, area * head, head)) * root
        own = jnp.where(odd, head * scale, scale)
        mix = jnp.where(odd, cross * scale, 0.0)
        for i, group in enumerate(rest):
            width = group[g].shape[1]
            above = jnp.concatenate([group[g][SUB - 1 :, :], group[g][: SUB - 1, :]], axis=0)
            outs[i].append(own[:, :width] * group[g] - mix[:, :width] * above)
    joined = [jnp.concatenate(parts, axis=0) for parts in outs]
    results, at = [], 0
    for other in others:
        count = -(-other.shape[1] // LANES)
        part = joined[at : at + count]
        results.append(part[0] if count == 1 else jnp.concatenate(part, axis=1))
        at += count
    return results


def eye(modes):
    row = lax.broadcasted_iota(jnp.int32, (modes, modes), 0)
    col = lax.broadcasted_iota(jnp.int32, (modes, modes), 1)
    return (row == col).astype(F32)


def store_lanes(ref, value):
    rows, width = value.shape
    ref[0:rows, 0:width] = value


def store_folded(ref, value, modes):
    rows, width = value.shape
    old = rows - modes
    spare = LANES - width
    corner, mass_corner = value[old:, :modes], value[old:, modes:]
    row = lax.broadcasted_iota(jnp.int32, (modes, modes), 0)
    col = lax.broadcasted_iota(jnp.int32, (modes, modes), 1)
    both = jnp.where(row >= col, corner, mass_corner)
    diagonal = jnp.sum(jnp.where(row == col, mass_corner, 0.0), axis=1, keepdims=True)
    rest = jnp.zeros((modes, 2 * spare - modes - 1), F32)
    second = jnp.concatenate([both[:, spare:], diagonal, rest], axis=1)
    folded = jnp.concatenate([both[:, :spare], second], axis=0)
    ref[...] = jnp.concatenate([value[:old, :], folded], axis=1)


def unfold(value, modes):
    width = 2 * modes
    spare = LANES - width
    both = jnp.concatenate([value[:modes, width:], value[modes : 2 * modes, width : width + modes - spare]], axis=1)
    diagonal = value[modes : 2 * modes, width + modes - spare : width + modes - spare + 1]
    row = lax.broadcasted_iota(jnp.int32, (modes, modes), 0)
    col = lax.broadcasted_iota(jnp.int32, (modes, modes), 1)
    turned = both.T
    corner = jnp.where(row >= col, both, turned)
    mass_corner = jnp.where(row < col, both, jnp.where(row > col, turned, diagonal))
    return jnp.concatenate([value[:, :width], jnp.concatenate([corner, mass_corner], axis=1)], axis=0)


def chosen_nodes(nodes, base, window):
    place = lax.broadcasted_iota(jnp.int32, (window, LANES), 0) + base
    parts = [(place == nodes[a : a + 1, :]).astype(F32).astype(BF16) for a in range(nodes.shape[0])]
    return jnp.concatenate(parts, axis=1)


def pick(halves, chosen, base, picked):
    window = chosen.shape[0]
    picked[...] = dot1(halves[0][:, base : base + window], chosen, NN) + dot1(
        halves[1][:, base : base + window], chosen, NN
    )


def multiply(dims, entries, groups, picked, high, low, marks, out):
    comps, modes = dims
    pair = 2 * modes
    width = groups * 2 * LANES
    high[:pair, :] = jnp.zeros((pair, high.shape[1]), BF16)
    low[:pair, :] = jnp.zeros((pair, low.shape[1]), BF16)

    def place(comp):
        rows = pl.ds(pl.multiple_of(comp * pair, pair), pair)
        target = marks[:, :width]
        out[rows, :] += dot1(high[rows, :width], target, NT) + dot1(low[rows, :width], target, NT)

    def one(comp, unused):
        place(comp)
        for group in range(groups):
            totals = [jnp.zeros((modes, LANES), F32) for _ in range(4)]
            for j in range(comps * CORNERS):
                start = (j // CORNERS) * modes
                value = picked[start : start + modes, (j % CORNERS) * LANES : (j % CORNERS + 1) * LANES]
                for q in range(2):
                    for m in range(2):
                        totals[2 * q + m] = totals[2 * q + m] + entries(comp, group, q, m, j) * value
            for q in range(2):
                for m in range(2):
                    upper, lower = split(totals[2 * q + m])
                    rows = pl.ds(pl.multiple_of((comp + 1) * pair + m * modes, 16), modes)
                    lanes = slice((group * 2 + q) * LANES, (group * 2 + q + 1) * LANES)
                    high[rows, lanes] = upper
                    low[rows, lanes] = lower
        return unused

    lax.fori_loop(0, comps, one, 0)
    place(comps)


def all_products(dims, ext, stiffness, mass, edges, connect, edge_nodes, picked, high, low, marks, out):
    halves = split(ext)
    own_products(dims, halves, stiffness, mass, connect, picked, high, low, marks, out)
    edge_products(dims, halves, edges, edge_nodes, picked, high, low, marks, out)


def own_products(dims, halves, stiffness, mass, connect, picked, high, low, marks, out):
    own_nodes = connect[...] + (LANES - HALO)
    out[...] = jnp.zeros(out.shape, F32)
    for number in range(2):
        lane = number * LANES
        chosen = chosen_nodes(own_nodes[:, lane : lane + LANES], lane, 3 * LANES)
        pick(halves, chosen, lane, picked)

        def entries(comp, group, q, m, j):
            matrix = mass if m else stiffness
            return matrix[comp * CORNERS + group * 2 + q, j : j + 1, lane : lane + LANES]

        marks[...] = chosen[LANES - lane : 3 * LANES - lane, :]
        multiply(dims, entries, CORNERS // 2, picked, high, low, marks, out)


def edge_products(dims, halves, edges, edge_nodes, picked, high, low, marks, out):
    comps, _ = dims
    nodes = edge_nodes[...]
    pick(halves, chosen_nodes(nodes[:CORNERS], 0, 4 * LANES), 0, picked)
    first = lax.broadcasted_iota(jnp.int32, (1, LANES), 1) < HALO
    reached = jnp.concatenate(
        [jnp.where(first, nodes[3:4], nodes[2:3]), jnp.where(first, nodes[1:2], -1)], axis=0
    )
    marks[:, : 2 * LANES] = chosen_nodes(reached, LANES, 2 * LANES)
    multiply(
        dims,
        lambda comp, group, q, m, j: edges[m, q * comps + comp, j : j + 1, :],
        1, picked, high, low, marks, out,
    )


def grams(basis, products, dims):
    comps, modes = dims
    total = None
    for c in range(comps):
        left = jnp.concatenate([part[c * modes : (c + 1) * modes, :] for part in basis], axis=0)
        right = products[c * 2 * modes : (c + 1) * 2 * modes, :]
        term = dot3(left, right, NT)
        total = term if total is None else total + term
    return total


def by_side(first_case, second_case):
    odd = lax.rem(lax.axis_index("sub"), 2)
    pl.when(odd == 0)(first_case)
    pl.when(odd == 1)(second_case)


def start_all(pairs, sems, first=0):
    copies = [pltpu.make_async_copy(a, b, sems.at[first + i]) for i, (a, b) in enumerate(pairs)]
    for copy in copies:
        copy.start()
    return copies


def start_sides(from_a, from_b, below, above, sems, first):
    by_side(
        lambda: start_all([(from_b, below), (from_a, above)], sems, first) and None,
        lambda: start_all([(from_a, below), (from_b, above)], sems, first) and None,
    )
    return [pltpu.make_async_copy(a, b, sems.at[first + i]) for i, (a, b) in enumerate([(from_a, below), (from_b, above)])]


def node_kernel(dims, block_in, block, node_a, node_b, sems):
    for copy in start_all([(block_in, block)], sems):
        copy.wait()
    store_sides(block, node_a, node_b)


def pack_kernel(dims, connect_in, stiff_in, mass_in, connect, stiffness, mass, edge_a, edge_b, sems):
    comps, _ = dims
    size = comps * CORNERS
    copies = start_all([(connect_in, connect), (stiff_in, stiffness), (mass_in, mass)], sems)
    pad = jnp.zeros((SUB - CORNERS, LANES), F32)
    rows = comps * size
    first = lax.broadcasted_iota(jnp.int32, (rows, LANES), 1) < HALO
    top = 2 * rows
    for copy in copies:
        copy.wait()
    links = connect[...].astype(F32)

    def corner(matrix, which, lane):
        return jnp.concatenate([matrix[c * CORNERS + which, :, lane : lane + LANES] for c in range(comps)], axis=0)

    def fill(up, down):
        for slot, which in enumerate((3, 1)):
            up[slot * rows : (slot + 1) * rows, :] = jnp.where(
                first, pltpu.roll(corner(stiffness, which, LANES), HALO, 1), corner(mass, which, LANES)
            )
        down[:rows, :] = jnp.where(first, corner(stiffness, 2, 0), pltpu.roll(corner(mass, 2, 0), HALO, 1))
        down[rows:top, :] = jnp.zeros((rows, LANES), F32)
        up[top:, :] = jnp.concatenate([pltpu.roll(links[:, LANES:], HALO, 1), pad], axis=0)
        down[top:, :] = jnp.concatenate([links[:, :LANES], pad], axis=0)

    by_side(lambda: fill(edge_a, edge_b), lambda: fill(edge_b, edge_a))


def store_sides(out, side_a, side_b):
    def put(low, high):
        low[...] = out[:, :LANES]
        high[...] = out[:, LANES:]

    by_side(lambda: put(side_b, side_a), lambda: put(side_a, side_b))


def first_kernel(dims, block, connect, stiffness, mass, from_a, from_b, ext, sums, picked, high, low, marks, sems):
    below, above = ext.at[:, :LANES], ext.at[:, 3 * LANES :]
    copies = start_sides(from_a, from_b, below, above, sems, 0)
    ext[:, LANES : 3 * LANES] = block[...]
    for copy in copies:
        copy.wait()
    own_products(dims, split(ext[...]), stiffness, mass, connect, picked, high, low, marks, sums)


def edge_kernel(dims, block, connect, ext, part, from_a, from_b, edges, edge_nodes, side_a, side_b, gram, picked, high, low, marks, sums, below, above, sems):
    comps, modes = dims
    size = comps * CORNERS
    rows = comps * size
    top = 2 * rows
    copies = start_sides(from_a, from_b, below, above, sems, 0)
    first = lax.broadcasted_iota(jnp.int32, (rows, LANES), 1) < HALO
    halves = split(ext[...])
    sums[...] = part[...]
    for copy in copies:
        copy.wait()
    for slot in range(2):
        lower = below[slot * rows : (slot + 1) * rows, :]
        upper = above[slot * rows : (slot + 1) * rows, :]
        rest = jnp.zeros((rows, LANES), F32)
        here = slice(slot * comps, (slot + 1) * comps)
        edges[0, here] = jnp.where(first, lower, rest if slot else pltpu.roll(upper, HALO, 1)).reshape(comps, size, LANES)
        edges[1, here] = jnp.where(first, pltpu.roll(lower, HALO, 1), rest if slot else upper).reshape(comps, size, LANES)
    count = connect.shape[1]
    before = below[top:, :] + (LANES - HALO - count)
    after = pltpu.roll(above[top:, :], HALO, 1) + (LANES - HALO + count)
    edge_nodes[...] = jnp.where(first[:SUB], before, after).astype(jnp.int32)
    edge_products(dims, halves, edges, edge_nodes, picked, high, low, marks, sums)
    out = sums.at[2 * modes :, :]
    store_sides(out, side_a, side_b)
    store_lanes(gram, grams([block[...]], out[...], dims))


def second_kernel(dims, gram_in, connect, edge_nodes, block, stiffness, mass, edges, from_a, from_b, own_a, own_b, residual, side_a, side_b, gram, state, picked, high, low, marks, sums, below, above, lower, upper, sems):
    comps, modes = dims
    tiles = (below, lower, upper, above)
    copies = start_sides(from_a, from_b, below, above, sems, 0)
    copies += start_sides(own_a, own_b, lower, upper, sems, 2)
    reduced = gram_in[...]
    stiff_gram = symmetric(reduced[:, :modes])
    mass_gram = symmetric(reduced[:, modes : 2 * modes])
    unit = eye(modes)
    (inverse,) = eliminate(mass_gram, [unit], modes)
    (stiff_root,) = eliminate(stiff_gram, [unit], modes)
    ratio = dotf(stiff_gram, dotf(inverse, inverse, TN))
    state[0] = inverse
    state[1] = dotf(stiff_root, stiff_root, TN)
    state[2] = mass_gram
    ratio_high, ratio_low = split(ratio)
    for copy in copies:
        copy.wait()
    pieces = []
    for c in range(comps):
        row = c * 2 * modes
        left = jnp.concatenate([part[row : row + modes, :] for part in tiles], axis=1)
        right_high, right_low = split(jnp.concatenate([part[row + modes : row + 2 * modes, :] for part in tiles], axis=1))
        pieces.append(
            left - (dot1(ratio_high, right_high, NN) + (dot1(ratio_high, right_low, NN) + dot1(ratio_low, right_high, NN)))
        )
    ext = jnp.concatenate(pieces, axis=0)
    residual[...] = ext[:, LANES : 3 * LANES]
    all_products(dims, ext, stiffness, mass, edges, connect, edge_nodes, picked, high, low, marks, sums)
    out = sums.at[2 * modes :, :]
    store_sides(out, side_a, side_b)
    store_lanes(gram, grams([block[...], residual[...]], out[...], dims))


def small_step(reduced, solver, mass_old, start, modes):
    rows = reduced.shape[0]
    old = rows - modes
    turned = reduced.T
    cross = reduced[:old, :modes]
    corner = symmetric(reduced[old:, :modes])
    mass_cross = reduced[:old, modes : 2 * modes]
    mass_corner = symmetric(reduced[old:, modes : 2 * modes])
    mass_turned = turned[modes : 2 * modes, :old]
    mass_all = jnp.concatenate(
        [
            jnp.concatenate([mass_old, mass_cross], axis=1),
            jnp.concatenate([mass_turned, mass_corner], axis=1),
        ],
        axis=0,
    )
    unit = eye(modes)
    carried = dotf(turned[:modes, :old], solver)
    schur = symmetric(corner - dotf(carried, cross))
    root = jnp.concatenate(eliminate(schur, [-carried, unit], modes), axis=1)
    wide = jnp.concatenate(
        [
            jnp.concatenate([solver, jnp.zeros((old, modes), F32)], axis=1),
            jnp.zeros((modes, rows), F32),
        ],
        axis=0,
    )
    solver = wide + dotf(root, root, TN)
    pushed = dotf(start, mass_all[: start.shape[1], :])
    solved = dotf(pushed, solver)
    again = dotf(solved, mass_all)
    (pushed,) = eliminate(symmetric(dotf(solved, again, NT)), [again], modes)
    solved = dotf(pushed, solver)
    again = dotf(solved, mass_all)
    normal = symmetric(dotf(solved, again, NT))
    energy = dotf(solved, pushed, NT)
    coeff, half, root = eliminate(normal, [solved, energy, unit], modes)
    return coeff, half, root, solver, mass_all


def third_kernel(dims, gram_in, state_in, connect, edge_nodes, block, residual, stiffness, mass, edges, from_a, from_b, own_a, own_b, more_a, more_b, new_a, new_b, new, gram, coeff_out, state, picked, high, low, marks, sums, below, above, lower, upper, new_below, new_above, new_lower, new_upper, sems):
    comps, modes = dims
    tiles = ((below, new_below), (lower, new_lower), (upper, new_upper), (above, new_above))
    copies = start_sides(from_a, from_b, below, above, sems, 0)
    copies += start_sides(own_a, own_b, lower, upper, sems, 2)
    copies += start_sides(more_a, more_b, new_below, new_above, sems, 4)
    copies += start_sides(new_a, new_b, new_lower, new_upper, sems, 6)
    coeff, half, root, solver, mass_all = small_step(gram_in[...], state_in[1], state_in[2], state_in[0], modes)
    rayleigh = symmetric(dotf(half, root, NT))
    coeff_out[...] = coeff
    state[0] = solver
    state[1] = mass_all
    bent = dotf(rayleigh, coeff)
    mixed = jnp.concatenate([coeff[:, :modes], -bent[:, :modes], coeff[:, modes:], -bent[:, modes:]], axis=1)
    mixed_high, mixed_low = split(mixed)
    for copy in copies:
        copy.wait()
    pieces = []
    for c in range(comps):
        rows = slice(c * 2 * modes, (c + 1) * 2 * modes)
        right = jnp.concatenate(
            [jnp.concatenate([part[rows, :] for part in parts], axis=0) for parts in tiles], axis=1
        )
        right_high, right_low = split(right)
        pieces.append(dot1(mixed_high, right_high, NN) + (dot1(mixed_high, right_low, NN) + dot1(mixed_low, right_high, NN)))
    ext = jnp.concatenate(pieces, axis=0)
    new[...] = ext[:, LANES : 3 * LANES]
    all_products(dims, ext, stiffness, mass, edges, connect, edge_nodes, picked, high, low, marks, sums)
    out = sums.at[2 * modes :, :]
    store_folded(gram, grams([block[...], residual[...], new[...]], out[...], dims), modes)


def last_kernel(dims, gram_in, coeff_in, state_in, block, residual, new, modes_out, ritz_out):
    comps, modes = dims
    coeff, half, root, _, _ = small_step(unfold(gram_in[...], modes), state_in[0], state_in[1], coeff_in[...], modes)
    ritz_out[...] = jnp.sum(dotf(half, root, NT) * eye(modes), axis=0, keepdims=True)
    coeff_high, coeff_low = split(coeff)
    for c in range(comps):
        rows = slice(c * modes, (c + 1) * modes)
        right_high, right_low = split(jnp.concatenate([part[rows, :] for part in (block, residual, new)], axis=0))
        modes_out[rows, :] = dot1(coeff_high, right_high, NN) + (
            dot1(coeff_high, right_low, NN) + dot1(coeff_low, right_high, NN)
        )


def total_over(value, axis):
    count = lax.axis_size(axis)
    if count & (count - 1):
        return lax.psum(value, axis)

    def from_partner(part, bits):
        return lax.ppermute(part, axis, [(i, i ^ bits) for i in range(count)])

    stride = 1
    while stride < count:
        if 4 * stride <= count:
            one, two, three = (from_partner(value, k * stride) for k in (1, 2, 3))
            value = (value + one) + (two + three)
            stride *= 4
        else:
            value = value + from_partner(value, stride)
            stride *= 2
    return value


def exchange(side_a, side_b, axis):
    count = lax.axis_size(axis)

    def swap(value, start):
        pairs = [(i, i + 1) for i in range(start, count - 1, 2)]
        return lax.ppermute(value, axis, pairs + [(b, a) for a, b in pairs])

    from_a = swap(side_a, 0)
    from_b = swap(side_b, 1)
    return from_a, from_b


VMEM = pl.BlockSpec(memory_space=pltpu.VMEM)
HBM = pl.BlockSpec(memory_space=pltpu.HBM)


def call(kernel, dims, outs, scratch, operands, remote):
    shapes = tuple(kind(shape, dtype) for kind, shape, dtype in outs)
    operands = [pltpu.with_memory_space_constraint(x, pltpu.VMEM) for x in operands]
    return pl.pallas_call(
        functools.partial(kernel, dims),
        out_shape=shapes,
        in_specs=[VMEM] * len(operands) + [HBM] * len(remote),
        out_specs=tuple(VMEM for _ in shapes),
        scratch_shapes=scratch,
        compiler_params=pltpu.CompilerParams(vmem_limit_bytes=24 << 20),
    )(*operands, *[pltpu.with_memory_space_constraint(x, pltpu.HBM) for x in remote])


def room(*arrays):
    return [pltpu.VMEM(x.shape, x.dtype) for x in arrays]


def body(modes_start, stiffness, mass, connect):
    modes, comps, count = modes_start.shape
    size = comps * CORNERS
    dims = (comps, modes)
    rows = comps * modes
    work = [
        pltpu.VMEM((rows, CORNERS * LANES), F32),
        pltpu.VMEM((2 * rows + 2 * modes, CORNERS * LANES), BF16),
        pltpu.VMEM((2 * rows + 2 * modes, CORNERS * LANES), BF16),
        pltpu.VMEM((count, CORNERS * LANES), BF16),
        pltpu.VMEM((2 * rows + 2 * modes, count), F32),
    ]
    near, far = pltpu.VMEM, jax.ShapeDtypeStruct
    wide = (near, (rows, count), F32)
    side = (near, (2 * rows, LANES), F32)
    node = (near, (rows, LANES), F32)
    packed = (near, (2 * comps * size + SUB, LANES), F32)
    sems = pltpu.SemaphoreType.DMA
    block = modes_start.transpose(1, 0, 2).reshape(rows, count)

    block, node_a, node_b = call(node_kernel, dims, [wide, node, node], [sems((1,))], (), (block,))
    node_from = exchange(node_a, node_b, "sub")
    link, stiff_near, mass_near, edge_a, edge_b = call(
        pack_kernel,
        dims,
        [(near, connect.shape, connect.dtype), (near, stiffness.shape, F32), (near, mass.shape, F32), packed, packed],
        [sems((3,))],
        (),
        (connect, stiffness, mass),
    )
    edge_from = exchange(edge_a, edge_b, "sub")
    ext, part = call(
        first_kernel,
        dims,
        [(near, (rows, 2 * count), F32), (near, (2 * rows + 2 * modes, count), F32)],
        work[:4] + [sems((2,))],
        (block, link, stiff_near, mass_near, *node_from),
        (),
    )
    edges, edge_nodes, p_a, p_b, gram = call(
        edge_kernel,
        dims,
        [(near, (2, 2 * comps, size, LANES), F32), (near, (SUB, LANES), jnp.int32), side, side, (near, (modes, LANES), F32)],
        work + room(*edge_from) + [sems((2,))],
        (block, link, ext, part, *edge_from),
        (),
    )
    gram = total_over(gram, "sub")
    p_from_a, p_from_b = exchange(p_a, p_b, "sub")
    p = (p_from_a, p_from_b, p_a, p_b)
    residual, q_a, q_b, gram, state = call(
        second_kernel,
        dims,
        [wide, side, side, (near, (2 * modes, LANES), F32), (near, (3, modes, modes), F32)],
        work + room(*p) + [sems((4,))],
        (gram, link, edge_nodes, block, stiff_near, mass_near, edges, *p),
        (),
    )
    gram = total_over(gram, "sub")
    q_from_a, q_from_b = exchange(q_a, q_b, "sub")
    q = (q_from_a, q_from_b, q_a, q_b)
    new, gram, coeff, state = call(
        third_kernel,
        dims,
        [wide, (near, (2 * modes, LANES), F32), (near, (modes, 2 * modes), F32), (near, (2, 2 * modes, 2 * modes), F32)],
        work + room(*p, *q) + [sems((8,))],
        (gram, state, link, edge_nodes, block, residual, stiff_near, mass_near, edges, *p, *q),
        (),
    )
    gram = total_over(gram, "sub")
    result, ritz = call(
        last_kernel,
        dims,
        [(far, (rows, count), F32), (far, (1, modes), F32)],
        [],
        (gram, coeff, state, block, residual, new),
        (),
    )
    return result.reshape(comps, modes, count).transpose(1, 0, 2), ritz.reshape(modes)


def solution(mesh):
    in_specs = (
        P(None, None, ("groups", "sub")),
        P(None, None, ("groups", "sub")),
        P(None, None, ("groups", "sub")),
        P(None, ("groups", "sub")),
    )
    out_specs = (P(None, None, ("groups", "sub")), P("groups"))
    return jax.shard_map(body, mesh=mesh, in_specs=in_specs, out_specs=out_specs, check_vma=False)
```

```python
import functools

import jax
import jax.numpy as jnp
from jax import lax
from jax.experimental import pallas as pl
from jax.experimental.pallas import tpu as pltpu
from jax.sharding import PartitionSpec as P


HALO = 64
LANES = 128
SUB = 8
CORNERS = 4
F32 = jnp.float32
BF16 = jnp.bfloat16

NN = (((1,), (0,)), ((), ()))
NT = (((1,), (1,)), ((), ()))
TN = (((0,), (0,)), ((), ()))


def split(value):
    high = value.astype(BF16)
    return high, (value - high.astype(F32)).astype(BF16)


def dot1(left, right, dims):
    return lax.dot_general(left, right, dims, preferred_element_type=F32)


def dot3(left, right, dims=NN):
    left_high, left_low = split(left)
    right_high, right_low = split(right)
    return dot1(left_high, right_high, dims) + (
        dot1(left_high, right_low, dims) + dot1(left_low, right_high, dims)
    )


def dotf(left, right, dims=NN):
    return lax.dot_general(
        left, right, dims, precision=lax.Precision.HIGHEST, preferred_element_type=F32
    )


def symmetric(matrix):
    return 0.5 * (matrix + matrix.T)


def whole(row):
    return jnp.broadcast_to(row,(SUB,row.shape[1]))


def eliminate(matrix, others, modes):
    tiles = modes // SUB
    chunks = []
    for other in others:
        for start in range(0, other.shape[1], LANES):
            chunks.append(other[:, start : start + LANES])
    unit = 1.0 / matrix[:1, :1]
    matrix = matrix * unit
    root = jnp.sqrt(jnp.broadcast_to(unit, (SUB, LANES)))
    left = [matrix[SUB * t : SUB * (t + 1), :] for t in range(tiles)]
    rest = [[chunk[SUB * t : SUB * (t + 1), :] for t in range(tiles)] for chunk in chunks]
    line = lax.broadcasted_iota(jnp.int32, (SUB, LANES), 0)
    outs = [[] for _ in chunks]
    for g in range(tiles):
        cols = [
            [jnp.broadcast_to(left[t][:, SUB * g + j : SUB * g + j + 1], (SUB, LANES)) for t in range(g, tiles)]
            for j in range(SUB)
        ]
        head = jnp.ones((SUB, LANES), F32)
        cross = jnp.zeros((SUB, LANES), F32)
        area = jnp.ones((SUB, LANES), F32)
        for s in range(0, SUB, 2):
            a = whole(cols[s][0][s : s + 1, :])
            b = whole(cols[s][0][s + 1 : s + 2, :])
            d = whole(cols[s + 1][0][s + 1 : s + 2, :])
            det = a * d - b * b
            inverse = 1.0 / det
            mine = (line // 2) == (s // 2)
            head = jnp.where(mine, a, head)
            cross = jnp.where(mine, b, cross)
            area = jnp.where(mine, det, area)
            p, q, r = d * inverse, b * inverse, a * inverse
            first, second = [], []
            for n, (x, y) in enumerate(zip(cols[s], cols[s + 1])):
                f0 = x * p - y * q
                f1 = y * r - x * q
                if n == 0:
                    f0 = jnp.where(line > s + 1, f0, 0.0)
                    f1 = jnp.where(line > s + 1, f1, 0.0)
                first.append(f0)
                second.append(f1)
            for j in range(s + 2, SUB):
                r0 = whole(cols[j][0][s : s + 1, :])
                r1 = whole(cols[j][0][s + 1 : s + 2, :])
                cols[j] = [c - (f0 * r0 + f1 * r1) for c, f0, f1 in zip(cols[j], first, second)]
            for group in ([left] if g + 1 < tiles else []) + rest:
                width = group[g].shape[1]
                r0 = whole(group[g][s : s + 1, :])
                r1 = whole(group[g][s + 1 : s + 2, :])
                for n, t in enumerate(range(g, tiles)):
                    if n == 0 and s + 2 == SUB:
                        continue
                    group[t] = group[t] - (first[n][:, :width] * r0 + second[n][:, :width] * r1)
        odd = (line % 2) == 1
        scale = lax.rsqrt(jnp.where(odd, area * head, head)) * root
        own = jnp.where(odd, head * scale, scale)
        mix = jnp.where(odd, cross * scale, 0.0)
        for i, group in enumerate(rest):
            width = group[g].shape[1]
            above = jnp.concatenate([group[g][SUB - 1 :, :], group[g][: SUB - 1, :]], axis=0)
            outs[i].append(own[:, :width] * group[g] - mix[:, :width] * above)
    joined = [jnp.concatenate(parts, axis=0) for parts in outs]
    results, at = [], 0
    for other in others:
        count = -(-other.shape[1] // LANES)
        part = joined[at : at + count]
        results.append(part[0] if count == 1 else jnp.concatenate(part, axis=1))
        at += count
    return results


def eye(modes):
    row = lax.broadcasted_iota(jnp.int32, (modes, modes), 0)
    col = lax.broadcasted_iota(jnp.int32, (modes, modes), 1)
    return (row == col).astype(F32)


def store_lanes(ref, value):
    rows, width = value.shape
    ref[0:rows, 0:width] = value


def mirror(modes):
    row = lax.broadcasted_iota(jnp.int32, (modes, modes), 0)
    col = lax.broadcasted_iota(jnp.int32, (modes, modes), 1)
    return row, col


def store_folded(ref, value, modes):
    rows, width = value.shape
    old = rows - modes
    spare = LANES - width
    corner, mass_corner = value[old:, :modes], value[old:, modes:]
    row, col = mirror(modes)
    both = jnp.where(row >= col, corner, mass_corner)
    diagonal = jnp.sum(jnp.where(row == col, mass_corner, 0.0), axis=1, keepdims=True)
    if old > modes:
        rest = jnp.zeros((modes, 2 * spare - modes - 1), F32)
        second = jnp.concatenate([both[:, spare:], diagonal, rest], axis=1)
        folded = jnp.concatenate([both[:, :spare], second], axis=0)
        ref[...] = jnp.concatenate([value[:old, :], folded], axis=1)
    else:
        ref[:old, :] = jnp.concatenate([value[:old, :], both[:, :spare]], axis=1)
        other = jnp.concatenate([both[:, spare:], jnp.broadcast_to(diagonal, (modes, modes - spare))], axis=1)
        turned = other.T
        left = modes - spare
        ref[old:, :modes] = turned[:left]
        ref[old:, modes : 2 * modes] = turned[left:]


def unfold(value, modes):
    width = 2 * modes
    spare = LANES - width
    left = modes - spare
    row, col = mirror(modes)
    if value.shape[0] >= 2 * modes:
        old = 2 * modes
        both = jnp.concatenate([value[:modes, width:], value[modes:old, width : width + left]], axis=1)
        diagonal = value[modes:old, width + left : width + left + 1]
    else:
        old = modes
        back = jnp.concatenate([value[old:, :modes], value[old:, modes:width]], axis=0).T
        both = jnp.concatenate([value[:old, width:], back[:, :left]], axis=1)
        diagonal = back[:, left : left + 1]
    turned = both.T
    corner = jnp.where(row >= col, both, turned)
    mass_corner = jnp.where(row < col, both, jnp.where(row > col, turned, diagonal))
    return jnp.concatenate([value[:old, :width], jnp.concatenate([corner, mass_corner], axis=1)], axis=0)


def chosen_nodes(nodes, base, window):
    place = lax.broadcasted_iota(jnp.int32, (window, LANES), 0) + base
    parts = [(place == nodes[a : a + 1, :]).astype(F32).astype(BF16) for a in range(nodes.shape[0])]
    return jnp.concatenate(parts, axis=1)


def pick(halves, chosen, base, picked):
    window = chosen.shape[0]
    rows = halves[0].shape[0]
    both = jnp.concatenate([half[:, base : base + window] for half in halves], axis=0)
    values = dot1(both, chosen, NN)
    picked[...] = values[:rows] + values[rows:]


def multiply(dims, entries, groups, picked, high, low, marks, out):
    comps, modes = dims
    pair = 2 * modes
    width = groups * 2 * LANES
    high[:pair, :] = jnp.zeros((pair, high.shape[1]), BF16)
    low[:pair, :] = jnp.zeros((pair, low.shape[1]), BF16)

    def place(comp):
        rows = pl.ds(pl.multiple_of(comp * pair, pair), pair)
        both = jnp.concatenate([high[rows, :width], low[rows, :width]], axis=0)
        sums = dot1(both, marks[:, :width], NT)
        out[rows, :] += sums[:pair] + sums[pair:]

    def one(comp, unused):
        place(comp)
        for group in range(groups):
            totals = [jnp.zeros((modes, LANES), F32) for _ in range(4)]
            for j in range(comps * CORNERS):
                start = (j // CORNERS) * modes
                value = picked[start : start + modes, (j % CORNERS) * LANES : (j % CORNERS + 1) * LANES]
                for q in range(2):
                    for m in range(2):
                        totals[2 * q + m] = totals[2 * q + m] + entries(comp, group, q, m, j) * value
            for q in range(2):
                for m in range(2):
                    upper, lower = split(totals[2 * q + m])
                    rows = pl.ds(pl.multiple_of((comp + 1) * pair + m * modes, 16), modes)
                    lanes = slice((group * 2 + q) * LANES, (group * 2 + q + 1) * LANES)
                    high[rows, lanes] = upper
                    low[rows, lanes] = lower
        return unused

    lax.fori_loop(0, comps, one, 0)
    place(comps)


def all_products(dims, ext, stiffness, mass, edges, connect, edge_nodes, picked, high, low, marks, out):
    halves = split(ext)
    own_products(dims, halves, stiffness, mass, connect, picked, high, low, marks, out)
    edge_products(dims, halves, edges, edge_nodes, picked, high, low, marks, out)


def own_products(dims, halves, stiffness, mass, connect, picked, high, low, marks, out):
    own_nodes = connect[...] + (LANES - HALO)
    out[...] = jnp.zeros(out.shape, F32)
    for number in range(2):
        lane = number * LANES
        chosen = chosen_nodes(own_nodes[:, lane : lane + LANES], lane, 3 * LANES)
        pick(halves, chosen, lane, picked)

        def entries(comp, group, q, m, j):
            matrix = mass if m else stiffness
            return matrix[comp * CORNERS + group * 2 + q, j : j + 1, lane : lane + LANES]

        marks[...] = chosen[LANES - lane : 3 * LANES - lane, :]
        multiply(dims, entries, CORNERS // 2, picked, high, low, marks, out)


def edge_products(dims, halves, edges, edge_nodes, picked, high, low, marks, out):
    comps, _ = dims
    nodes = edge_nodes[...]
    pick(halves, chosen_nodes(nodes[:CORNERS], 0, 4 * LANES), 0, picked)
    first = lax.broadcasted_iota(jnp.int32, (1, LANES), 1) < HALO
    reached = jnp.concatenate(
        [jnp.where(first, nodes[3:4], nodes[2:3]), jnp.where(first, nodes[1:2], -1)], axis=0
    )
    marks[:, : 2 * LANES] = chosen_nodes(reached, LANES, 2 * LANES)
    multiply(
        dims,
        lambda comp, group, q, m, j: edges[m, q * comps + comp, j : j + 1, :],
        1, picked, high, low, marks, out,
    )


def grams(basis, products, dims):
    comps, modes = dims
    total = None
    for c in range(comps):
        left = jnp.concatenate([part[c * modes : (c + 1) * modes, :] for part in basis], axis=0)
        right = products[c * 2 * modes : (c + 1) * 2 * modes, :]
        term = dot3(left, right, NT)
        total = term if total is None else total + term
    return total


def by_side(first_case, second_case):
    odd = lax.rem(lax.axis_index("sub"), 2)
    pl.when(odd == 0)(first_case)
    pl.when(odd == 1)(second_case)


def start_all(pairs, sems, first=0):
    copies = [pltpu.make_async_copy(a, b, sems.at[first + i]) for i, (a, b) in enumerate(pairs)]
    for copy in copies:
        copy.start()
    return copies


def start_sides(from_a, from_b, below, above, sems, first):
    by_side(
        lambda: start_all([(from_b, below), (from_a, above)], sems, first) and None,
        lambda: start_all([(from_a, below), (from_b, above)], sems, first) and None,
    )
    return [pltpu.make_async_copy(a, b, sems.at[first + i]) for i, (a, b) in enumerate([(from_a, below), (from_b, above)])]


def node_kernel(dims, block_in, block, node_a, node_b, sems):
    for copy in start_all([(block_in, block)], sems):
        copy.wait()
    store_sides(block, node_a, node_b)


def pack_kernel(dims, connect_in, stiff_in, mass_in, connect, stiffness, mass, edge_a, edge_b, sems):
    comps, _ = dims
    size = comps * CORNERS
    copies = start_all([(connect_in, connect), (stiff_in, stiffness), (mass_in, mass)], sems)
    pad = jnp.zeros((SUB - CORNERS, LANES), F32)
    rows = comps * size
    first = lax.broadcasted_iota(jnp.int32, (rows, LANES), 1) < HALO
    top = 2 * rows
    for copy in copies:
        copy.wait()
    links = connect[...].astype(F32)

    def corner(matrix, which, lane):
        return jnp.concatenate([matrix[c * CORNERS + which, :, lane : lane + LANES] for c in range(comps)], axis=0)

    def fill(up, down):
        for slot, which in enumerate((3, 1)):
            up[slot * rows : (slot + 1) * rows, :] = jnp.where(
                first, pltpu.roll(corner(stiffness, which, LANES), HALO, 1), corner(mass, which, LANES)
            )
        down[:rows, :] = jnp.where(first, corner(stiffness, 2, 0), pltpu.roll(corner(mass, 2, 0), HALO, 1))
        down[rows:top, :] = jnp.zeros((rows, LANES), F32)
        up[top:, :] = jnp.concatenate([pltpu.roll(links[:, LANES:], HALO, 1), pad], axis=0)
        down[top:, :] = jnp.concatenate([links[:, :LANES], pad], axis=0)

    by_side(lambda: fill(edge_a, edge_b), lambda: fill(edge_b, edge_a))


def store_sides(out, side_a, side_b):
    def put(low, high):
        low[...] = out[:, :LANES]
        high[...] = out[:, LANES:]

    by_side(lambda: put(side_b, side_a), lambda: put(side_a, side_b))


def first_kernel(dims, block, connect, stiffness, mass, from_a, from_b, ext, sums, picked, high, low, marks, sems):
    below, above = ext.at[:, :LANES], ext.at[:, 3 * LANES :]
    copies = start_sides(from_a, from_b, below, above, sems, 0)
    ext[:, LANES : 3 * LANES] = block[...]
    for copy in copies:
        copy.wait()
    own_products(dims, split(ext[...]), stiffness, mass, connect, picked, high, low, marks, sums)


def edge_kernel(dims, block, connect, ext, part, from_a, from_b, edges, edge_nodes, side_a, side_b, gram, picked, high, low, marks, sums, below, above, sems):
    comps, modes = dims
    size = comps * CORNERS
    rows = comps * size
    top = 2 * rows
    copies = start_sides(from_a, from_b, below, above, sems, 0)
    first = lax.broadcasted_iota(jnp.int32, (rows, LANES), 1) < HALO
    halves = split(ext[...])
    sums[...] = part[...]
    for copy in copies:
        copy.wait()
    for slot in range(2):
        lower = below[slot * rows : (slot + 1) * rows, :]
        upper = above[slot * rows : (slot + 1) * rows, :]
        rest = jnp.zeros((rows, LANES), F32)
        here = slice(slot * comps, (slot + 1) * comps)
        edges[0, here] = jnp.where(first, lower, rest if slot else pltpu.roll(upper, HALO, 1)).reshape(comps, size, LANES)
        edges[1, here] = jnp.where(first, pltpu.roll(lower, HALO, 1), rest if slot else upper).reshape(comps, size, LANES)
    count = connect.shape[1]
    before = below[top:, :] + (LANES - HALO - count)
    after = pltpu.roll(above[top:, :], HALO, 1) + (LANES - HALO + count)
    edge_nodes[...] = jnp.where(first[:SUB], before, after).astype(jnp.int32)
    edge_products(dims, halves, edges, edge_nodes, picked, high, low, marks, sums)
    out = sums.at[2 * modes :, :]
    store_sides(out, side_a, side_b)
    store_lanes(gram, grams([block[...]], out[...], dims))


def second_kernel(dims, gram_in, connect, edge_nodes, block, stiffness, mass, edges, from_a, from_b, own_a, own_b, residual, side_a, side_b, gram, state, picked, high, low, marks, sums, below, above, lower, upper, sems):
    comps, modes = dims
    tiles = (below, lower, upper, above)
    copies = start_sides(from_a, from_b, below, above, sems, 0)
    copies += start_sides(own_a, own_b, lower, upper, sems, 2)
    reduced = gram_in[...]
    stiff_gram = symmetric(reduced[:, :modes])
    mass_gram = symmetric(reduced[:, modes : 2 * modes])
    unit = eye(modes)
    (inverse,) = eliminate(mass_gram, [unit], modes)
    (stiff_root,) = eliminate(stiff_gram, [unit], modes)
    ratio = dotf(stiff_gram, dotf(inverse, inverse, TN))
    state[0] = inverse
    state[1] = dotf(stiff_root, stiff_root, TN)
    state[2] = mass_gram
    ratio_high, ratio_low = split(ratio)
    for copy in copies:
        copy.wait()
    pieces = []
    for c in range(comps):
        row = c * 2 * modes
        left = jnp.concatenate([part[row : row + modes, :] for part in tiles], axis=1)
        right_high, right_low = split(jnp.concatenate([part[row + modes : row + 2 * modes, :] for part in tiles], axis=1))
        pieces.append(
            left - (dot1(ratio_high, right_high, NN) + (dot1(ratio_high, right_low, NN) + dot1(ratio_low, right_high, NN)))
        )
    ext = jnp.concatenate(pieces, axis=0)
    residual[...] = ext[:, LANES : 3 * LANES]
    all_products(dims, ext, stiffness, mass, edges, connect, edge_nodes, picked, high, low, marks, sums)
    out = sums.at[2 * modes :, :]
    store_sides(out, side_a, side_b)
    store_folded(gram, grams([block[...], residual[...]], out[...], dims), modes)


def small_step(reduced, solver, mass_old, start, modes):
    rows = reduced.shape[0]
    old = rows - modes
    turned = reduced.T
    cross = reduced[:old, :modes]
    corner = symmetric(reduced[old:, :modes])
    mass_cross = reduced[:old, modes : 2 * modes]
    mass_corner = symmetric(reduced[old:, modes : 2 * modes])
    mass_turned = turned[modes : 2 * modes, :old]
    mass_all = jnp.concatenate(
        [
            jnp.concatenate([mass_old, mass_cross], axis=1),
            jnp.concatenate([mass_turned, mass_corner], axis=1),
        ],
        axis=0,
    )
    unit = eye(modes)
    carried = dotf(turned[:modes, :old], solver)
    schur = symmetric(corner - dotf(carried, cross))
    pushed = dotf(start, mass_all[: start.shape[1], :])
    behind = pushed[:, :old]
    ahead = pushed[:, old:].T - dotf(carried, behind, NT)
    left, right, along = eliminate(schur, [-carried, unit, ahead], modes)
    root = jnp.concatenate([left, right], axis=1)
    wide = jnp.concatenate(
        [
            jnp.concatenate([solver, jnp.zeros((old, modes), F32)], axis=1),
            jnp.zeros((modes, rows), F32),
        ],
        axis=0,
    )
    base = jnp.concatenate([dotf(behind, solver), jnp.zeros((modes, modes), F32)], axis=1)
    solved = base + dotf(along, root, TN)
    solver = wide + dotf(root, root, TN)
    again = dotf(solved, mass_all)
    (pushed,) = eliminate(symmetric(dotf(solved, again, NT)), [again], modes)
    solved = dotf(pushed, solver)
    again = dotf(solved, mass_all)
    normal = symmetric(dotf(solved, again, NT))
    energy = dotf(solved, pushed, NT)
    coeff, half, root = eliminate(normal, [solved, energy, unit], modes)
    return coeff, half, root, solver, mass_all


def third_kernel(dims, gram_in, state_in, connect, edge_nodes, block, residual, stiffness, mass, edges, from_a, from_b, own_a, own_b, more_a, more_b, new_a, new_b, new, gram, coeff_out, state, picked, high, low, marks, sums, below, above, lower, upper, new_below, new_above, new_lower, new_upper, sems):
    comps, modes = dims
    tiles = ((below, new_below), (lower, new_lower), (upper, new_upper), (above, new_above))
    copies = start_sides(from_a, from_b, below, above, sems, 0)
    copies += start_sides(own_a, own_b, lower, upper, sems, 2)
    copies += start_sides(more_a, more_b, new_below, new_above, sems, 4)
    copies += start_sides(new_a, new_b, new_lower, new_upper, sems, 6)
    coeff, half, root, solver, mass_all = small_step(unfold(gram_in[...], modes), state_in[1], state_in[2], state_in[0], modes)
    rayleigh = symmetric(dotf(half, root, NT))
    coeff_out[...] = coeff
    state[0] = solver
    state[1] = mass_all
    bent = dotf(rayleigh, coeff)
    mixed = jnp.concatenate([coeff[:, :modes], -bent[:, :modes], coeff[:, modes:], -bent[:, modes:]], axis=1)
    mixed_high, mixed_low = split(mixed)
    for copy in copies:
        copy.wait()
    pieces = []
    for c in range(comps):
        rows = slice(c * 2 * modes, (c + 1) * 2 * modes)
        right = jnp.concatenate(
            [jnp.concatenate([part[rows, :] for part in parts], axis=0) for parts in tiles], axis=1
        )
        right_high, right_low = split(right)
        pieces.append(dot1(mixed_high, right_high, NN) + (dot1(mixed_high, right_low, NN) + dot1(mixed_low, right_high, NN)))
    ext = jnp.concatenate(pieces, axis=0)
    new[...] = ext[:, LANES : 3 * LANES]
    all_products(dims, ext, stiffness, mass, edges, connect, edge_nodes, picked, high, low, marks, sums)
    out = sums.at[2 * modes :, :]
    store_folded(gram, grams([block[...], residual[...], new[...]], out[...], dims), modes)


def last_kernel(dims, gram_in, coeff_in, state_in, block, residual, new, modes_out, ritz_out):
    comps, modes = dims
    coeff, half, root, _, _ = small_step(unfold(gram_in[...], modes), state_in[0], state_in[1], coeff_in[...], modes)
    ritz_out[...] = jnp.sum(dotf(half, root, NT) * eye(modes), axis=0, keepdims=True)
    coeff_high, coeff_low = split(coeff)
    for c in range(comps):
        rows = slice(c * modes, (c + 1) * modes)
        right_high, right_low = split(jnp.concatenate([part[rows, :] for part in (block, residual, new)], axis=0))
        modes_out[rows, :] = dot1(coeff_high, right_high, NN) + (
            dot1(coeff_high, right_low, NN) + dot1(coeff_low, right_high, NN)
        )


def total_over(value, axis):
    count = lax.axis_size(axis)
    if count & (count - 1):
        return lax.psum(value, axis)

    def from_partner(part, bits):
        return lax.ppermute(part, axis, [(i, i ^ bits) for i in range(count)])

    stride = 1
    while stride < count:
        if 4 * stride <= count:
            one, two, three = (from_partner(value, k * stride) for k in (1, 2, 3))
            value = (value + one) + (two + three)
            stride *= 4
        else:
            value = value + from_partner(value, stride)
            stride *= 2
    return value


def exchange(side_a, side_b, axis):
    count = lax.axis_size(axis)

    def swap(value, start):
        pairs = [(i, i + 1) for i in range(start, count - 1, 2)]
        return lax.ppermute(value, axis, pairs + [(b, a) for a, b in pairs])

    from_a = swap(side_a, 0)
    from_b = swap(side_b, 1)
    return from_a, from_b


VMEM = pl.BlockSpec(memory_space=pltpu.VMEM)
HBM = pl.BlockSpec(memory_space=pltpu.HBM)


def call(kernel, dims, outs, scratch, operands, remote):
    shapes = tuple(kind(shape, dtype) for kind, shape, dtype in outs)
    operands = [pltpu.with_memory_space_constraint(x, pltpu.VMEM) for x in operands]
    return pl.pallas_call(
        functools.partial(kernel, dims),
        out_shape=shapes,
        in_specs=[VMEM] * len(operands) + [HBM] * len(remote),
        out_specs=tuple(VMEM for _ in shapes),
        scratch_shapes=scratch,
        compiler_params=pltpu.CompilerParams(vmem_limit_bytes=24 << 20),
    )(*operands, *[pltpu.with_memory_space_constraint(x, pltpu.HBM) for x in remote])


def room(*arrays):
    return [pltpu.VMEM(x.shape, x.dtype) for x in arrays]


def body(modes_start, stiffness, mass, connect):
    modes, comps, count = modes_start.shape
    size = comps * CORNERS
    dims = (comps, modes)
    rows = comps * modes
    work = [
        pltpu.VMEM((rows, CORNERS * LANES), F32),
        pltpu.VMEM((2 * rows + 2 * modes, CORNERS * LANES), BF16),
        pltpu.VMEM((2 * rows + 2 * modes, CORNERS * LANES), BF16),
        pltpu.VMEM((count, CORNERS * LANES), BF16),
        pltpu.VMEM((2 * rows + 2 * modes, count), F32),
    ]
    near, far = pltpu.VMEM, jax.ShapeDtypeStruct
    wide = (near, (rows, count), F32)
    side = (near, (2 * rows, LANES), F32)
    node = (near, (rows, LANES), F32)
    packed = (near, (2 * comps * size + SUB, LANES), F32)
    sems = pltpu.SemaphoreType.DMA
    block = modes_start.transpose(1, 0, 2).reshape(rows, count)

    block, node_a, node_b = call(node_kernel, dims, [wide, node, node], [sems((1,))], (), (block,))
    node_from = exchange(node_a, node_b, "sub")
    link, stiff_near, mass_near, edge_a, edge_b = call(
        pack_kernel,
        dims,
        [(near, connect.shape, connect.dtype), (near, stiffness.shape, F32), (near, mass.shape, F32), packed, packed],
        [sems((3,))],
        (),
        (connect, stiffness, mass),
    )
    edge_from = exchange(edge_a, edge_b, "sub")
    ext, part = call(
        first_kernel,
        dims,
        [(near, (rows, 2 * count), F32), (near, (2 * rows + 2 * modes, count), F32)],
        work[:4] + [sems((2,))],
        (block, link, stiff_near, mass_near, *node_from),
        (),
    )
    edges, edge_nodes, p_a, p_b, gram = call(
        edge_kernel,
        dims,
        [(near, (2, 2 * comps, size, LANES), F32), (near, (SUB, LANES), jnp.int32), side, side, (near, (modes, LANES), F32)],
        work + room(*edge_from) + [sems((2,))],
        (block, link, ext, part, *edge_from),
        (),
    )
    gram = total_over(gram, "sub")
    p_from_a, p_from_b = exchange(p_a, p_b, "sub")
    p = (p_from_a, p_from_b, p_a, p_b)
    residual, q_a, q_b, gram, state = call(
        second_kernel,
        dims,
        [wide, side, side, (near, (4 * modes - LANES, LANES), F32), (near, (3, modes, modes), F32)],
        work + room(*p) + [sems((4,))],
        (gram, link, edge_nodes, block, stiff_near, mass_near, edges, *p),
        (),
    )
    gram = total_over(gram, "sub")
    q_from_a, q_from_b = exchange(q_a, q_b, "sub")
    q = (q_from_a, q_from_b, q_a, q_b)
    new, gram, coeff, state = call(
        third_kernel,
        dims,
        [wide, (near, (2 * modes, LANES), F32), (near, (modes, 2 * modes), F32), (near, (2, 2 * modes, 2 * modes), F32)],
        work + room(*p, *q) + [sems((8,))],
        (gram, state, link, edge_nodes, block, residual, stiff_near, mass_near, edges, *p, *q),
        (),
    )
    gram = total_over(gram, "sub")
    result, ritz = call(
        last_kernel,
        dims,
        [(far, (rows, count), F32), (far, (1, modes), F32)],
        [],
        (gram, coeff, state, block, residual, new),
        (),
    )
    return result.reshape(comps, modes, count).transpose(1, 0, 2), ritz.reshape(modes)


def solution(mesh):
    in_specs = (
        P(None, None, ("groups", "sub")),
        P(None, None, ("groups", "sub")),
        P(None, None, ("groups", "sub")),
        P(None, ("groups", "sub")),
    )
    out_specs = (P(None, None, ("groups", "sub")), P("groups"))
    return jax.shard_map(body, mesh=mesh, in_specs=in_specs, out_specs=out_specs, check_vma=False)
```

```python
import functools

import jax
import jax.numpy as jnp
from jax import lax
from jax.experimental import pallas as pl
from jax.experimental.pallas import tpu as pltpu
from jax.sharding import PartitionSpec as P


HALO = 64
LANES = 128
SUB = 8
CORNERS = 4
F32 = jnp.float32
BF16 = jnp.bfloat16

NN = (((1,), (0,)), ((), ()))
NT = (((1,), (1,)), ((), ()))
TN = (((0,), (0,)), ((), ()))


def split(value):
    high = value.astype(BF16)
    return high, (value - high.astype(F32)).astype(BF16)


def dot1(left, right, dims):
    return lax.dot_general(left, right, dims, preferred_element_type=F32)


def dot3(left, right, dims=NN):
    rows = left.shape[0]
    left_high, left_low = split(left)
    right_high, right_low = split(right)
    both = dot1(jnp.concatenate([left_high, left_low], axis=0), right_high, dims)
    return both[:rows] + (both[rows:] + dot1(left_high, right_low, dims))


def dotf(left, right, dims=NN):
    return lax.dot_general(
        left, right, dims, precision=lax.Precision.HIGHEST, preferred_element_type=F32
    )


def symmetric(matrix):
    return 0.5 * (matrix + matrix.T)


def whole(row):
    return jnp.broadcast_to(row,(SUB,row.shape[1]))


def eliminate(matrix, others, modes):
    tiles = modes // SUB
    chunks = []
    for other in others:
        for start in range(0, other.shape[1], LANES):
            chunks.append(other[:, start : start + LANES])
    unit = 1.0 / matrix[:1, :1]
    matrix = matrix * unit
    root = jnp.sqrt(jnp.broadcast_to(unit, (SUB, LANES)))
    left = [matrix[SUB * t : SUB * (t + 1), :] for t in range(tiles)]
    rest = [[chunk[SUB * t : SUB * (t + 1), :] for t in range(tiles)] for chunk in chunks]
    line = lax.broadcasted_iota(jnp.int32, (SUB, LANES), 0)
    outs = [[] for _ in chunks]
    for g in range(tiles):
        cols = [
            [jnp.broadcast_to(left[t][:, SUB * g + j : SUB * g + j + 1], (SUB, LANES)) for t in range(g, tiles)]
            for j in range(SUB)
        ]
        head = jnp.ones((SUB, LANES), F32)
        cross = jnp.zeros((SUB, LANES), F32)
        area = jnp.ones((SUB, LANES), F32)
        for s in range(0, SUB, 2):
            a = whole(cols[s][0][s : s + 1, :])
            b = whole(cols[s][0][s + 1 : s + 2, :])
            d = whole(cols[s + 1][0][s + 1 : s + 2, :])
            det = a * d - b * b
            inverse = 1.0 / det
            mine = (line // 2) == (s // 2)
            head = jnp.where(mine, a, head)
            cross = jnp.where(mine, b, cross)
            area = jnp.where(mine, det, area)
            p, q, r = d * inverse, b * inverse, a * inverse
            first, second = [], []
            for n, (x, y) in enumerate(zip(cols[s], cols[s + 1])):
                f0 = x * p - y * q
                f1 = y * r - x * q
                if n == 0:
                    f0 = jnp.where(line > s + 1, f0, 0.0)
                    f1 = jnp.where(line > s + 1, f1, 0.0)
                first.append(f0)
                second.append(f1)
            for j in range(s + 2, SUB):
                r0 = whole(cols[j][0][s : s + 1, :])
                r1 = whole(cols[j][0][s + 1 : s + 2, :])
                cols[j] = [c - (f0 * r0 + f1 * r1) for c, f0, f1 in zip(cols[j], first, second)]
            for group in ([left] if g + 1 < tiles else []) + rest:
                width = group[g].shape[1]
                r0 = whole(group[g][s : s + 1, :])
                r1 = whole(group[g][s + 1 : s + 2, :])
                for n, t in enumerate(range(g, tiles)):
                    if n == 0 and s + 2 == SUB:
                        continue
                    group[t] = group[t] - (first[n][:, :width] * r0 + second[n][:, :width] * r1)
        odd = (line % 2) == 1
        scale = lax.rsqrt(jnp.where(odd, area * head, head)) * root
        own = jnp.where(odd, head * scale, scale)
        mix = jnp.where(odd, cross * scale, 0.0)
        for i, group in enumerate(rest):
            width = group[g].shape[1]
            above = jnp.concatenate([group[g][SUB - 1 :, :], group[g][: SUB - 1, :]], axis=0)
            outs[i].append(own[:, :width] * group[g] - mix[:, :width] * above)
    joined = [jnp.concatenate(parts, axis=0) for parts in outs]
    results, at = [], 0
    for other in others:
        count = -(-other.shape[1] // LANES)
        part = joined[at : at + count]
        results.append(part[0] if count == 1 else jnp.concatenate(part, axis=1))
        at += count
    return results


def eye(modes):
    row = lax.broadcasted_iota(jnp.int32, (modes, modes), 0)
    col = lax.broadcasted_iota(jnp.int32, (modes, modes), 1)
    return (row == col).astype(F32)


def store_lanes(ref, value):
    rows, width = value.shape
    ref[0:rows, 0:width] = value


def mirror(modes):
    row = lax.broadcasted_iota(jnp.int32, (modes, modes), 0)
    col = lax.broadcasted_iota(jnp.int32, (modes, modes), 1)
    return row, col


def store_folded(ref, value, modes):
    rows, width = value.shape
    old = rows - modes
    spare = LANES - width
    corner, mass_corner = value[old:, :modes], value[old:, modes:]
    row, col = mirror(modes)
    both = jnp.where(row >= col, corner, mass_corner)
    diagonal = jnp.sum(jnp.where(row == col, mass_corner, 0.0), axis=1, keepdims=True)
    if old > modes:
        rest = jnp.zeros((modes, 2 * spare - modes - 1), F32)
        second = jnp.concatenate([both[:, spare:], diagonal, rest], axis=1)
        folded = jnp.concatenate([both[:, :spare], second], axis=0)
        ref[...] = jnp.concatenate([value[:old, :], folded], axis=1)
    else:
        ref[:old, :] = jnp.concatenate([value[:old, :], both[:, :spare]], axis=1)
        other = jnp.concatenate([both[:, spare:], jnp.broadcast_to(diagonal, (modes, modes - spare))], axis=1)
        turned = other.T
        left = modes - spare
        ref[old:, :modes] = turned[:left]
        ref[old:, modes : 2 * modes] = turned[left:]


def unfold(value, modes):
    width = 2 * modes
    spare = LANES - width
    left = modes - spare
    row, col = mirror(modes)
    if value.shape[0] >= 2 * modes:
        old = 2 * modes
        both = jnp.concatenate([value[:modes, width:], value[modes:old, width : width + left]], axis=1)
        diagonal = value[modes:old, width + left : width + left + 1]
    else:
        old = modes
        back = jnp.concatenate([value[old:, :modes], value[old:, modes:width]], axis=0).T
        both = jnp.concatenate([value[:old, width:], back[:, :left]], axis=1)
        diagonal = back[:, left : left + 1]
    turned = both.T
    corner = jnp.where(row >= col, both, turned)
    mass_corner = jnp.where(row < col, both, jnp.where(row > col, turned, diagonal))
    return jnp.concatenate([value[:old, :width], jnp.concatenate([corner, mass_corner], axis=1)], axis=0)


def chosen_nodes(nodes, base, window):
    place = lax.broadcasted_iota(jnp.int32, (window, LANES), 0) + base
    parts = [(place == nodes[a : a + 1, :]).astype(F32).astype(BF16) for a in range(nodes.shape[0])]
    return jnp.concatenate(parts, axis=1)


def pick(halves, chosen, base, picked):
    window = chosen.shape[0]
    rows = halves[0].shape[0]
    both = jnp.concatenate([half[:, base : base + window] for half in halves], axis=0)
    values = dot1(both, chosen, NN)
    picked[...] = values[:rows] + values[rows:]


def multiply(dims, entries, groups, picked, high, low, marks, out):
    comps, modes = dims
    pair = 2 * modes
    width = groups * 2 * LANES
    high[:pair, :] = jnp.zeros((pair, high.shape[1]), BF16)
    low[:pair, :] = jnp.zeros((pair, low.shape[1]), BF16)

    def place(comp):
        rows = pl.ds(pl.multiple_of(comp * pair, pair), pair)
        both = jnp.concatenate([high[rows, :width], low[rows, :width]], axis=0)
        sums = dot1(both, marks[:, :width], NT)
        out[rows, :] += sums[:pair] + sums[pair:]

    def one(comp, unused):
        place(comp)
        for group in range(groups):
            totals = [jnp.zeros((modes, LANES), F32) for _ in range(4)]
            for j in range(comps * CORNERS):
                start = (j // CORNERS) * modes
                value = picked[start : start + modes, (j % CORNERS) * LANES : (j % CORNERS + 1) * LANES]
                for q in range(2):
                    for m in range(2):
                        totals[2 * q + m] = totals[2 * q + m] + entries(comp, group, q, m, j) * value
            for q in range(2):
                for m in range(2):
                    upper, lower = split(totals[2 * q + m])
                    rows = pl.ds(pl.multiple_of((comp + 1) * pair + m * modes, 16), modes)
                    lanes = slice((group * 2 + q) * LANES, (group * 2 + q + 1) * LANES)
                    high[rows, lanes] = upper
                    low[rows, lanes] = lower
        return unused

    lax.fori_loop(0, comps, one, 0)
    place(comps)


def all_products(dims, ext, stiffness, mass, edges, connect, edge_nodes, picked, high, low, marks, out):
    halves = split(ext)
    own_products(dims, halves, stiffness, mass, connect, picked, high, low, marks, out)
    edge_products(dims, halves, edges, edge_nodes, picked, high, low, marks, out)


def own_products(dims, halves, stiffness, mass, connect, picked, high, low, marks, out):
    own_nodes = connect[...] + (LANES - HALO)
    out[...] = jnp.zeros(out.shape, F32)
    for number in range(2):
        lane = number * LANES
        chosen = chosen_nodes(own_nodes[:, lane : lane + LANES], lane, 3 * LANES)
        pick(halves, chosen, lane, picked)

        def entries(comp, group, q, m, j):
            matrix = mass if m else stiffness
            return matrix[comp * CORNERS + group * 2 + q, j : j + 1, lane : lane + LANES]

        marks[...] = chosen[LANES - lane : 3 * LANES - lane, :]
        multiply(dims, entries, CORNERS // 2, picked, high, low, marks, out)


def edge_products(dims, halves, edges, edge_nodes, picked, high, low, marks, out):
    comps, _ = dims
    nodes = edge_nodes[...]
    pick(halves, chosen_nodes(nodes[:CORNERS], 0, 4 * LANES), 0, picked)
    first = lax.broadcasted_iota(jnp.int32, (1, LANES), 1) < HALO
    reached = jnp.concatenate(
        [jnp.where(first, nodes[3:4], nodes[2:3]), jnp.where(first, nodes[1:2], -1)], axis=0
    )
    marks[:, : 2 * LANES] = chosen_nodes(reached, LANES, 2 * LANES)
    multiply(
        dims,
        lambda comp, group, q, m, j: edges[m, q * comps + comp, j : j + 1, :],
        1, picked, high, low, marks, out,
    )


def grams(basis, products, dims):
    comps, modes = dims
    total = None
    for c in range(comps):
        left = jnp.concatenate([part[c * modes : (c + 1) * modes, :] for part in basis], axis=0)
        right = products[c * 2 * modes : (c + 1) * 2 * modes, :]
        term = dot3(left, right, NT)
        total = term if total is None else total + term
    return total


def by_side(first_case, second_case):
    odd = lax.rem(lax.axis_index("sub"), 2)
    pl.when(odd == 0)(first_case)
    pl.when(odd == 1)(second_case)


def start_all(pairs, sems, first=0):
    copies = [pltpu.make_async_copy(a, b, sems.at[first + i]) for i, (a, b) in enumerate(pairs)]
    for copy in copies:
        copy.start()
    return copies


def start_sides(from_a, from_b, below, above, sems, first):
    by_side(
        lambda: start_all([(from_b, below), (from_a, above)], sems, first) and None,
        lambda: start_all([(from_a, below), (from_b, above)], sems, first) and None,
    )
    return [pltpu.make_async_copy(a, b, sems.at[first + i]) for i, (a, b) in enumerate([(from_a, below), (from_b, above)])]


def node_kernel(dims, block_in, block, node_a, node_b, sems):
    for copy in start_all([(block_in, block)], sems):
        copy.wait()
    store_sides(block, node_a, node_b)


def pack_kernel(dims, connect_in, stiff_in, mass_in, connect, stiffness, mass, edge_a, edge_b, sems):
    comps, _ = dims
    size = comps * CORNERS
    copies = start_all([(connect_in, connect), (stiff_in, stiffness), (mass_in, mass)], sems)
    pad = jnp.zeros((SUB - CORNERS, LANES), F32)
    rows = comps * size
    first = lax.broadcasted_iota(jnp.int32, (rows, LANES), 1) < HALO
    top = 2 * rows
    for copy in copies:
        copy.wait()
    links = connect[...].astype(F32)

    def corner(matrix, which, lane):
        return jnp.concatenate([matrix[c * CORNERS + which, :, lane : lane + LANES] for c in range(comps)], axis=0)

    def fill(up, down):
        for slot, which in enumerate((3, 1)):
            up[slot * rows : (slot + 1) * rows, :] = jnp.where(
                first, pltpu.roll(corner(stiffness, which, LANES), HALO, 1), corner(mass, which, LANES)
            )
        down[:rows, :] = jnp.where(first, corner(stiffness, 2, 0), pltpu.roll(corner(mass, 2, 0), HALO, 1))
        down[rows:top, :] = jnp.zeros((rows, LANES), F32)
        up[top:, :] = jnp.concatenate([pltpu.roll(links[:, LANES:], HALO, 1), pad], axis=0)
        down[top:, :] = jnp.concatenate([links[:, :LANES], pad], axis=0)

    by_side(lambda: fill(edge_a, edge_b), lambda: fill(edge_b, edge_a))


def store_sides(out, side_a, side_b):
    def put(low, high):
        low[...] = out[:, :LANES]
        high[...] = out[:, LANES:]

    by_side(lambda: put(side_b, side_a), lambda: put(side_a, side_b))


def first_kernel(dims, block, connect, stiffness, mass, from_a, from_b, ext, sums, picked, high, low, marks, sems):
    below, above = ext.at[:, :LANES], ext.at[:, 3 * LANES :]
    copies = start_sides(from_a, from_b, below, above, sems, 0)
    ext[:, LANES : 3 * LANES] = block[...]
    for copy in copies:
        copy.wait()
    own_products(dims, split(ext[...]), stiffness, mass, connect, picked, high, low, marks, sums)


def edge_kernel(dims, block, connect, ext, part, from_a, from_b, edges, edge_nodes, side_a, side_b, gram, picked, high, low, marks, sums, below, above, sems):
    comps, modes = dims
    size = comps * CORNERS
    rows = comps * size
    top = 2 * rows
    copies = start_sides(from_a, from_b, below, above, sems, 0)
    first = lax.broadcasted_iota(jnp.int32, (rows, LANES), 1) < HALO
    halves = split(ext[...])
    sums[...] = part[...]
    for copy in copies:
        copy.wait()
    for slot in range(2):
        lower = below[slot * rows : (slot + 1) * rows, :]
        upper = above[slot * rows : (slot + 1) * rows, :]
        rest = jnp.zeros((rows, LANES), F32)
        here = slice(slot * comps, (slot + 1) * comps)
        edges[0, here] = jnp.where(first, lower, rest if slot else pltpu.roll(upper, HALO, 1)).reshape(comps, size, LANES)
        edges[1, here] = jnp.where(first, pltpu.roll(lower, HALO, 1), rest if slot else upper).reshape(comps, size, LANES)
    count = connect.shape[1]
    before = below[top:, :] + (LANES - HALO - count)
    after = pltpu.roll(above[top:, :], HALO, 1) + (LANES - HALO + count)
    edge_nodes[...] = jnp.where(first[:SUB], before, after).astype(jnp.int32)
    edge_products(dims, halves, edges, edge_nodes, picked, high, low, marks, sums)
    out = sums.at[2 * modes :, :]
    store_sides(out, side_a, side_b)
    store_lanes(gram, grams([block[...]], out[...], dims))


def second_kernel(dims, gram_in, connect, edge_nodes, block, stiffness, mass, edges, from_a, from_b, own_a, own_b, residual, side_a, side_b, gram, state, picked, high, low, marks, sums, below, above, lower, upper, sems):
    comps, modes = dims
    tiles = (below, lower, upper, above)
    copies = start_sides(from_a, from_b, below, above, sems, 0)
    copies += start_sides(own_a, own_b, lower, upper, sems, 2)
    reduced = gram_in[...]
    stiff_gram = symmetric(reduced[:, :modes])
    mass_gram = symmetric(reduced[:, modes : 2 * modes])
    unit = eye(modes)
    (inverse,) = eliminate(mass_gram, [unit], modes)
    (stiff_root,) = eliminate(stiff_gram, [unit], modes)
    ratio = dotf(stiff_gram, dotf(inverse, inverse, TN))
    state[0] = inverse
    state[1] = dotf(stiff_root, stiff_root, TN)
    state[2] = mass_gram
    for copy in copies:
        copy.wait()
    pieces = []
    for c in range(comps):
        row = c * 2 * modes
        left = jnp.concatenate([part[row : row + modes, :] for part in tiles], axis=1)
        right = jnp.concatenate([part[row + modes : row + 2 * modes, :] for part in tiles], axis=1)
        pieces.append(left - dot3(ratio, right))
    ext = jnp.concatenate(pieces, axis=0)
    residual[...] = ext[:, LANES : 3 * LANES]
    all_products(dims, ext, stiffness, mass, edges, connect, edge_nodes, picked, high, low, marks, sums)
    out = sums.at[2 * modes :, :]
    store_sides(out, side_a, side_b)
    store_folded(gram, grams([block[...], residual[...]], out[...], dims), modes)


def small_step(reduced, solver, mass_old, start, modes):
    rows = reduced.shape[0]
    old = rows - modes
    turned = reduced.T
    cross = reduced[:old, :modes]
    corner = symmetric(reduced[old:, :modes])
    mass_cross = reduced[:old, modes : 2 * modes]
    mass_corner = symmetric(reduced[old:, modes : 2 * modes])
    mass_turned = turned[modes : 2 * modes, :old]
    mass_all = jnp.concatenate(
        [
            jnp.concatenate([mass_old, mass_cross], axis=1),
            jnp.concatenate([mass_turned, mass_corner], axis=1),
        ],
        axis=0,
    )
    unit = eye(modes)
    carried = dotf(turned[:modes, :old], solver)
    schur = symmetric(corner - dotf(carried, cross))
    pushed = dotf(start, mass_all[: start.shape[1], :])
    behind = pushed[:, :old]
    ahead = pushed[:, old:].T - dotf(carried, behind, NT)
    left, right, along = eliminate(schur, [-carried, unit, ahead], modes)
    root = jnp.concatenate([left, right], axis=1)
    wide = jnp.concatenate(
        [
            jnp.concatenate([solver, jnp.zeros((old, modes), F32)], axis=1),
            jnp.zeros((modes, rows), F32),
        ],
        axis=0,
    )
    base = jnp.concatenate([dotf(behind, solver), jnp.zeros((modes, modes), F32)], axis=1)
    solved = base + dotf(along, root, TN)
    solver = wide + dotf(root, root, TN)
    again = dotf(solved, mass_all)
    (pushed,) = eliminate(symmetric(dotf(solved, again, NT)), [again], modes)
    solved = dotf(pushed, solver)
    again = dotf(solved, mass_all)
    normal = symmetric(dotf(solved, again, NT))
    energy = dotf(solved, pushed, NT)
    coeff, half, root = eliminate(normal, [solved, energy, unit], modes)
    return coeff, half, root, solver, mass_all


def third_kernel(dims, gram_in, state_in, connect, edge_nodes, block, residual, stiffness, mass, edges, from_a, from_b, own_a, own_b, more_a, more_b, new_a, new_b, new, gram, coeff_out, state, picked, high, low, marks, sums, below, above, lower, upper, new_below, new_above, new_lower, new_upper, sems):
    comps, modes = dims
    tiles = ((below, new_below), (lower, new_lower), (upper, new_upper), (above, new_above))
    copies = start_sides(from_a, from_b, below, above, sems, 0)
    copies += start_sides(own_a, own_b, lower, upper, sems, 2)
    copies += start_sides(more_a, more_b, new_below, new_above, sems, 4)
    copies += start_sides(new_a, new_b, new_lower, new_upper, sems, 6)
    coeff, half, root, solver, mass_all = small_step(unfold(gram_in[...], modes), state_in[1], state_in[2], state_in[0], modes)
    rayleigh = symmetric(dotf(half, root, NT))
    coeff_out[...] = coeff
    state[0] = solver
    state[1] = mass_all
    bent = dotf(rayleigh, coeff)
    mixed = jnp.concatenate([coeff[:, :modes], -bent[:, :modes], coeff[:, modes:], -bent[:, modes:]], axis=1)
    for copy in copies:
        copy.wait()
    pieces = []
    for c in range(comps):
        rows = slice(c * 2 * modes, (c + 1) * 2 * modes)
        right = jnp.concatenate(
            [jnp.concatenate([part[rows, :] for part in parts], axis=0) for parts in tiles], axis=1
        )
        pieces.append(dot3(mixed, right))
    ext = jnp.concatenate(pieces, axis=0)
    new[...] = ext[:, LANES : 3 * LANES]
    all_products(dims, ext, stiffness, mass, edges, connect, edge_nodes, picked, high, low, marks, sums)
    out = sums.at[2 * modes :, :]
    store_folded(gram, grams([block[...], residual[...], new[...]], out[...], dims), modes)


def last_kernel(dims, gram_in, coeff_in, state_in, block, residual, new, modes_out, ritz_out):
    comps, modes = dims
    coeff, half, root, _, _ = small_step(unfold(gram_in[...], modes), state_in[0], state_in[1], coeff_in[...], modes)
    ritz_out[...] = jnp.sum(dotf(half, root, NT) * eye(modes), axis=0, keepdims=True)
    for c in range(comps):
        rows = slice(c * modes, (c + 1) * modes)
        modes_out[rows, :] = dot3(coeff, jnp.concatenate([part[rows, :] for part in (block, residual, new)], axis=0))


def total_over(value, axis):
    count = lax.axis_size(axis)
    if count & (count - 1):
        return lax.psum(value, axis)

    def from_partner(part, bits):
        return lax.ppermute(part, axis, [(i, i ^ bits) for i in range(count)])

    stride = 1
    while stride < count:
        if 4 * stride <= count:
            one, two, three = (from_partner(value, k * stride) for k in (1, 2, 3))
            value = (value + one) + (two + three)
            stride *= 4
        else:
            value = value + from_partner(value, stride)
            stride *= 2
    return value


def exchange(side_a, side_b, axis):
    count = lax.axis_size(axis)

    def swap(value, start):
        pairs = [(i, i + 1) for i in range(start, count - 1, 2)]
        return lax.ppermute(value, axis, pairs + [(b, a) for a, b in pairs])

    from_a = swap(side_a, 0)
    from_b = swap(side_b, 1)
    return from_a, from_b


VMEM = pl.BlockSpec(memory_space=pltpu.VMEM)
HBM = pl.BlockSpec(memory_space=pltpu.HBM)


def call(kernel, dims, outs, scratch, operands, remote):
    shapes = tuple(kind(shape, dtype) for kind, shape, dtype in outs)
    operands = [pltpu.with_memory_space_constraint(x, pltpu.VMEM) for x in operands]
    return pl.pallas_call(
        functools.partial(kernel, dims),
        out_shape=shapes,
        in_specs=[VMEM] * len(operands) + [HBM] * len(remote),
        out_specs=tuple(VMEM for _ in shapes),
        scratch_shapes=scratch,
        compiler_params=pltpu.CompilerParams(vmem_limit_bytes=24 << 20),
    )(*operands, *[pltpu.with_memory_space_constraint(x, pltpu.HBM) for x in remote])


def room(*arrays):
    return [pltpu.VMEM(x.shape, x.dtype) for x in arrays]


def body(modes_start, stiffness, mass, connect):
    modes, comps, count = modes_start.shape
    size = comps * CORNERS
    dims = (comps, modes)
    rows = comps * modes
    work = [
        pltpu.VMEM((rows, CORNERS * LANES), F32),
        pltpu.VMEM((2 * rows + 2 * modes, CORNERS * LANES), BF16),
        pltpu.VMEM((2 * rows + 2 * modes, CORNERS * LANES), BF16),
        pltpu.VMEM((count, CORNERS * LANES), BF16),
        pltpu.VMEM((2 * rows + 2 * modes, count), F32),
    ]
    near, far = pltpu.VMEM, jax.ShapeDtypeStruct
    wide = (near, (rows, count), F32)
    side = (near, (2 * rows, LANES), F32)
    node = (near, (rows, LANES), F32)
    packed = (near, (2 * comps * size + SUB, LANES), F32)
    sems = pltpu.SemaphoreType.DMA
    block = modes_start.transpose(1, 0, 2).reshape(rows, count)

    block, node_a, node_b = call(node_kernel, dims, [wide, node, node], [sems((1,))], (), (block,))
    node_from = exchange(node_a, node_b, "sub")
    link, stiff_near, mass_near, edge_a, edge_b = call(
        pack_kernel,
        dims,
        [(near, connect.shape, connect.dtype), (near, stiffness.shape, F32), (near, mass.shape, F32), packed, packed],
        [sems((3,))],
        (),
        (connect, stiffness, mass),
    )
    edge_from = exchange(edge_a, edge_b, "sub")
    ext, part = call(
        first_kernel,
        dims,
        [(near, (rows, 2 * count), F32), (near, (2 * rows + 2 * modes, count), F32)],
        work[:4] + [sems((2,))],
        (block, link, stiff_near, mass_near, *node_from),
        (),
    )
    edges, edge_nodes, p_a, p_b, gram = call(
        edge_kernel,
        dims,
        [(near, (2, 2 * comps, size, LANES), F32), (near, (SUB, LANES), jnp.int32), side, side, (near, (modes, LANES), F32)],
        work + room(*edge_from) + [sems((2,))],
        (block, link, ext, part, *edge_from),
        (),
    )
    gram = total_over(gram, "sub")
    p_from_a, p_from_b = exchange(p_a, p_b, "sub")
    p = (p_from_a, p_from_b, p_a, p_b)
    residual, q_a, q_b, gram, state = call(
        second_kernel,
        dims,
        [wide, side, side, (near, (4 * modes - LANES, LANES), F32), (near, (3, modes, modes), F32)],
        work + room(*p) + [sems((4,))],
        (gram, link, edge_nodes, block, stiff_near, mass_near, edges, *p),
        (),
    )
    gram = total_over(gram, "sub")
    q_from_a, q_from_b = exchange(q_a, q_b, "sub")
    q = (q_from_a, q_from_b, q_a, q_b)
    new, gram, coeff, state = call(
        third_kernel,
        dims,
        [wide, (near, (2 * modes, LANES), F32), (near, (modes, 2 * modes), F32), (near, (2, 2 * modes, 2 * modes), F32)],
        work + room(*p, *q) + [sems((8,))],
        (gram, state, link, edge_nodes, block, residual, stiff_near, mass_near, edges, *p, *q),
        (),
    )
    gram = total_over(gram, "sub")
    result, ritz = call(
        last_kernel,
        dims,
        [(far, (rows, count), F32), (far, (1, modes), F32)],
        [],
        (gram, coeff, state, block, residual, new),
        (),
    )
    return result.reshape(comps, modes, count).transpose(1, 0, 2), ritz.reshape(modes)


def solution(mesh):
    in_specs = (
        P(None, None, ("groups", "sub")),
        P(None, None, ("groups", "sub")),
        P(None, None, ("groups", "sub")),
        P(None, ("groups", "sub")),
    )
    out_specs = (P(None, None, ("groups", "sub")), P("groups"))
    return jax.shard_map(body, mesh=mesh, in_specs=in_specs, out_specs=out_specs, check_vma=False)
```

```python
import functools

import jax
import jax.numpy as jnp
from jax import lax
from jax.experimental import pallas as pl
from jax.experimental.pallas import tpu as pltpu
from jax.sharding import PartitionSpec as P


HALO = 64
LANES = 128
SUB = 8
CORNERS = 4
F32 = jnp.float32
BF16 = jnp.bfloat16

NN = (((1,), (0,)), ((), ()))
NT = (((1,), (1,)), ((), ()))
TN = (((0,), (0,)), ((), ()))


def split(value):
    high = value.astype(BF16)
    return high, (value - high.astype(F32)).astype(BF16)


def dot1(left, right, dims):
    return lax.dot_general(left, right, dims, preferred_element_type=F32)


def dot3(left, right, dims=NN):
    rows = left.shape[0]
    left_high, left_low = split(left)
    right_high, right_low = split(right)
    both = dot1(jnp.concatenate([left_high, left_low], axis=0), right_high, dims)
    return both[:rows] + (both[rows:] + dot1(left_high, right_low, dims))


def dotf(left, right, dims=NN):
    return lax.dot_general(
        left, right, dims, precision=lax.Precision.HIGHEST, preferred_element_type=F32
    )


def symmetric(matrix):
    return 0.5 * (matrix + matrix.T)


def whole(row):
    return jnp.broadcast_to(row,(SUB,row.shape[1]))


def eliminate(matrix, others, modes):
    tiles = modes // SUB
    chunks = []
    for other in others:
        for start in range(0, other.shape[1], LANES):
            chunks.append(other[:, start : start + LANES])
    unit = 1.0 / matrix[:1, :1]
    matrix = matrix * unit
    root = jnp.sqrt(jnp.broadcast_to(unit, (SUB, LANES)))
    left = [matrix[SUB * t : SUB * (t + 1), :] for t in range(tiles)]
    rest = [[chunk[SUB * t : SUB * (t + 1), :] for t in range(tiles)] for chunk in chunks]
    line = lax.broadcasted_iota(jnp.int32, (SUB, LANES), 0)
    outs = [[] for _ in chunks]
    for g in range(tiles):
        cols = [
            [jnp.broadcast_to(left[t][:, SUB * g + j : SUB * g + j + 1], (SUB, LANES)) for t in range(g, tiles)]
            for j in range(SUB)
        ]
        head = jnp.ones((SUB, LANES), F32)
        cross = jnp.zeros((SUB, LANES), F32)
        area = jnp.ones((SUB, LANES), F32)
        for s in range(0, SUB, 2):
            a = whole(cols[s][0][s : s + 1, :])
            b = whole(cols[s][0][s + 1 : s + 2, :])
            d = whole(cols[s + 1][0][s + 1 : s + 2, :])
            det = a * d - b * b
            inverse = 1.0 / det
            mine = (line // 2) == (s // 2)
            head = jnp.where(mine, a, head)
            cross = jnp.where(mine, b, cross)
            area = jnp.where(mine, det, area)
            p, q, r = d * inverse, b * inverse, a * inverse
            first, second = [], []
            for n, (x, y) in enumerate(zip(cols[s], cols[s + 1])):
                f0 = x * p - y * q
                f1 = y * r - x * q
                if n == 0:
                    f0 = jnp.where(line > s + 1, f0, 0.0)
                    f1 = jnp.where(line > s + 1, f1, 0.0)
                first.append(f0)
                second.append(f1)
            for j in range(s + 2, SUB):
                r0 = whole(cols[j][0][s : s + 1, :])
                r1 = whole(cols[j][0][s + 1 : s + 2, :])
                cols[j] = [c - (f0 * r0 + f1 * r1) for c, f0, f1 in zip(cols[j], first, second)]
            for group in ([left] if g + 1 < tiles else []) + rest:
                width = group[g].shape[1]
                r0 = whole(group[g][s : s + 1, :])
                r1 = whole(group[g][s + 1 : s + 2, :])
                for n, t in enumerate(range(g, tiles)):
                    if n == 0 and s + 2 == SUB:
                        continue
                    group[t] = group[t] - (first[n][:, :width] * r0 + second[n][:, :width] * r1)
        odd = (line % 2) == 1
        scale = lax.rsqrt(jnp.where(odd, area * head, head)) * root
        own = jnp.where(odd, head * scale, scale)
        mix = jnp.where(odd, cross * scale, 0.0)
        for i, group in enumerate(rest):
            width = group[g].shape[1]
            above = jnp.concatenate([group[g][SUB - 1 :, :], group[g][: SUB - 1, :]], axis=0)
            outs[i].append(own[:, :width] * group[g] - mix[:, :width] * above)
    joined = [jnp.concatenate(parts, axis=0) for parts in outs]
    results, at = [], 0
    for other in others:
        count = -(-other.shape[1] // LANES)
        part = joined[at : at + count]
        results.append(part[0] if count == 1 else jnp.concatenate(part, axis=1))
        at += count
    return results


def eye(modes):
    row = lax.broadcasted_iota(jnp.int32, (modes, modes), 0)
    col = lax.broadcasted_iota(jnp.int32, (modes, modes), 1)
    return (row == col).astype(F32)


def store_lanes(ref, value):
    rows, width = value.shape
    ref[0:rows, 0:width] = value


def mirror(modes):
    row = lax.broadcasted_iota(jnp.int32, (modes, modes), 0)
    col = lax.broadcasted_iota(jnp.int32, (modes, modes), 1)
    return row, col


def store_folded(ref, value, modes):
    rows, width = value.shape
    old = rows - modes
    spare = LANES - width
    corner, mass_corner = value[old:, :modes], value[old:, modes:]
    row, col = mirror(modes)
    both = jnp.where(row >= col, corner, mass_corner)
    diagonal = jnp.sum(jnp.where(row == col, mass_corner, 0.0), axis=1, keepdims=True)
    if old > modes:
        rest = jnp.zeros((modes, 2 * spare - modes - 1), F32)
        second = jnp.concatenate([both[:, spare:], diagonal, rest], axis=1)
        folded = jnp.concatenate([both[:, :spare], second], axis=0)
        ref[...] = jnp.concatenate([value[:old, :], folded], axis=1)
    else:
        ref[:old, :] = jnp.concatenate([value[:old, :], both[:, :spare]], axis=1)
        other = jnp.concatenate([both[:, spare:], jnp.broadcast_to(diagonal, (modes, modes - spare))], axis=1)
        turned = other.T
        left = modes - spare
        ref[old:, :modes] = turned[:left]
        ref[old:, modes : 2 * modes] = turned[left:]


def unfold(value, modes):
    width = 2 * modes
    spare = LANES - width
    left = modes - spare
    row, col = mirror(modes)
    if value.shape[0] >= 2 * modes:
        old = 2 * modes
        both = jnp.concatenate([value[:modes, width:], value[modes:old, width : width + left]], axis=1)
        diagonal = value[modes:old, width + left : width + left + 1]
    else:
        old = modes
        back = jnp.concatenate([value[old:, :modes], value[old:, modes:width]], axis=0).T
        both = jnp.concatenate([value[:old, width:], back[:, :left]], axis=1)
        diagonal = back[:, left : left + 1]
    turned = both.T
    corner = jnp.where(row >= col, both, turned)
    mass_corner = jnp.where(row < col, both, jnp.where(row > col, turned, diagonal))
    return jnp.concatenate([value[:old, :width], jnp.concatenate([corner, mass_corner], axis=1)], axis=0)


def chosen_nodes(nodes, base, window):
    place = lax.broadcasted_iota(jnp.int32, (window, LANES), 0) + base
    parts = [(place == nodes[a : a + 1, :]).astype(F32).astype(BF16) for a in range(nodes.shape[0])]
    return jnp.concatenate(parts, axis=1)


def pick(halves, chosen, base, picked):
    window = chosen.shape[0]
    rows = halves[0].shape[0]
    both = jnp.concatenate([half[:, base : base + window] for half in halves], axis=0)
    values = dot1(both, chosen, NN)
    picked[...] = values[:rows] + values[rows:]


def multiply(dims, entries, groups, picked, high, low, marks, out):
    comps, modes = dims
    pair = 2 * modes
    width = groups * 2 * LANES
    high[:pair, :] = jnp.zeros((pair, high.shape[1]), BF16)
    low[:pair, :] = jnp.zeros((pair, low.shape[1]), BF16)

    def place(comp):
        rows = pl.ds(pl.multiple_of(comp * pair, pair), pair)
        both = jnp.concatenate([high[rows, :width], low[rows, :width]], axis=0)
        sums = dot1(both, marks[:, :width], NT)
        out[rows, :] += sums[:pair] + sums[pair:]

    def one(comp, unused):
        place(comp)
        for group in range(groups):
            totals = [jnp.zeros((modes, LANES), F32) for _ in range(4)]
            for j in range(comps * CORNERS):
                start = (j // CORNERS) * modes
                value = picked[start : start + modes, (j % CORNERS) * LANES : (j % CORNERS + 1) * LANES]
                for q in range(2):
                    for m in range(2):
                        totals[2 * q + m] = totals[2 * q + m] + entries(comp, group, q, m, j) * value
            for q in range(2):
                for m in range(2):
                    upper, lower = split(totals[2 * q + m])
                    rows = pl.ds(pl.multiple_of((comp + 1) * pair + m * modes, 16), modes)
                    lanes = slice((group * 2 + q) * LANES, (group * 2 + q + 1) * LANES)
                    high[rows, lanes] = upper
                    low[rows, lanes] = lower
        return unused

    lax.fori_loop(0, comps, one, 0)
    place(comps)


def all_products(dims, ext, stiffness, mass, edges, connect, edge_nodes, picked, high, low, marks, out):
    halves = split(ext)
    own_products(dims, halves, stiffness, mass, connect, picked, high, low, marks, out)
    edge_products(dims, halves, edges, edge_nodes, picked, high, low, marks, out)


def own_products(dims, halves, stiffness, mass, connect, picked, high, low, marks, out):
    own_nodes = connect[...] + (LANES - HALO)
    out[...] = jnp.zeros(out.shape, F32)
    for number in range(2):
        lane = number * LANES
        chosen = chosen_nodes(own_nodes[:, lane : lane + LANES], lane, 3 * LANES)
        pick(halves, chosen, lane, picked)

        def entries(comp, group, q, m, j):
            matrix = mass if m else stiffness
            return matrix[comp * CORNERS + group * 2 + q, j : j + 1, lane : lane + LANES]

        marks[...] = chosen[LANES - lane : 3 * LANES - lane, :]
        multiply(dims, entries, CORNERS // 2, picked, high, low, marks, out)


def edge_products(dims, halves, edges, edge_nodes, picked, high, low, marks, out):
    comps, _ = dims
    nodes = edge_nodes[...]
    pick(halves, chosen_nodes(nodes[:CORNERS], 0, 4 * LANES), 0, picked)
    first = lax.broadcasted_iota(jnp.int32, (1, LANES), 1) < HALO
    reached = jnp.concatenate(
        [jnp.where(first, nodes[3:4], nodes[2:3]), jnp.where(first, nodes[1:2], -1)], axis=0
    )
    marks[:, : 2 * LANES] = chosen_nodes(reached, LANES, 2 * LANES)
    multiply(
        dims,
        lambda comp, group, q, m, j: edges[m, q * comps + comp, j : j + 1, :],
        1, picked, high, low, marks, out,
    )


def grams(basis, products, dims):
    comps, modes = dims
    total = None
    for c in range(comps):
        left = jnp.concatenate([part[c * modes : (c + 1) * modes, :] for part in basis], axis=0)
        right = products[c * 2 * modes : (c + 1) * 2 * modes, :]
        term = dot3(left, right, NT)
        total = term if total is None else total + term
    return total


def by_side(first_case, second_case):
    odd = lax.rem(lax.axis_index("sub"), 2)
    pl.when(odd == 0)(first_case)
    pl.when(odd == 1)(second_case)


def start_all(pairs, sems, first=0):
    copies = [pltpu.make_async_copy(a, b, sems.at[first + i]) for i, (a, b) in enumerate(pairs)]
    for copy in copies:
        copy.start()
    return copies


def start_sides(from_a, from_b, below, above, sems, first):
    by_side(
        lambda: start_all([(from_b, below), (from_a, above)], sems, first) and None,
        lambda: start_all([(from_a, below), (from_b, above)], sems, first) and None,
    )
    return [pltpu.make_async_copy(a, b, sems.at[first + i]) for i, (a, b) in enumerate([(from_a, below), (from_b, above)])]


def node_kernel(dims, block_in, block, node_a, node_b, sems):
    for copy in start_all([(block_in, block)], sems):
        copy.wait()
    store_sides(block, node_a, node_b)


def pack_kernel(dims, connect_in, stiff_in, mass_in, connect, stiffness, mass, edge_a, edge_b, sems):
    comps, _ = dims
    size = comps * CORNERS
    copies = start_all([(connect_in, connect), (stiff_in, stiffness), (mass_in, mass)], sems)
    pad = jnp.zeros((SUB - CORNERS, LANES), F32)
    rows = comps * size
    first = lax.broadcasted_iota(jnp.int32, (rows, LANES), 1) < HALO
    top = 2 * rows
    for copy in copies:
        copy.wait()
    links = connect[...].astype(F32)

    def corner(matrix, which, lane):
        return jnp.concatenate([matrix[c * CORNERS + which, :, lane : lane + LANES] for c in range(comps)], axis=0)

    def fill(up, down):
        for slot, which in enumerate((3, 1)):
            up[slot * rows : (slot + 1) * rows, :] = jnp.where(
                first, pltpu.roll(corner(stiffness, which, LANES), HALO, 1), corner(mass, which, LANES)
            )
        down[:rows, :] = jnp.where(first, corner(stiffness, 2, 0), pltpu.roll(corner(mass, 2, 0), HALO, 1))
        down[rows:top, :] = jnp.zeros((rows, LANES), F32)
        up[top:, :] = jnp.concatenate([pltpu.roll(links[:, LANES:], HALO, 1), pad], axis=0)
        down[top:, :] = jnp.concatenate([links[:, :LANES], pad], axis=0)

    by_side(lambda: fill(edge_a, edge_b), lambda: fill(edge_b, edge_a))


def store_sides(out, side_a, side_b):
    def put(low, high):
        low[...] = out[:, :LANES]
        high[...] = out[:, LANES:]

    by_side(lambda: put(side_b, side_a), lambda: put(side_a, side_b))


def first_kernel(dims, block, connect, stiffness, mass, from_a, from_b, ext, sums, picked, high, low, marks, sems):
    below, above = ext.at[:, :LANES], ext.at[:, 3 * LANES :]
    copies = start_sides(from_a, from_b, below, above, sems, 0)
    ext[:, LANES : 3 * LANES] = block[...]
    for copy in copies:
        copy.wait()
    own_products(dims, split(ext[...]), stiffness, mass, connect, picked, high, low, marks, sums)


def edge_kernel(dims, block, connect, ext, part, from_a, from_b, edges, edge_nodes, side_a, side_b, gram, picked, high, low, marks, sums, below, above, sems):
    comps, modes = dims
    size = comps * CORNERS
    rows = comps * size
    top = 2 * rows
    copies = start_sides(from_a, from_b, below, above, sems, 0)
    first = lax.broadcasted_iota(jnp.int32, (rows, LANES), 1) < HALO
    halves = split(ext[...])
    sums[...] = part[...]
    for copy in copies:
        copy.wait()
    for slot in range(2):
        lower = below[slot * rows : (slot + 1) * rows, :]
        upper = above[slot * rows : (slot + 1) * rows, :]
        rest = jnp.zeros((rows, LANES), F32)
        here = slice(slot * comps, (slot + 1) * comps)
        edges[0, here] = jnp.where(first, lower, rest if slot else pltpu.roll(upper, HALO, 1)).reshape(comps, size, LANES)
        edges[1, here] = jnp.where(first, pltpu.roll(lower, HALO, 1), rest if slot else upper).reshape(comps, size, LANES)
    count = connect.shape[1]
    before = below[top:, :] + (LANES - HALO - count)
    after = pltpu.roll(above[top:, :], HALO, 1) + (LANES - HALO + count)
    edge_nodes[...] = jnp.where(first[:SUB], before, after).astype(jnp.int32)
    edge_products(dims, halves, edges, edge_nodes, picked, high, low, marks, sums)
    out = sums.at[2 * modes :, :]
    store_sides(out, side_a, side_b)
    store_lanes(gram, grams([block[...]], out[...], dims))


def second_kernel(dims, gram_in, connect, edge_nodes, block, stiffness, mass, edges, from_a, from_b, own_a, own_b, residual, side_a, side_b, gram, state, picked, high, low, marks, sums, below, above, lower, upper, sems):
    comps, modes = dims
    tiles = (below, lower, upper, above)
    copies = start_sides(from_a, from_b, below, above, sems, 0)
    copies += start_sides(own_a, own_b, lower, upper, sems, 2)
    reduced = gram_in[...]
    stiff_gram = symmetric(reduced[:, :modes])
    mass_gram = symmetric(reduced[:, modes : 2 * modes])
    unit = eye(modes)
    (inverse,) = eliminate(mass_gram, [unit], modes)
    (stiff_root,) = eliminate(stiff_gram, [unit], modes)
    ratio = dotf(stiff_gram, dotf(inverse, inverse, TN))
    state[0] = inverse
    state[1] = dotf(stiff_root, stiff_root, TN)
    state[2] = mass_gram
    for copy in copies:
        copy.wait()
    pieces = []
    for c in range(comps):
        row = c * 2 * modes
        left = jnp.concatenate([part[row : row + modes, :] for part in tiles], axis=1)
        right = jnp.concatenate([part[row + modes : row + 2 * modes, :] for part in tiles], axis=1)
        pieces.append(left - dot3(ratio, right))
    ext = jnp.concatenate(pieces, axis=0)
    residual[...] = ext[:, LANES : 3 * LANES]
    all_products(dims, ext, stiffness, mass, edges, connect, edge_nodes, picked, high, low, marks, sums)
    out = sums.at[2 * modes :, :]
    store_sides(out, side_a, side_b)
    store_folded(gram, grams([block[...], residual[...]], out[...], dims), modes)


def small_step(reduced, solver, mass_old, start, modes):
    rows = reduced.shape[0]
    old = rows - modes
    turned = reduced.T
    cross = reduced[:old, :modes]
    corner = symmetric(reduced[old:, :modes])
    mass_cross = reduced[:old, modes : 2 * modes]
    mass_corner = symmetric(reduced[old:, modes : 2 * modes])
    mass_turned = turned[modes : 2 * modes, :old]
    mass_all = jnp.concatenate(
        [
            jnp.concatenate([mass_old, mass_cross], axis=1),
            jnp.concatenate([mass_turned, mass_corner], axis=1),
        ],
        axis=0,
    )
    unit = eye(modes)
    carried = dotf(turned[:modes, :old], solver)
    schur = symmetric(corner - dotf(carried, cross))
    pushed = dotf(start, mass_all[: start.shape[1], :])
    behind = pushed[:, :old]
    ahead = pushed[:, old:].T - dotf(carried, behind, NT)
    left, right, along = eliminate(schur, [-carried, unit, ahead], modes)
    root = jnp.concatenate([left, right], axis=1)
    wide = jnp.concatenate(
        [
            jnp.concatenate([solver, jnp.zeros((old, modes), F32)], axis=1),
            jnp.zeros((modes, rows), F32),
        ],
        axis=0,
    )
    base = jnp.concatenate([dotf(behind, solver), jnp.zeros((modes, modes), F32)], axis=1)
    solved = base + dotf(along, root, TN)
    solver = wide + dotf(root, root, TN)
    again = dot3(solved, mass_all)
    (pushed,) = eliminate(symmetric(dot3(solved, again, NT)), [again], modes)
    solved = dot3(pushed, solver)
    again = dot3(solved, mass_all)
    normal = symmetric(dot3(solved, again, NT))
    energy = dot3(solved, pushed, NT)
    coeff, half, root = eliminate(normal, [solved, energy, unit], modes)
    return coeff, half, root, solver, mass_all


def third_kernel(dims, gram_in, state_in, connect, edge_nodes, block, residual, stiffness, mass, edges, from_a, from_b, own_a, own_b, more_a, more_b, new_a, new_b, new, gram, coeff_out, state, picked, high, low, marks, sums, below, above, lower, upper, new_below, new_above, new_lower, new_upper, sems):
    comps, modes = dims
    tiles = ((below, new_below), (lower, new_lower), (upper, new_upper), (above, new_above))
    copies = start_sides(from_a, from_b, below, above, sems, 0)
    copies += start_sides(own_a, own_b, lower, upper, sems, 2)
    copies += start_sides(more_a, more_b, new_below, new_above, sems, 4)
    copies += start_sides(new_a, new_b, new_lower, new_upper, sems, 6)
    coeff, half, root, solver, mass_all = small_step(unfold(gram_in[...], modes), state_in[1], state_in[2], state_in[0], modes)
    rayleigh = symmetric(dotf(half, root, NT))
    coeff_out[...] = coeff
    state[0] = solver
    state[1] = mass_all
    bent = dotf(rayleigh, coeff)
    mixed = jnp.concatenate([coeff[:, :modes], -bent[:, :modes], coeff[:, modes:], -bent[:, modes:]], axis=1)
    for copy in copies:
        copy.wait()
    pieces = []
    for c in range(comps):
        rows = slice(c * 2 * modes, (c + 1) * 2 * modes)
        right = jnp.concatenate(
            [jnp.concatenate([part[rows, :] for part in parts], axis=0) for parts in tiles], axis=1
        )
        pieces.append(dot3(mixed, right))
    ext = jnp.concatenate(pieces, axis=0)
    new[...] = ext[:, LANES : 3 * LANES]
    all_products(dims, ext, stiffness, mass, edges, connect, edge_nodes, picked, high, low, marks, sums)
    out = sums.at[2 * modes :, :]
    store_folded(gram, grams([block[...], residual[...], new[...]], out[...], dims), modes)


def last_kernel(dims, gram_in, coeff_in, state_in, block, residual, new, modes_out, ritz_out):
    comps, modes = dims
    coeff, half, root, _, _ = small_step(unfold(gram_in[...], modes), state_in[0], state_in[1], coeff_in[...], modes)
    ritz_out[...] = jnp.sum(dotf(half, root, NT) * eye(modes), axis=0, keepdims=True)
    for c in range(comps):
        rows = slice(c * modes, (c + 1) * modes)
        modes_out[rows, :] = dot3(coeff, jnp.concatenate([part[rows, :] for part in (block, residual, new)], axis=0))


def total_over(value, axis):
    count = lax.axis_size(axis)
    if count & (count - 1):
        return lax.psum(value, axis)

    def from_partner(part, bits):
        return lax.ppermute(part, axis, [(i, i ^ bits) for i in range(count)])

    stride = 1
    while stride < count:
        if 4 * stride <= count:
            one, two, three = (from_partner(value, k * stride) for k in (1, 2, 3))
            value = (value + one) + (two + three)
            stride *= 4
        else:
            value = value + from_partner(value, stride)
            stride *= 2
    return value


def exchange(side_a, side_b, axis):
    count = lax.axis_size(axis)

    def swap(value, start):
        pairs = [(i, i + 1) for i in range(start, count - 1, 2)]
        return lax.ppermute(value, axis, pairs + [(b, a) for a, b in pairs])

    from_a = swap(side_a, 0)
    from_b = swap(side_b, 1)
    return from_a, from_b


VMEM = pl.BlockSpec(memory_space=pltpu.VMEM)
HBM = pl.BlockSpec(memory_space=pltpu.HBM)


def call(kernel, dims, outs, scratch, operands, remote):
    shapes = tuple(kind(shape, dtype) for kind, shape, dtype in outs)
    operands = [pltpu.with_memory_space_constraint(x, pltpu.VMEM) for x in operands]
    return pl.pallas_call(
        functools.partial(kernel, dims),
        out_shape=shapes,
        in_specs=[VMEM] * len(operands) + [HBM] * len(remote),
        out_specs=tuple(VMEM for _ in shapes),
        scratch_shapes=scratch,
        compiler_params=pltpu.CompilerParams(vmem_limit_bytes=24 << 20),
    )(*operands, *[pltpu.with_memory_space_constraint(x, pltpu.HBM) for x in remote])


def room(*arrays):
    return [pltpu.VMEM(x.shape, x.dtype) for x in arrays]


def body(modes_start, stiffness, mass, connect):
    modes, comps, count = modes_start.shape
    size = comps * CORNERS
    dims = (comps, modes)
    rows = comps * modes
    work = [
        pltpu.VMEM((rows, CORNERS * LANES), F32),
        pltpu.VMEM((2 * rows + 2 * modes, CORNERS * LANES), BF16),
        pltpu.VMEM((2 * rows + 2 * modes, CORNERS * LANES), BF16),
        pltpu.VMEM((count, CORNERS * LANES), BF16),
        pltpu.VMEM((2 * rows + 2 * modes, count), F32),
    ]
    near, far = pltpu.VMEM, jax.ShapeDtypeStruct
    wide = (near, (rows, count), F32)
    side = (near, (2 * rows, LANES), F32)
    node = (near, (rows, LANES), F32)
    packed = (near, (2 * comps * size + SUB, LANES), F32)
    sems = pltpu.SemaphoreType.DMA
    block = modes_start.transpose(1, 0, 2).reshape(rows, count)

    block, node_a, node_b = call(node_kernel, dims, [wide, node, node], [sems((1,))], (), (block,))
    node_from = exchange(node_a, node_b, "sub")
    link, stiff_near, mass_near, edge_a, edge_b = call(
        pack_kernel,
        dims,
        [(near, connect.shape, connect.dtype), (near, stiffness.shape, F32), (near, mass.shape, F32), packed, packed],
        [sems((3,))],
        (),
        (connect, stiffness, mass),
    )
    edge_from = exchange(edge_a, edge_b, "sub")
    ext, part = call(
        first_kernel,
        dims,
        [(near, (rows, 2 * count), F32), (near, (2 * rows + 2 * modes, count), F32)],
        work[:4] + [sems((2,))],
        (block, link, stiff_near, mass_near, *node_from),
        (),
    )
    edges, edge_nodes, p_a, p_b, gram = call(
        edge_kernel,
        dims,
        [(near, (2, 2 * comps, size, LANES), F32), (near, (SUB, LANES), jnp.int32), side, side, (near, (modes, LANES), F32)],
        work + room(*edge_from) + [sems((2,))],
        (block, link, ext, part, *edge_from),
        (),
    )
    gram = total_over(gram, "sub")
    p_from_a, p_from_b = exchange(p_a, p_b, "sub")
    p = (p_from_a, p_from_b, p_a, p_b)
    residual, q_a, q_b, gram, state = call(
        second_kernel,
        dims,
        [wide, side, side, (near, (4 * modes - LANES, LANES), F32), (near, (3, modes, modes), F32)],
        work + room(*p) + [sems((4,))],
        (gram, link, edge_nodes, block, stiff_near, mass_near, edges, *p),
        (),
    )
    gram = total_over(gram, "sub")
    q_from_a, q_from_b = exchange(q_a, q_b, "sub")
    q = (q_from_a, q_from_b, q_a, q_b)
    new, gram, coeff, state = call(
        third_kernel,
        dims,
        [wide, (near, (2 * modes, LANES), F32), (near, (modes, 2 * modes), F32), (near, (2, 2 * modes, 2 * modes), F32)],
        work + room(*p, *q) + [sems((8,))],
        (gram, state, link, edge_nodes, block, residual, stiff_near, mass_near, edges, *p, *q),
        (),
    )
    gram = total_over(gram, "sub")
    result, ritz = call(
        last_kernel,
        dims,
        [(far, (rows, count), F32), (far, (1, modes), F32)],
        [],
        (gram, coeff, state, block, residual, new),
        (),
    )
    return result.reshape(comps, modes, count).transpose(1, 0, 2), ritz.reshape(modes)


def solution(mesh):
    in_specs = (
        P(None, None, ("groups", "sub")),
        P(None, None, ("groups", "sub")),
        P(None, None, ("groups", "sub")),
        P(None, ("groups", "sub")),
    )
    out_specs = (P(None, None, ("groups", "sub")), P("groups"))
    return jax.shard_map(body, mesh=mesh, in_specs=in_specs, out_specs=out_specs, check_vma=False)
```
